32 devices in a mesh: dp: 32 (over z, y, x, core).
Axes of the slice: x: 2, y: 2, z: 4, core: 2. Of those that a mesh axis runs over, the one named last changes fastest.
Arguments:
- patches: bfloat16 [32768, 768], P('dp'), may hold values from -6 to 6
- img_length: int32 [512], P('dp'), may hold values from 0 to 576, as said below
- img_start: int32 [512], P('dp'), may hold values from 0 to 1024, as said below
- class_count: int32 [32], P('dp'), may hold values from 1 to 63, as said below
- gain_attend: bfloat16 [2, 768], replicated, may hold values from 0.25 to 1.75
- shift_attend: bfloat16 [2, 768], replicated, may hold values from -1 to 1
- qkv_weight: bfloat16 [2, 768, 2304], replicated, may hold values from -0.21875 to 0.21875
- qv_bias: bfloat16 [2, 1536], replicated, may hold values from -1 to 1
- out_weight: bfloat16 [2, 768, 768], replicated, may hold values from -0.875 to 0.875
- out_bias: bfloat16 [2, 768], replicated, may hold values from -1 to 1
- gain_mlp: bfloat16 [2, 768], replicated, may hold values from 0.25 to 1.75
- shift_mlp: bfloat16 [2, 768], replicated, may hold values from -1 to 1
- up_weight: bfloat16 [2, 768, 3072], replicated, may hold values from -0.21875 to 0.21875
- up_bias: bfloat16 [2, 3072], replicated, may hold values from -1 to 1
- down_weight: bfloat16 [2, 3072, 768], replicated, may hold values from -0.109375 to 0.109375
- down_bias: bfloat16 [2, 768], replicated, may hold values from -1 to 1
- cls_weight: bfloat16 [768, 2048], P(None, 'dp'), may hold values from -0.21875 to 0.21875
- cls_bias: bfloat16 [2048], P('dp'), may hold values from -2.5 to 2.5
- logit_grad: bfloat16 [512, 2048], P(None, 'dp'), may hold values from -48 to 48
Outputs:
- logits: float32 [512, 2048], P(None, 'dp')
- patch_grad: float32 [32768, 768], P('dp')
- gain_attend_grad: float32 [2, 768], P(None, 'dp')
- shift_attend_grad: float32 [2, 768], P(None, 'dp')
- qkv_weight_grad: float32 [2, 768, 2304], P(None, 'dp')
- qv_bias_grad: float32 [2, 1536], P(None, 'dp')
- out_weight_grad: float32 [2, 768, 768], P(None, 'dp')
- out_bias_grad: float32 [2, 768], P(None, 'dp')
- gain_mlp_grad: float32 [2, 768], P(None, 'dp')
- shift_mlp_grad: float32 [2, 768], P(None, 'dp')
- up_weight_grad: float32 [2, 768, 3072], P(None, 'dp')
- up_bias_grad: float32 [2, 3072], P(None, 'dp')
- down_weight_grad: float32 [2, 3072, 768], P(None, 'dp')
- down_bias_grad: float32 [2, 768], P(None, 'dp')
- cls_weight_grad: float32 [768, 2048], P(None, 'dp')
- cls_bias_grad: float32 [2048], P('dp')
The draws below stay inside these ranges and needn't reach their ends.
Inputs may be any that keep to these rules, and one draw needn't show every extreme that they name: `img_length`: each device's 16 slots hold images of 64 or 576 patches, or 0 for an empty slot; a device holds at most one image of 576 patches, in its first slot, and its images take at most 1024 rows. In every draw some device fills all 1024 rows and some device uses all 16 slots. `img_start`: A device's images lie end to end from row 0 in slot order; an empty slot starts where the device's images end. `class_count`: the live columns of a device are the first ones of its 64; the counts of all devices sum to 1024.
All inputs are finite; a program needn't handle non-finite values.
Results may differ from the reference program's by a relative error of at most 0.01.
Values may be sent and summed in bfloat16 or wider, within the bound.
A program may use at most 320 MiB of HBM per device.

```python
import jax
import jax.numpy as jnp
from jax import lax

D = 768
H = 12
HD = 64
FF = 3072
CLASSES = 1024
SMALL_LEN = 64
LARGE_LEN = 576
IMG_CAP = 16
LAYERS = 2
TOK = 1024
ROWS = 32768
IMAGES = 512
CLS_CAP = 64
CLS_SLOTS = 2048
N_DP = 32


def pack_images(key):
    folded = jax.random.fold_in(key, 11)
    key_kind, key_extra, key_small = jax.random.split(folded, 3)
    device_kind = jax.random.randint(key_kind, (N_DP,), 0, 2)
    device_kind = device_kind.at[0].set(1).at[1].set(0)
    extra_small = jax.random.randint(key_extra, (N_DP,), 0, IMG_CAP - 8)
    extra_small = extra_small.at[0].set(IMG_CAP - 9)
    small_count = jax.random.randint(key_small, (N_DP,), 1, IMG_CAP + 1)
    small_count = small_count.at[1].set(IMG_CAP)
    slot_index = jnp.arange(IMG_CAP, dtype=jnp.int32)[None, :]
    with_large = jnp.where(slot_index == 0, LARGE_LEN, jnp.where(slot_index <= extra_small[:, None], SMALL_LEN, 0))
    only_small = jnp.where(slot_index < small_count[:, None], SMALL_LEN, 0)
    lengths = jnp.where(device_kind[:, None] == 1, with_large, only_small).astype(jnp.int32)
    starts = (jnp.cumsum(lengths, axis=1) - lengths).astype(jnp.int32)
    return (lengths.reshape(-1), starts.reshape(-1))


def draw_img_length(key, part):
    return pack_images(key)[0]


def draw_img_start(key, part):
    return pack_images(key)[1]


def draw_class_count(key, part):
    folded = jax.random.fold_in(key, 23)
    base_count = CLASSES // N_DP
    delta_count = jax.random.randint(folded, (N_DP // 2,), -(base_count - 1), base_count)
    delta_count = delta_count.at[0].set(base_count - 1)
    paired = jnp.stack([base_count + delta_count, base_count - delta_count], axis=1)
    return paired.reshape(-1).astype(jnp.int32)


def raised(array, key, source, target, blocks, factor):
    owner, partner = [(jnp.arange(array.shape[dim]) // (array.shape[dim] // blocks)).reshape([-1 if axis == dim else 1 for axis in range(array.ndim)]) for dim in (source, target)]
    chosen = jax.random.permutation(key, blocks)[partner]
    strong = (owner == chosen) | (owner == (partner + blocks // 2) % blocks)
    return jnp.where(strong, factor * array, array)


def levels(key, shape, cuts, least, high):
    gain, own = 1.0, jax.random.fold_in(key, 6)
    for dim, blocks in cuts:
        steps = jnp.exp(jax.random.uniform(jax.random.fold_in(own, dim), (blocks,), jnp.float32, least / len(cuts), high / len(cuts)))
        gain = gain * jnp.repeat(steps, shape[dim] // blocks).reshape([-1 if axis == dim else 1 for axis in range(len(shape))])
    return gain


def noise(key, dims, scale, limit, cuts=(), held_as=jnp.bfloat16):
    array = jax.random.normal(key, dims, jnp.float32) * scale
    if len(cuts) > 0:
        array = levels(key, dims, cuts, -0.22, 0.18) * array
    return jnp.clip(array, min=-limit, max=limit).astype(held_as)


def gaussian_with(rng, shape, scale, most, cuts, heavy, kind=jnp.bfloat16):
    values = scale * jax.random.normal(rng, shape, jnp.float32)
    if cuts:
        values = values * levels(rng, shape, cuts, -0.22, 0.18)
    return jnp.clip(raised(values, jax.random.fold_in(rng, 3), *heavy), -most, most).astype(kind)


def setup_inputs(seed: int = 0) -> dict:
    keys = jax.random.split(jax.random.key(seed), 20)
    return {
        "patches": gaussian_with(keys[0], (ROWS, D), 1.0, 6.0, ((0, 32),), (0, 1, 32, 2.75)),
        "img_length": draw_img_length(jax.random.fold_in(keys[19], 71), 0),
        "img_start": draw_img_start(jax.random.fold_in(keys[19], 71), 0),
        "class_count": draw_class_count(jax.random.fold_in(keys[19], 71), 0),
        "gain_attend": jnp.clip(1.0 + 0.15 * jax.random.normal(keys[4], (LAYERS, D), jnp.float32), 0.25, 1.75).astype(jnp.bfloat16),
        "shift_attend": noise(keys[5], (LAYERS, D), 0.2, 1.0),
        "qkv_weight": noise(keys[6], (LAYERS, D, 3 * D), D ** -0.5, 0.21875),
        "qv_bias": noise(keys[7], (LAYERS, 2 * D), 0.2, 1.0),
        "out_weight": noise(keys[8], (LAYERS, D, D), (D // 16) ** -0.5, 0.875),
        "out_bias": noise(keys[9], (LAYERS, D), 0.2, 1.0),
        "gain_mlp": jnp.clip(1.0 + 0.15 * jax.random.normal(keys[10], (LAYERS, D), jnp.float32), 0.25, 1.75).astype(jnp.bfloat16),
        "shift_mlp": noise(keys[11], (LAYERS, D), 0.2, 1.0),
        "up_weight": noise(keys[12], (LAYERS, D, FF), D ** -0.5, 0.21875),
        "up_bias": noise(keys[13], (LAYERS, FF), 0.2, 1.0),
        "down_weight": noise(keys[14], (LAYERS, FF, D), FF ** -0.5, 0.109375),
        "down_bias": noise(keys[15], (LAYERS, D), 0.2, 1.0),
        "cls_weight": noise(keys[16], (D, CLS_SLOTS), D ** -0.5, 0.21875, ((1, 32),)),
        "cls_bias": noise(keys[17], (CLS_SLOTS,), 0.5, 2.5, ((0, 32),)),
        "logit_grad": noise(keys[18], (IMAGES, CLS_SLOTS), 8.0, 48.0, ((1, 32),)),
    }


@jax.custom_vjp
def low(v):
    return lax.optimization_barrier(v.astype(jnp.bfloat16)).astype(jnp.float32)

@jax.custom_vjp
def low_back(v):
    return v

def low_keep(v):
    return (low(v), None)

def low_pass(kept, grad):
    return (grad,)

def back_keep(v):
    return (v, None)

def back_low(kept, grad):
    return (low(grad),)
low.defvjp(low_keep, low_pass)
low_back.defvjp(back_keep, back_low)
EPSILON = 1e-06
HIGHEST = lax.Precision.HIGHEST

def product(left, right):
    return jnp.dot(left, right, precision=HIGHEST, preferred_element_type=jnp.float32)

def layer_norm(stream, gain_vector, shift_vector):
    center = stream - lax.optimization_barrier(jnp.mean(stream, axis=-1, keepdims=True))
    spread = lax.optimization_barrier(jnp.mean(center * center, axis=-1, keepdims=True))
    return center * lax.rsqrt(spread + EPSILON) * gain_vector + shift_vector

def both_round(value):
    return low(low_back(value))

def block_forward(stream, weights, same_image):
    gain_one, shift_one, qkv_w, qv_b, out_w, out_b, gain_two, shift_two, up_w, up_b, down_w, down_b = weights
    row_count = stream.shape[0]
    normed = low(layer_norm(stream, gain_one, shift_one))
    zeros_middle = jnp.zeros((D,), jnp.float32)
    joined = product(normed, qkv_w) + jnp.concatenate([qv_b[:D], zeros_middle, qv_b[D:]])
    queries = both_round(joined[:, :D]).reshape(row_count, H, HD)
    keys_all = both_round(joined[:, D:2 * D]).reshape(row_count, H, HD)
    values_all = both_round(joined[:, 2 * D:]).reshape(row_count, H, HD)
    scores = jnp.einsum('qhd,khd->hqk', queries, keys_all, precision=HIGHEST) * HD ** (-0.5)
    scores = low_back(scores)
    scores = jnp.where(same_image[None], scores, -jnp.inf)
    largest = lax.optimization_barrier(jnp.max(scores, axis=-1, keepdims=True))
    exponent = jnp.exp(scores - largest)
    probabilities = exponent / lax.optimization_barrier(jnp.sum(exponent, axis=-1, keepdims=True))
    mixed_values = jnp.einsum('hqk,khd->qhd', low(probabilities), values_all, precision=HIGHEST)
    attended = both_round(mixed_values.reshape(row_count, D))
    middle = stream + low_back(product(attended, out_w) + out_b)
    normed_two = low(layer_norm(middle, gain_two, shift_two))
    hidden = low_back(product(normed_two, up_w) + up_b)
    activated = low(jax.nn.gelu(hidden, approximate=False))
    return middle + low_back(product(activated, down_w) + down_b)

def reference(patches, img_length, img_start, class_count, gain_attend, shift_attend, qkv_weight, qv_bias, out_weight, out_bias, gain_mlp, shift_mlp, up_weight, up_bias, down_weight, down_bias, cls_weight, cls_bias, logit_grad):
    lengths = img_length.reshape(N_DP, IMG_CAP).astype(jnp.int32)
    starts = img_start.reshape(N_DP, IMG_CAP).astype(jnp.int32)
    positions = jnp.arange(TOK, dtype=jnp.int32)
    inside = (positions[None, None, :] >= starts[:, :, None]) & (positions[None, None, :] < (starts + lengths)[:, :, None])
    member = inside.astype(jnp.float32)
    slot_ids = jnp.arange(IMG_CAP, dtype=jnp.int32)
    live_rows = lax.optimization_barrier(jnp.sum(inside.astype(jnp.int32), axis=1))
    segment = lax.optimization_barrier(jnp.sum(inside.astype(jnp.int32) * slot_ids[None, :, None], axis=1)) + (1 - live_rows) * IMG_CAP
    counts = jnp.maximum(lengths, 1).astype(jnp.float32)
    live_columns = (jnp.arange(CLS_CAP, dtype=jnp.int32)[None, :] < class_count.astype(jnp.int32)[:, None]).reshape(CLS_SLOTS)
    params = tuple((weight.astype(jnp.float32) for weight in (gain_attend, shift_attend, qkv_weight, qv_bias, out_weight, out_bias, gain_mlp, shift_mlp, up_weight, up_bias, down_weight, down_bias)))
    streams = patches.astype(jnp.float32).reshape(N_DP, TOK, D)

    def forward(streams, params, class_w, class_b):

        def one_device(pieces):
            stream, member_rows, segment_rows, count_rows = pieces
            same_image = segment_rows[:, None] == segment_rows[None, :]
            for layer_index in range(LAYERS):
                stream = block_forward(stream, tuple((weight[layer_index] for weight in params)), same_image)
            return product(member_rows, stream) / count_rows[:, None]
        pooled = lax.map(jax.checkpoint(one_device), (streams, member, segment, counts)).reshape(IMAGES, D)
        scores = product(low(pooled), class_w) + class_b
        return jnp.where(live_columns[None, :], scores, 0.0)
    logits, backward = jax.vjp(forward, streams, params, cls_weight.astype(jnp.float32), cls_bias.astype(jnp.float32))
    grad_streams, grad_params, grad_class_w, grad_class_b = backward(logit_grad.astype(jnp.float32))
    return (logits, grad_streams.reshape(ROWS, D), grad_params[0], grad_params[1], grad_params[2], grad_params[3], grad_params[4], grad_params[5], grad_params[6], grad_params[7], grad_params[8], grad_params[9], grad_params[10], grad_params[11], grad_class_w, grad_class_b)
```

```python
from functools import partial

import jax
import jax.numpy as jnp
from jax import lax
from jax.experimental import pallas as pl
from jax.experimental.pallas import tpu as pltpu
from jax.sharding import PartitionSpec as P

HD = 64
LAYERS = 2
BIG = 1e30
EPSILON = 1e-06
HIGHEST = lax.Precision.HIGHEST
NT = (((1,), (1,)), ((), ()))
f32 = jnp.float32
bf16 = jnp.bfloat16
VMEM_LIMIT = 56 << 20


def layer_norm(stream, gain_vector, shift_vector):
    center = stream - jnp.mean(stream, axis=-1, keepdims=True)
    spread = jnp.mean(center * center, axis=-1, keepdims=True)
    return center * lax.rsqrt(spread + EPSILON) * gain_vector + shift_vector


def dot32(left, right):
    return jnp.dot(left, right, preferred_element_type=f32)


def dot_nt(left, right):
    return lax.dot_general(left, right, NT, preferred_element_type=f32)


def seg_features(segment, slot_count):
    lane = jnp.arange(128, dtype=jnp.int32) % HD
    hit = segment[:, None] == lane[None, :]
    live = (lane <= slot_count)[None, :]
    query_side = (hit & live).astype(bf16)
    key_side = jnp.where(live & ~hit, -BIG, 0.0).astype(bf16)
    return query_side, key_side


def attend_forward_kernel(q_ref, k_ref, v_ref, fq_ref, fk_ref, o_ref, lse_ref, *, chunk):
    rows = q_ref.shape[0]
    left = lax.broadcasted_iota(jnp.int32, (rows, 128), 1) < HD
    q = q_ref[...] * jnp.asarray(HD**-0.5, bf16)
    k = k_ref[...]
    fq = fq_ref[...]
    fk = fk_ref[...]
    v_t = v_ref[...].T
    q_side = [jnp.where(left, q, fq), jnp.where(left, fq, q)]
    k_side = [jnp.where(left, k, fk), jnp.where(left, fk, k)]
    for c in range(rows // chunk):
        span = slice(c * chunk, (c + 1) * chunk)
        outs = []
        for h in range(2):
            scores = dot_nt(k_side[h], q_side[h][span])
            largest = jnp.max(scores, axis=0, keepdims=True)
            p = jnp.exp(scores - largest)
            total = jnp.sum(p, axis=0, keepdims=True)
            mixed = dot32(v_t[h * HD : (h + 1) * HD], p.astype(bf16))
            outs.append(mixed / total)
            lse_ref[0, h : h + 1, span] = largest + jnp.log(total)
        o_ref[span, :] = jnp.concatenate(outs, axis=0).T.astype(bf16)


def attend_forward(joined, fq, fk):
    rows = joined.shape[0]
    width = joined.shape[1] // 3
    n = width // 128
    col = lambda off: pl.BlockSpec((rows, 128), lambda i, off=off: (0, off + i))
    full = pl.BlockSpec((rows, 128), lambda i: (0, 0))
    return pl.pallas_call(
        partial(attend_forward_kernel, chunk=rows),
        grid=(n,),
        in_specs=[col(0), col(n), col(2 * n), full, full],
        out_specs=[
            pl.BlockSpec((rows, 128), lambda i: (0, i)),
            pl.BlockSpec((1, 2, rows), lambda i: (i, 0, 0)),
        ],
        out_shape=[
            jax.ShapeDtypeStruct((rows, width), bf16),
            jax.ShapeDtypeStruct((n, 2, rows), f32),
        ],
        compiler_params=pltpu.CompilerParams(vmem_limit_bytes=VMEM_LIMIT),
        cost_estimate=pl.CostEstimate(
            flops=16 * rows * rows * width, bytes_accessed=10 * rows * width, transcendentals=0
        ),
        name="attend_forward",
    )(joined, joined, joined, fq, fk)


def attend_backward_kernel(
    q_ref, k_ref, v_ref, g_ref, o_ref, lse_ref, fq_ref, fk_ref, dj_ref, cs_ref, *, chunk
):
    rows = q_ref.shape[0]
    width = dj_ref.shape[1] // 3
    step = pl.program_id(0)
    left = lax.broadcasted_iota(jnp.int32, (rows, 128), 1) < HD
    left_chunk = left[:chunk]
    scale = HD**-0.5
    q = q_ref[...] * jnp.asarray(scale, bf16)
    k = k_ref[...]
    v = v_ref[...]
    g = g_ref[...]
    fq = fq_ref[...]
    fk = fk_ref[...]
    zero = jnp.zeros_like(q)
    k_t = k.T
    product_t = (g.astype(f32) * o_ref[...].astype(f32)).T
    q_side = [jnp.where(left, q, fq), jnp.where(left, fq, q)]
    k_side = [jnp.where(left, k, fk), jnp.where(left, fk, k)]
    v_side = [jnp.where(left, v, zero), jnp.where(left, zero, v)]
    delta = [jnp.sum(product_t[h * HD : (h + 1) * HD], axis=0, keepdims=True) for h in range(2)]
    lse = [lse_ref[0, h : h + 1, :] for h in range(2)]
    dq = [None, None]
    sum_v = jnp.zeros((1, 128), f32)
    for c in range(rows // chunk):
        span = slice(c * chunk, (c + 1) * chunk)
        dk = []
        dv = []
        for h in range(2):
            scores = dot_nt(k_side[h][span], q_side[h])
            p = jnp.exp(scores - lse[h])
            dp = dot_nt(v_side[h][span], g)
            dv.append(dot32(p.astype(bf16), g))
            ds = (p * (dp - delta[h])).astype(bf16)
            dk.append(dot32(ds, q))
            part = dot32(k_t[h * HD : (h + 1) * HD, span], ds)
            dq[h] = part if dq[h] is None else dq[h] + part
        dk_low = jnp.where(left_chunk, dk[0], dk[1]).astype(bf16)
        dv_low = jnp.where(left_chunk, dv[0], dv[1]).astype(bf16)
        dj_ref[span, pl.ds(pl.multiple_of(width + step * 128, 128), 128)] = dk_low
        dj_ref[span, pl.ds(pl.multiple_of(2 * width + step * 128, 128), 128)] = dv_low
        sum_v += jnp.sum(dv_low.astype(f32), axis=0, keepdims=True)
    dq_low = (jnp.concatenate(dq, axis=0) * scale).T.astype(bf16)
    dj_ref[:, pl.ds(pl.multiple_of(step * 128, 128), 128)] = dq_low
    cs_ref[0:1, :] = jnp.sum(dq_low.astype(f32), axis=0, keepdims=True)
    cs_ref[1:2, :] = sum_v


def attend_backward(joined, grad_attended, attended, lse, fq, fk):
    rows = joined.shape[0]
    width = joined.shape[1] // 3
    n = width // 128
    col = lambda off: pl.BlockSpec((rows, 128), lambda i, off=off: (0, off + i))
    full = pl.BlockSpec((rows, 128), lambda i: (0, 0))
    return pl.pallas_call(
        partial(attend_backward_kernel, chunk=rows // 2),
        grid=(n,),
        in_specs=[
            col(0),
            col(n),
            col(2 * n),
            col(0),
            col(0),
            pl.BlockSpec((1, 2, rows), lambda i: (i, 0, 0)),
            full,
            full,
        ],
        out_specs=[
            pl.BlockSpec((rows, 3 * width), lambda i: (0, 0)),
            pl.BlockSpec((2, 128), lambda i: (0, i)),
        ],
        out_shape=[
            jax.ShapeDtypeStruct((rows, 3 * width), bf16),
            jax.ShapeDtypeStruct((2, width), f32),
        ],
        compiler_params=pltpu.CompilerParams(vmem_limit_bytes=VMEM_LIMIT),
        cost_estimate=pl.CostEstimate(
            flops=40 * rows * rows * width, bytes_accessed=16 * rows * width, transcendentals=0
        ),
        name="attend_backward",
    )(joined, joined, joined, grad_attended, attended, lse, fq, fk)


def scatter_sum(blocks, me, order, wire):
    n = blocks.shape[0]
    rest = blocks.shape[1:]
    low_bits = n.bit_length() - 3
    dims = (4,) + (2,) * low_bits
    terms = [blocks.reshape(dims + rest)]
    axes = ["top"] + list(range(low_bits - 1, -1, -1))

    def pick(values, axis, index):
        return lax.dynamic_index_in_dim(values, index, axis, keepdims=False)

    def total(values):
        out = values[0].astype(f32)
        for value in values[1:]:
            out = out + value.astype(f32)
        return out

    for bit in order:
        axis = axes.index(bit)
        mine = (me >> bit) & 1
        sent = total([pick(term, axis, 1 - mine) for term in terms]).astype(wire)
        came = lax.ppermute(sent, "dp", [(i, i ^ (1 << bit)) for i in range(n)])
        terms = [pick(term, axis, mine) for term in terms] + [came]
        axes.remove(bit)
    mine = me >> low_bits
    arrived = []
    for k in range(1, 4):
        sent = total([pick(term, 0, mine ^ k) for term in terms]).astype(wire)
        arrived.append(lax.ppermute(sent, "dp", [(i, i ^ (k << low_bits)) for i in range(n)]))
    return total([pick(term, 0, mine) for term in terms] + arrived)


def reduce_rows(grad, me, n, flip):
    rows, columns = grad.shape
    if n < 8 or n & (n - 1) or (rows // n) % 8:
        return lax.psum_scatter(grad.astype(f32), "dp", scatter_dimension=0, tiled=True)
    low_bits = n.bit_length() - 3
    middle = list(range(1, low_bits))
    order = [0] + (middle[::-1] if flip else middle)
    return scatter_sum(grad.reshape(n, rows // n, columns), me, order, bf16)


def reduce_small(vectors, me, n):
    pieces = [vector.reshape(LAYERS, n, -1).transpose(1, 0, 2).reshape(n, -1) for vector in vectors]
    packed = jnp.concatenate(pieces, axis=1)
    size = packed.shape[1]
    padded = jnp.pad(packed, ((0, 0), (0, -size % 1024))).reshape(n, -1, 128)
    if n < 8 or n & (n - 1):
        mine = lax.psum_scatter(padded, "dp", scatter_dimension=0, tiled=False)
    else:
        mine = scatter_sum(padded, me, list(range(n.bit_length() - 3)), f32)
    flat = mine.reshape(-1)
    outs = []
    start = 0
    for piece in pieces:
        outs.append(flat[start : start + piece.shape[1]].reshape(LAYERS, -1))
        start += piece.shape[1]
    return outs


def layer_forward(stream, weights, fq, fk):
    gain_one, shift_one, qkv_w, qv_b, out_w, out_b, gain_two, shift_two, up_w, up_b, down_w, down_b = weights
    width = stream.shape[1]
    normed = layer_norm(stream, gain_one.astype(f32), shift_one.astype(f32)).astype(bf16)
    bias_full = jnp.concatenate([qv_b[:width], jnp.zeros((width,), bf16), qv_b[width:]]).astype(f32)
    joined = (dot32(normed, qkv_w) + bias_full).astype(bf16)
    attended, lse = attend_forward(joined, fq, fk)
    middle = stream + dot32(attended, out_w) + out_b.astype(f32)
    normed_two = layer_norm(middle, gain_two.astype(f32), shift_two.astype(f32)).astype(bf16)
    hidden = dot32(normed_two, up_w) + up_b.astype(f32)
    activated = jax.nn.gelu(hidden, approximate=False).astype(bf16)
    output = middle + dot32(activated, down_w) + down_b.astype(f32)
    return output, (stream, normed, joined, attended, lse, middle, normed_two, hidden, activated)


def norm_backward(grad_normed, values, gain, shift):
    unused, back = jax.vjp(layer_norm, values, gain.astype(f32), shift.astype(f32))
    return back(grad_normed)


def layer_backward(grad_stream, cache, weights, fq, fk, me, n):
    stream, normed, joined, attended, lse, middle, normed_two, hidden, activated = cache
    gain_one, shift_one, qkv_w, qv_b, out_w, out_b, gain_two, shift_two, up_w, up_b, down_w, down_b = weights
    grad_low = grad_stream.astype(bf16)
    grad_down_w = jnp.einsum("tf,td->fd", activated, grad_low, preferred_element_type=f32).astype(bf16)
    down_sum = reduce_rows(grad_down_w, me, n, False)
    grad_down_b = jnp.sum(grad_low.astype(f32), axis=0)
    grad_activated = dot_nt(grad_low, down_w)
    unused, gelu_back = jax.vjp(partial(jax.nn.gelu, approximate=False), hidden)
    grad_hidden = gelu_back(grad_activated)[0].astype(bf16)
    grad_up_w = jnp.einsum("td,tf->df", normed_two, grad_hidden, preferred_element_type=f32).astype(bf16)
    up_sum = reduce_rows(grad_up_w, me, n, True)
    grad_up_b = jnp.sum(grad_hidden.astype(f32), axis=0)
    grad_normed = dot_nt(grad_hidden, up_w)
    grad_input, grad_gain_two, grad_shift_two = norm_backward(grad_normed, middle, gain_two, shift_two)
    grad_middle = grad_stream + grad_input
    branch = grad_middle.astype(bf16)
    grad_out_w = jnp.einsum("tc,td->cd", attended, branch, preferred_element_type=f32).astype(bf16)
    out_sum = reduce_rows(grad_out_w, me, n, True)
    grad_out_b = jnp.sum(branch.astype(f32), axis=0)
    grad_attended = dot_nt(branch, out_w).astype(bf16)
    grad_joined, column_sums = attend_backward(joined, grad_attended, attended, lse, fq, fk)
    grad_qkv_w = jnp.einsum("td,te->de", normed, grad_joined, preferred_element_type=f32).astype(bf16)
    qkv_sum = reduce_rows(grad_qkv_w, me, n, False)
    grad_qv_b = column_sums.reshape(-1)
    grad_normed = dot_nt(grad_joined, qkv_w)
    grad_input, grad_gain_one, grad_shift_one = norm_backward(grad_normed, stream, gain_one, shift_one)
    small = (
        grad_gain_one,
        grad_shift_one,
        grad_qv_b,
        grad_out_b,
        grad_gain_two,
        grad_shift_two,
        grad_up_b,
        grad_down_b,
    )
    return grad_middle + grad_input, (qkv_sum, out_sum, up_sum, down_sum), small


def local(n, *arguments):
    (
        patches,
        img_length,
        img_start,
        class_count,
        *stacked,
        cls_weight,
        cls_bias,
        logit_grad,
    ) = arguments
    me = lax.axis_index("dp")
    row_count = patches.shape[0]
    slot_count = img_length.shape[0]
    positions = jnp.arange(row_count, dtype=jnp.int32)
    inside = (positions[None, :] >= img_start[:, None]) & (
        positions[None, :] < (img_start + img_length)[:, None]
    )
    member = inside.astype(f32)
    live_rows = jnp.sum(inside.astype(jnp.int32), axis=0)
    segment = (
        jnp.sum(inside.astype(jnp.int32) * jnp.arange(slot_count, dtype=jnp.int32)[:, None], axis=0)
        + (1 - live_rows) * slot_count
    )
    fq, fk = seg_features(segment, slot_count)
    counts = jnp.maximum(img_length, 1).astype(f32)
    live_columns = jnp.arange(cls_weight.shape[1], dtype=jnp.int32) < class_count[0]
    masked_grad = jnp.where(live_columns[None, :], logit_grad, jnp.zeros_like(logit_grad))
    pooled_grad = lax.psum_scatter(
        dot_nt(masked_grad, cls_weight), "dp", scatter_dimension=0, tiled=True
    )
    stream = patches.astype(f32)
    layers = [tuple(weight[layer] for weight in stacked) for layer in range(LAYERS)]
    caches = []
    for weights in layers:
        stream, cache = layer_forward(stream, weights, fq, fk)
        caches.append(cache)
    pooled = (
        jnp.dot(member, stream, precision=HIGHEST, preferred_element_type=f32) / counts[:, None]
    )
    gathered = lax.all_gather(pooled.astype(bf16), "dp", axis=0, tiled=True)
    scores = dot32(gathered, cls_weight) + cls_bias.astype(f32)
    logits = jnp.where(live_columns[None, :], scores, 0.0)
    grad_cls_weight = jnp.einsum("id,ic->dc", gathered, masked_grad, preferred_element_type=f32)
    grad_cls_bias = jnp.sum(masked_grad.astype(f32), axis=0)
    grad_stream = jnp.einsum(
        "it,id->td",
        member,
        pooled_grad / counts[:, None],
        precision=HIGHEST,
        preferred_element_type=f32,
    )
    large = [None] * LAYERS
    small = [None] * LAYERS
    for layer in reversed(range(LAYERS)):
        grad_stream, large[layer], small[layer] = layer_backward(
            grad_stream, caches[layer], layers[layer], fq, fk, me, n
        )
    qkv_sum, out_sum, up_sum, down_sum = (jnp.stack(pair) for pair in zip(*large))
    gain_one, shift_one, qv_b, out_b, gain_two, shift_two, up_b, down_b = reduce_small(
        [jnp.stack(pair) for pair in zip(*small)], me, n
    )
    return (
        logits,
        grad_stream,
        gain_one,
        shift_one,
        qkv_sum,
        qv_b,
        out_sum,
        out_b,
        gain_two,
        shift_two,
        up_sum,
        up_b,
        down_sum,
        down_b,
        grad_cls_weight,
        grad_cls_bias,
    )


def solution(mesh):
    whole = P()
    placed = (
        (P("dp", None), P("dp"), P("dp"), P("dp"))
        + (whole,) * 12
        + (P(None, "dp"), P("dp"), P(None, "dp"))
    )
    vector = P(None, "dp")
    matrix = P(None, "dp", None)
    return jax.shard_map(
        partial(local, mesh.size),
        mesh=mesh,
        in_specs=placed,
        out_specs=(
            P(None, "dp"),
            P("dp", None),
            vector,
            vector,
            matrix,
            vector,
            matrix,
            vector,
            vector,
            vector,
            matrix,
            vector,
            matrix,
            vector,
            P(None, "dp"),
            P("dp"),
        ),
        check_vma=False,
    )
```

```python
from functools import partial

import jax
import jax.numpy as jnp
from jax import lax
from jax.experimental import pallas as pl
from jax.experimental.pallas import tpu as pltpu
from jax.sharding import PartitionSpec as P

HD = 64
LAYERS = 2
BIG = 1e30
EPSILON = 1e-06
HIGHEST = lax.Precision.HIGHEST
NT = (((1,), (1,)), ((), ()))
f32 = jnp.float32
bf16 = jnp.bfloat16
VMEM_LIMIT = 56 << 20


def layer_norm(stream, gain_vector, shift_vector):
    center = stream - jnp.mean(stream, axis=-1, keepdims=True)
    spread = jnp.mean(center * center, axis=-1, keepdims=True)
    return center * lax.rsqrt(spread + EPSILON) * gain_vector + shift_vector


def dot32(left, right):
    return jnp.dot(left, right, preferred_element_type=f32)


def dot_nt(left, right):
    return lax.dot_general(left, right, NT, preferred_element_type=f32)


def seg_features(segment, slot_count):
    lane = jnp.arange(128, dtype=jnp.int32) % HD
    hit = segment[:, None] == lane[None, :]
    live = (lane <= slot_count)[None, :]
    query_side = (hit & live).astype(bf16)
    key_side = jnp.where(live & ~hit, -BIG, 0.0).astype(bf16)
    return query_side, key_side


def attend_forward_kernel(q_ref, k_ref, v_ref, fq_ref, fk_ref, o_ref, lse_ref, *, chunk):
    rows = q_ref.shape[0]
    left = lax.broadcasted_iota(jnp.int32, (rows, 128), 1) < HD
    q = q_ref[...] * jnp.asarray(HD**-0.5, bf16)
    k = k_ref[...]
    fq = fq_ref[...]
    fk = fk_ref[...]
    v_t = v_ref[...].T
    q_side = [jnp.where(left, q, fq), jnp.where(left, fq, q)]
    k_side = [jnp.where(left, k, fk), jnp.where(left, fk, k)]
    for c in range(rows // chunk):
        span = slice(c * chunk, (c + 1) * chunk)
        outs = []
        for h in range(2):
            scores = dot_nt(k_side[h], q_side[h][span])
            largest = jnp.max(scores, axis=0, keepdims=True)
            p = jnp.exp(scores - largest)
            total = jnp.sum(p, axis=0, keepdims=True)
            mixed = dot32(v_t[h * HD : (h + 1) * HD], p.astype(bf16))
            outs.append(mixed / total)
            lse_ref[0, h : h + 1, span] = largest + jnp.log(total)
        o_ref[span, :] = jnp.concatenate(outs, axis=0).T.astype(bf16)


def attend_forward(joined, fq, fk):
    rows = joined.shape[0]
    width = joined.shape[1] // 3
    n = width // 128
    col = lambda off: pl.BlockSpec((rows, 128), lambda i, off=off: (0, off + i))
    full = pl.BlockSpec((rows, 128), lambda i: (0, 0))
    return pl.pallas_call(
        partial(attend_forward_kernel, chunk=rows),
        grid=(n,),
        in_specs=[col(0), col(n), col(2 * n), full, full],
        out_specs=[
            pl.BlockSpec((rows, 128), lambda i: (0, i)),
            pl.BlockSpec((1, 2, rows), lambda i: (i, 0, 0)),
        ],
        out_shape=[
            jax.ShapeDtypeStruct((rows, width), bf16),
            jax.ShapeDtypeStruct((n, 2, rows), f32),
        ],
        compiler_params=pltpu.CompilerParams(vmem_limit_bytes=VMEM_LIMIT),
        cost_estimate=pl.CostEstimate(
            flops=16 * rows * rows * width, bytes_accessed=10 * rows * width, transcendentals=0
        ),
        name="attend_forward",
    )(joined, joined, joined, fq, fk)


def attend_backward_kernel(
    q_ref, k_ref, v_ref, g_ref, o_ref, lse_ref, fq_ref, fk_ref, dj_ref, cs_ref, *, chunk
):
    rows = q_ref.shape[0]
    width = dj_ref.shape[1] // 3
    step = pl.program_id(0)
    left = lax.broadcasted_iota(jnp.int32, (rows, 128), 1) < HD
    left_chunk = left[:chunk]
    scale = HD**-0.5
    q = q_ref[...] * jnp.asarray(scale, bf16)
    k = k_ref[...]
    v = v_ref[...]
    g = g_ref[...]
    fq = fq_ref[...]
    fk = fk_ref[...]
    zero = jnp.zeros_like(q)
    k_t = k.T
    product_t = (g.astype(f32) * o_ref[...].astype(f32)).T
    q_side = [jnp.where(left, q, fq), jnp.where(left, fq, q)]
    k_side = [jnp.where(left, k, fk), jnp.where(left, fk, k)]
    v_side = [jnp.where(left, v, zero), jnp.where(left, zero, v)]
    delta = [jnp.sum(product_t[h * HD : (h + 1) * HD], axis=0, keepdims=True) for h in range(2)]
    lse = [lse_ref[0, h : h + 1, :] for h in range(2)]
    dq = [None, None]
    sum_v = jnp.zeros((1, 128), f32)
    for c in range(rows // chunk):
        span = slice(c * chunk, (c + 1) * chunk)
        dk = []
        dv = []
        for h in range(2):
            scores = dot_nt(k_side[h][span], q_side[h])
            p = jnp.exp(scores - lse[h])
            dp = dot_nt(v_side[h][span], g)
            dv.append(dot32(p.astype(bf16), g))
            ds = (p * (dp - delta[h])).astype(bf16)
            dk.append(dot32(ds, q))
            part = dot32(k_t[h * HD : (h + 1) * HD, span], ds)
            dq[h] = part if dq[h] is None else dq[h] + part
        dk_low = jnp.where(left_chunk, dk[0], dk[1]).astype(bf16)
        dv_low = jnp.where(left_chunk, dv[0], dv[1]).astype(bf16)
        dj_ref[span, pl.ds(pl.multiple_of(width + step * 128, 128), 128)] = dk_low
        dj_ref[span, pl.ds(pl.multiple_of(2 * width + step * 128, 128), 128)] = dv_low
        sum_v += jnp.sum(dv_low.astype(f32), axis=0, keepdims=True)
    dq_low = (jnp.concatenate(dq, axis=0) * scale).T.astype(bf16)
    dj_ref[:, pl.ds(pl.multiple_of(step * 128, 128), 128)] = dq_low
    cs_ref[0:1, :] = jnp.sum(dq_low.astype(f32), axis=0, keepdims=True)
    cs_ref[1:2, :] = sum_v


def attend_backward(joined, grad_attended, attended, lse, fq, fk):
    rows = joined.shape[0]
    width = joined.shape[1] // 3
    n = width // 128
    col = lambda off: pl.BlockSpec((rows, 128), lambda i, off=off: (0, off + i))
    full = pl.BlockSpec((rows, 128), lambda i: (0, 0))
    return pl.pallas_call(
        partial(attend_backward_kernel, chunk=rows // 2),
        grid=(n,),
        in_specs=[
            col(0),
            col(n),
            col(2 * n),
            col(0),
            col(0),
            pl.BlockSpec((1, 2, rows), lambda i: (i, 0, 0)),
            full,
            full,
        ],
        out_specs=[
            pl.BlockSpec((rows, 3 * width), lambda i: (0, 0)),
            pl.BlockSpec((2, 128), lambda i: (0, i)),
        ],
        out_shape=[
            jax.ShapeDtypeStruct((rows, 3 * width), bf16),
            jax.ShapeDtypeStruct((2, width), f32),
        ],
        compiler_params=pltpu.CompilerParams(vmem_limit_bytes=VMEM_LIMIT),
        cost_estimate=pl.CostEstimate(
            flops=40 * rows * rows * width, bytes_accessed=16 * rows * width, transcendentals=0
        ),
        name="attend_backward",
    )(joined, joined, joined, grad_attended, attended, lse, fq, fk)


def suits(n, rows):
    return n >= 8 and n & (n - 1) == 0 and rows % 8 == 0


def middle_bits(n):
    return list(range(1, n.bit_length() - 3))


def total(values):
    out = values[0].astype(f32)
    for value in values[1:]:
        out = out + value.astype(f32)
    return out


def pick(values, axis, index):
    return lax.dynamic_index_in_dim(values, index, axis, keepdims=False)


class ScatterSum:
    def __init__(self, blocks, me, n, flip, wire):
        self.n = n
        self.me = me
        self.wire = wire
        self.low_bits = n.bit_length() - 3
        middle = middle_bits(n)
        self.order = [0] + (middle[::-1] if flip else middle)
        self.axes = ["top"] + list(range(self.low_bits - 1, -1, -1))
        self.terms = [blocks.reshape((4,) + (2,) * self.low_bits + blocks.shape[1:])]
        self.result = None
        self.pending = None

    def sends(self):
        if self.order:
            self.bit = self.order.pop(0)
            self.axis = self.axes.index(self.bit)
            mine = (self.me >> self.bit) & 1
            self.keep = mine
            return [total([pick(t, self.axis, 1 - mine) for t in self.terms]).astype(self.wire)]
        self.bit = None
        self.axis = 0
        mine = self.me >> self.low_bits
        self.keep = mine
        return [total([pick(t, 0, mine ^ k) for t in self.terms]).astype(self.wire) for k in (1, 2, 3)]

    def launch(self, sends):
        if self.bit is not None:
            partners = [1 << self.bit]
        else:
            partners = [k << self.low_bits for k in (1, 2, 3)]
        self.pending = [
            lax.ppermute(sent, "dp", [(i, i ^ p) for i in range(self.n)])
            for sent, p in zip(sends, partners)
        ]

    def land(self, came):
        self.pending = None
        self.terms = [pick(t, self.axis, self.keep) for t in self.terms] + list(came)
        if self.bit is not None:
            self.axes.remove(self.bit)
        else:
            self.result = total(self.terms)


class Gather:
    def __init__(self, block, me, n):
        self.n = n
        self.me = me
        self.bits = list(range(n.bit_length() - 1))
        self.held = block
        self.result = None
        self.pending = None

    def sends(self):
        self.bit = self.bits.pop(0)
        return [self.held]

    def launch(self, sends):
        p = 1 << self.bit
        self.pending = [lax.ppermute(sends[0], "dp", [(i, i ^ p) for i in range(self.n)])]

    def land(self, came):
        self.pending = None
        upper = ((self.me >> self.bit) & 1) == 1
        low = jnp.where(upper, came[0], self.held)
        high = jnp.where(upper, self.held, came[0])
        self.held = jnp.concatenate([low, high], axis=0)
        if not self.bits:
            self.result = self.held


class Done:
    def __init__(self, result):
        self.result = result
        self.pending = None


def fence(main, exchanges):
    flying = [e for e in exchanges if e.pending is not None]
    main, came = lax.optimization_barrier((main, [e.pending for e in flying]))
    for e, values in zip(flying, came):
        e.land(values)
    ready = [e for e in exchanges if e.result is None]
    main, sends = lax.optimization_barrier((main, [e.sends() for e in ready]))
    for e, values in zip(ready, sends):
        e.launch(values)
    return main


def reduce_rows(grad, me, n, flip):
    rows, columns = grad.shape
    if not suits(n, rows // n):
        return Done(lax.psum_scatter(grad.astype(f32), "dp", scatter_dimension=0, tiled=True))
    return ScatterSum(grad.reshape(n, rows // n, columns), me, n, flip, bf16)


def pack_small(vectors, me, n):
    pieces = [vector.reshape(LAYERS, n, -1).transpose(1, 0, 2).reshape(n, -1) for vector in vectors]
    packed = jnp.concatenate(pieces, axis=1)
    padded = jnp.pad(packed, ((0, 0), (0, -packed.shape[1] % 1024))).reshape(n, -1, 128)
    sizes = [piece.shape[1] for piece in pieces]
    if not suits(n, 8):
        return Done(lax.psum_scatter(padded, "dp", scatter_dimension=0, tiled=False)), sizes
    return ScatterSum(padded, me, n, False, f32), sizes


def unpack_small(result, sizes):
    flat = result.reshape(-1)
    outs = []
    start = 0
    for size in sizes:
        outs.append(flat[start : start + size].reshape(LAYERS, -1))
        start += size
    return outs


def layer_forward(stream, weights, fq, fk):
    gain_one, shift_one, qkv_w, qv_b, out_w, out_b, gain_two, shift_two, up_w, up_b, down_w, down_b = weights
    width = stream.shape[1]
    normed = layer_norm(stream, gain_one.astype(f32), shift_one.astype(f32)).astype(bf16)
    bias_full = jnp.concatenate([qv_b[:width], jnp.zeros((width,), bf16), qv_b[width:]]).astype(f32)
    joined = (dot32(normed, qkv_w) + bias_full).astype(bf16)
    attended, lse = attend_forward(joined, fq, fk)
    middle = stream + dot32(attended, out_w) + out_b.astype(f32)
    normed_two = layer_norm(middle, gain_two.astype(f32), shift_two.astype(f32)).astype(bf16)
    hidden = dot32(normed_two, up_w) + up_b.astype(f32)
    activated = jax.nn.gelu(hidden, approximate=False).astype(bf16)
    output = middle + dot32(activated, down_w) + down_b.astype(f32)
    return output, (stream, normed, joined, attended, lse, middle, normed_two, hidden, activated)


def norm_backward(grad_normed, values, gain, shift):
    unused, back = jax.vjp(layer_norm, values, gain.astype(f32), shift.astype(f32))
    return back(grad_normed)


def layer_backward(grad_stream, cache, weights, fq, fk, me, n, live):
    stream, normed, joined, attended, lse, middle, normed_two, hidden, activated = cache
    gain_one, shift_one, qkv_w, qv_b, out_w, out_b, gain_two, shift_two, up_w, up_b, down_w, down_b = weights
    grad_low = grad_stream.astype(bf16)
    grad_down_w = jnp.einsum("tf,td->fd", activated, grad_low, preferred_element_type=f32).astype(bf16)
    grad_down_b = jnp.sum(grad_low.astype(f32), axis=0)
    grad_activated = dot_nt(grad_low, down_w)
    unused, gelu_back = jax.vjp(partial(jax.nn.gelu, approximate=False), hidden)
    grad_hidden = gelu_back(grad_activated)[0].astype(bf16)
    grad_up_w = jnp.einsum("td,tf->df", normed_two, grad_hidden, preferred_element_type=f32).astype(bf16)
    grad_up_b = jnp.sum(grad_hidden.astype(f32), axis=0)
    down_sum = reduce_rows(grad_down_w, me, n, False)
    up_sum = reduce_rows(grad_up_w, me, n, True)
    live += [down_sum, up_sum]
    grad_hidden = fence(grad_hidden, live)
    grad_normed = dot_nt(grad_hidden, up_w)
    grad_input, grad_gain_two, grad_shift_two = norm_backward(grad_normed, middle, gain_two, shift_two)
    grad_middle = grad_stream + grad_input
    branch = grad_middle.astype(bf16)
    grad_out_w = jnp.einsum("tc,td->cd", attended, branch, preferred_element_type=f32).astype(bf16)
    grad_out_b = jnp.sum(branch.astype(f32), axis=0)
    grad_attended = dot_nt(branch, out_w).astype(bf16)
    out_sum = reduce_rows(grad_out_w, me, n, True)
    live.append(out_sum)
    grad_attended = fence(grad_attended, live)
    grad_joined, column_sums = attend_backward(joined, grad_attended, attended, lse, fq, fk)
    grad_joined = fence(grad_joined, live)
    grad_qkv_w = jnp.einsum("td,te->de", normed, grad_joined, preferred_element_type=f32).astype(bf16)
    half = grad_qkv_w.shape[1] // 2
    qkv_sums = [
        reduce_rows(grad_qkv_w[:, :half], me, n, False),
        reduce_rows(grad_qkv_w[:, half:], me, n, True),
    ]
    live += qkv_sums
    grad_joined = fence(grad_joined, qkv_sums)
    grad_qv_b = column_sums.reshape(-1)
    grad_normed = dot_nt(grad_joined, qkv_w)
    grad_normed = fence(grad_normed, live)
    grad_input, grad_gain_one, grad_shift_one = norm_backward(grad_normed, stream, gain_one, shift_one)
    small = (
        grad_gain_one,
        grad_shift_one,
        grad_qv_b,
        grad_out_b,
        grad_gain_two,
        grad_shift_two,
        grad_up_b,
        grad_down_b,
    )
    return grad_middle + grad_input, (qkv_sums, out_sum, up_sum, down_sum), small


def local(n, *arguments):
    (
        patches,
        img_length,
        img_start,
        class_count,
        *stacked,
        cls_weight,
        cls_bias,
        logit_grad,
    ) = arguments
    me = lax.axis_index("dp")
    row_count = patches.shape[0]
    slot_count = img_length.shape[0]
    positions = jnp.arange(row_count, dtype=jnp.int32)
    inside = (positions[None, :] >= img_start[:, None]) & (
        positions[None, :] < (img_start + img_length)[:, None]
    )
    member = inside.astype(f32)
    live_rows = jnp.sum(inside.astype(jnp.int32), axis=0)
    segment = (
        jnp.sum(inside.astype(jnp.int32) * jnp.arange(slot_count, dtype=jnp.int32)[:, None], axis=0)
        + (1 - live_rows) * slot_count
    )
    fq, fk = seg_features(segment, slot_count)
    counts = jnp.maximum(img_length, 1).astype(f32)
    live_columns = jnp.arange(cls_weight.shape[1], dtype=jnp.int32) < class_count[0]
    masked_grad = jnp.where(live_columns[None, :], logit_grad, jnp.zeros_like(logit_grad))
    pooled_grad = lax.psum_scatter(
        dot_nt(masked_grad, cls_weight), "dp", scatter_dimension=0, tiled=True
    )
    stream = patches.astype(f32)
    layers = [tuple(weight[layer] for weight in stacked) for layer in range(LAYERS)]
    caches = []
    for weights in layers:
        stream, cache = layer_forward(stream, weights, fq, fk)
        caches.append(cache)
    pooled = (
        jnp.dot(member, stream, precision=HIGHEST, preferred_element_type=f32) / counts[:, None]
    )
    low_pooled = pooled.astype(bf16)
    if suits(n, 8):
        gather = Gather(low_pooled, me, n)
    else:
        gather = Done(lax.all_gather(low_pooled, "dp", axis=0, tiled=True))
    grad_stream = jnp.einsum(
        "it,id->td",
        member,
        pooled_grad / counts[:, None],
        precision=HIGHEST,
        preferred_element_type=f32,
    )
    live = [gather]
    grad_stream = fence(grad_stream, live)
    large = [None] * LAYERS
    small = [None] * LAYERS
    for layer in reversed(range(LAYERS)):
        grad_stream, large[layer], small[layer] = layer_backward(
            grad_stream, caches[layer], layers[layer], fq, fk, me, n, live
        )
    small_sum, sizes = pack_small([jnp.stack(pair) for pair in zip(*small)], me, n)
    live.append(small_sum)
    while any(e.result is None for e in live):
        grad_stream = fence(grad_stream, live)
    gathered = gather.result
    scores = dot32(gathered, cls_weight) + cls_bias.astype(f32)
    logits = jnp.where(live_columns[None, :], scores, 0.0)
    grad_cls_weight = jnp.einsum("id,ic->dc", gathered, masked_grad, preferred_element_type=f32)
    grad_cls_bias = jnp.sum(masked_grad.astype(f32), axis=0)
    qkv_sums, out_sum, up_sum, down_sum = zip(*large)
    qkv_sum = jnp.stack([jnp.concatenate([e.result for e in pair], axis=1) for pair in qkv_sums])
    out_sum, up_sum, down_sum = (
        jnp.stack([e.result for e in pair]) for pair in (out_sum, up_sum, down_sum)
    )
    gain_one, shift_one, qv_b, out_b, gain_two, shift_two, up_b, down_b = unpack_small(
        small_sum.result, sizes
    )
    return (
        logits,
        grad_stream,
        gain_one,
        shift_one,
        qkv_sum,
        qv_b,
        out_sum,
        out_b,
        gain_two,
        shift_two,
        up_sum,
        up_b,
        down_sum,
        down_b,
        grad_cls_weight,
        grad_cls_bias,
    )


def solution(mesh):
    whole = P()
    placed = (
        (P("dp", None), P("dp"), P("dp"), P("dp"))
        + (whole,) * 12
        + (P(None, "dp"), P("dp"), P(None, "dp"))
    )
    vector = P(None, "dp")
    matrix = P(None, "dp", None)
    return jax.shard_map(
        partial(local, mesh.size),
        mesh=mesh,
        in_specs=placed,
        out_specs=(
            P(None, "dp"),
            P("dp", None),
            vector,
            vector,
            matrix,
            vector,
            matrix,
            vector,
            vector,
            vector,
            matrix,
            vector,
            matrix,
            vector,
            P(None, "dp"),
            P("dp"),
        ),
        check_vma=False,
    )
```

```python
from functools import partial

import jax
import jax.numpy as jnp
from jax import lax
from jax.experimental import pallas as pl
from jax.experimental.pallas import tpu as pltpu
from jax.sharding import PartitionSpec as P

HD = 64
LAYERS = 2
BIG = 1e30
EPSILON = 1e-06
HIGHEST = lax.Precision.HIGHEST
NT = (((1,), (1,)), ((), ()))
f32 = jnp.float32
bf16 = jnp.bfloat16
VMEM_LIMIT = 56 << 20


def layer_norm(stream, gain_vector, shift_vector):
    center = stream - jnp.mean(stream, axis=-1, keepdims=True)
    spread = jnp.mean(center * center, axis=-1, keepdims=True)
    return center * lax.rsqrt(spread + EPSILON) * gain_vector + shift_vector


def dot32(left, right):
    return jnp.dot(left, right, preferred_element_type=f32)


def dot_nt(left, right):
    return lax.dot_general(left, right, NT, preferred_element_type=f32)


def seg_features(segment, slot_count):
    lane = jnp.arange(128, dtype=jnp.int32) % HD
    hit = segment[:, None] == lane[None, :]
    live = (lane <= slot_count)[None, :]
    query_side = (hit & live).astype(bf16)
    key_side = jnp.where(live & ~hit, -BIG, 0.0).astype(bf16)
    return query_side, key_side


def attend_forward_kernel(q_ref, k_ref, v_ref, fq_ref, fk_ref, o_ref, lse_ref, *, chunk):
    rows = q_ref.shape[0]
    left = lax.broadcasted_iota(jnp.int32, (rows, 128), 1) < HD
    q = q_ref[...] * jnp.asarray(HD**-0.5, bf16)
    k = k_ref[...]
    fq = fq_ref[...]
    fk = fk_ref[...]
    v_t = v_ref[...].T
    q_side = [jnp.where(left, q, fq), jnp.where(left, fq, q)]
    k_side = [jnp.where(left, k, fk), jnp.where(left, fk, k)]
    for c in range(rows // chunk):
        span = slice(c * chunk, (c + 1) * chunk)
        outs = []
        for h in range(2):
            scores = dot_nt(k_side[h], q_side[h][span])
            largest = jnp.max(scores, axis=0, keepdims=True)
            p = jnp.exp(scores - largest)
            total = jnp.sum(p, axis=0, keepdims=True)
            mixed = dot32(v_t[h * HD : (h + 1) * HD], p.astype(bf16))
            outs.append(mixed / total)
            lse_ref[0, h : h + 1, span] = largest + jnp.log(total)
        o_ref[span, :] = jnp.concatenate(outs, axis=0).T.astype(bf16)


def attend_forward(joined, fq, fk):
    rows = joined.shape[0]
    width = joined.shape[1] // 3
    n = width // 128
    col = lambda off: pl.BlockSpec((rows, 128), lambda i, off=off: (0, off + i))
    full = pl.BlockSpec((rows, 128), lambda i: (0, 0))
    return pl.pallas_call(
        partial(attend_forward_kernel, chunk=rows),
        grid=(n,),
        in_specs=[col(0), col(n), col(2 * n), full, full],
        out_specs=[
            pl.BlockSpec((rows, 128), lambda i: (0, i)),
            pl.BlockSpec((1, 2, rows), lambda i: (i, 0, 0)),
        ],
        out_shape=[
            jax.ShapeDtypeStruct((rows, width), bf16),
            jax.ShapeDtypeStruct((n, 2, rows), f32),
        ],
        compiler_params=pltpu.CompilerParams(vmem_limit_bytes=VMEM_LIMIT),
        cost_estimate=pl.CostEstimate(
            flops=16 * rows * rows * width, bytes_accessed=10 * rows * width, transcendentals=0
        ),
        name="attend_forward",
    )(joined, joined, joined, fq, fk)


def attend_backward_kernel(
    q_ref, k_ref, v_ref, g_ref, o_ref, lse_ref, fq_ref, fk_ref, dj_ref, cs_ref, *, chunk
):
    rows = q_ref.shape[0]
    width = dj_ref.shape[1] // 3
    step = pl.program_id(0)
    left = lax.broadcasted_iota(jnp.int32, (rows, 128), 1) < HD
    left_chunk = left[:chunk]
    scale = HD**-0.5
    q = q_ref[...] * jnp.asarray(scale, bf16)
    k = k_ref[...]
    v = v_ref[...]
    g = g_ref[...]
    fq = fq_ref[...]
    fk = fk_ref[...]
    zero = jnp.zeros_like(q)
    k_t = k.T
    product_t = (g.astype(f32) * o_ref[...].astype(f32)).T
    q_side = [jnp.where(left, q, fq), jnp.where(left, fq, q)]
    k_side = [jnp.where(left, k, fk), jnp.where(left, fk, k)]
    v_side = [jnp.where(left, v, zero), jnp.where(left, zero, v)]
    delta = [jnp.sum(product_t[h * HD : (h + 1) * HD], axis=0, keepdims=True) for h in range(2)]
    lse = [lse_ref[0, h : h + 1, :] for h in range(2)]
    dq = [None, None]
    sum_v = jnp.zeros((1, 128), f32)
    for c in range(rows // chunk):
        span = slice(c * chunk, (c + 1) * chunk)
        dk = []
        dv = []
        for h in range(2):
            scores = dot_nt(k_side[h][span], q_side[h])
            p = jnp.exp(scores - lse[h])
            dp = dot_nt(v_side[h][span], g)
            dv.append(dot32(p.astype(bf16), g))
            ds = (p * (dp - delta[h])).astype(bf16)
            dk.append(dot32(ds, q))
            part = dot32(k_t[h * HD : (h + 1) * HD, span], ds)
            dq[h] = part if dq[h] is None else dq[h] + part
        dk_low = jnp.where(left_chunk, dk[0], dk[1]).astype(bf16)
        dv_low = jnp.where(left_chunk, dv[0], dv[1]).astype(bf16)
        dj_ref[span, pl.ds(pl.multiple_of(width + step * 128, 128), 128)] = dk_low
        dj_ref[span, pl.ds(pl.multiple_of(2 * width + step * 128, 128), 128)] = dv_low
        sum_v += jnp.sum(dv_low.astype(f32), axis=0, keepdims=True)
    dq_low = (jnp.concatenate(dq, axis=0) * scale).T.astype(bf16)
    dj_ref[:, pl.ds(pl.multiple_of(step * 128, 128), 128)] = dq_low
    cs_ref[0:1, :] = jnp.sum(dq_low.astype(f32), axis=0, keepdims=True)
    cs_ref[1:2, :] = sum_v


def attend_backward(joined, grad_attended, attended, lse, fq, fk):
    rows = joined.shape[0]
    width = joined.shape[1] // 3
    n = width // 128
    col = lambda off: pl.BlockSpec((rows, 128), lambda i, off=off: (0, off + i))
    full = pl.BlockSpec((rows, 128), lambda i: (0, 0))
    return pl.pallas_call(
        partial(attend_backward_kernel, chunk=rows // 2),
        grid=(n,),
        in_specs=[
            col(0),
            col(n),
            col(2 * n),
            col(0),
            col(0),
            pl.BlockSpec((1, 2, rows), lambda i: (i, 0, 0)),
            full,
            full,
        ],
        out_specs=[
            pl.BlockSpec((rows, 3 * width), lambda i: (0, 0)),
            pl.BlockSpec((2, 128), lambda i: (0, i)),
        ],
        out_shape=[
            jax.ShapeDtypeStruct((rows, 3 * width), bf16),
            jax.ShapeDtypeStruct((2, width), f32),
        ],
        compiler_params=pltpu.CompilerParams(vmem_limit_bytes=VMEM_LIMIT),
        cost_estimate=pl.CostEstimate(
            flops=40 * rows * rows * width, bytes_accessed=16 * rows * width, transcendentals=0
        ),
        name="attend_backward",
    )(joined, joined, joined, grad_attended, attended, lse, fq, fk)


def total(values):
    out = values[0].astype(f32)
    for value in values[1:]:
        out = out + value.astype(f32)
    return out


def pick(values, axis, index):
    return lax.dynamic_index_in_dim(values, index, axis, keepdims=False)


def pack(grads, n, width):
    pieces = []
    for grad in grads:
        rows, columns = grad.shape
        blocks = grad.reshape(n, rows // n, columns)
        pieces += [blocks[:, :, at : at + width] for at in range(0, columns, width)]
    return jnp.concatenate(pieces, axis=1)


def unpack(packed, shapes, n):
    width = packed.shape[1]
    outs = []
    start = 0
    for rows, columns in shapes:
        count = rows // n
        pieces = []
        for unused in range(0, columns, width):
            pieces.append(packed[start : start + count])
            start += count
        outs.append(jnp.concatenate(pieces, axis=1))
    return outs


class PairSum:
    def __init__(self, a, b, me):
        self.me = me
        self.n = a.shape[0]
        self.rows = a.shape[1]
        dims = (4, 2, 2, 2)
        self.terms = [[a.reshape(dims + a.shape[1:])], [b.reshape(dims + b.shape[1:])]]
        self.round = 0
        self.result = None
        self.pending = None

    def bit(self, at):
        return (self.me >> at) & 1

    def steps(self):
        x, y = self.bit(1), self.bit(2)
        core = self.bit(0)
        top = self.me >> 3
        return [((3, core), (3, core)), ((2, x), (1, y)), ((1, y), (1, x)), ((0, top), (0, top))][self.round]

    def part(self, which, other):
        axis, mine = self.steps()[which]
        return total([pick(t, axis, mine ^ other) for t in self.terms[which]]).astype(bf16)

    def sends(self):
        if self.round == 0:
            return [jnp.concatenate([self.part(0, 1), self.part(1, 1)], axis=-2)]
        if self.round < 3:
            return [self.part(0, 1), self.part(1, 1)]
        return [jnp.concatenate([self.part(0, k), self.part(1, k)], axis=-2) for k in (1, 2, 3)]

    def launch(self, sends):
        partners = [[1], [2, 4], [4, 2], [8, 16, 24]][self.round]
        self.pending = [
            lax.ppermute(sent, "dp", [(i, i ^ p) for i in range(self.n)])
            for sent, p in zip(sends, partners)
        ]

    def land(self, came):
        self.pending = None
        steps = self.steps()
        if self.round in (0, 3):
            came = [
                [value[..., : self.rows, :] for value in came],
                [value[..., self.rows :, :] for value in came],
            ]
        else:
            came = [[came[0]], [came[1]]]
        for which in (0, 1):
            axis, mine = steps[which]
            self.terms[which] = [pick(t, axis, mine) for t in self.terms[which]] + came[which]
        self.round += 1
        if self.round == 4:
            self.result = [total(self.terms[0]), total(self.terms[1])]


class Scattered:
    def __init__(self, a, b):
        both = jnp.concatenate([a, b], axis=1)
        out = lax.psum_scatter(both, "dp", scatter_dimension=0, tiled=False).astype(f32)
        self.result = [out[: a.shape[1]], out[a.shape[1] :]]
        self.pending = None


def pair_sum(a, b, me, n):
    if n == 32 and a.shape[1] % 8 == 0 and b.shape[1] % 8 == 0:
        return PairSum(a, b, me)
    return Scattered(a, b)


def fence(main, exchanges):
    flying = [e for e in exchanges if e.pending is not None]
    main, came = lax.optimization_barrier((main, [e.pending for e in flying]))
    for e, values in zip(flying, came):
        e.land(values)
    ready = [e for e in exchanges if e.result is None]
    main, sends = lax.optimization_barrier((main, [e.sends() for e in ready]))
    for e, values in zip(ready, sends):
        e.launch(values)
    return main


def pack_small(vectors, n, width):
    pieces = [vector.reshape(LAYERS, n, -1).transpose(1, 0, 2).reshape(n, -1) for vector in vectors]
    packed = jnp.concatenate(pieces, axis=1).astype(bf16)
    padded = jnp.pad(packed, ((0, 0), (0, -packed.shape[1] % (8 * width))))
    return padded.reshape(n, -1, width), [piece.shape[1] for piece in pieces]


def unpack_small(block, sizes):
    flat = block.reshape(-1)
    outs = []
    start = 0
    for size in sizes:
        outs.append(flat[start : start + size].reshape(LAYERS, -1))
        start += size
    return outs


def layer_forward(stream, weights, fq, fk):
    gain_one, shift_one, qkv_w, qv_b, out_w, out_b, gain_two, shift_two, up_w, up_b, down_w, down_b = weights
    width = stream.shape[1]
    normed = layer_norm(stream, gain_one.astype(f32), shift_one.astype(f32)).astype(bf16)
    bias_full = jnp.concatenate([qv_b[:width], jnp.zeros((width,), bf16), qv_b[width:]]).astype(f32)
    joined = (dot32(normed, qkv_w) + bias_full).astype(bf16)
    attended, lse = attend_forward(joined, fq, fk)
    middle = stream + dot32(attended, out_w) + out_b.astype(f32)
    normed_two = layer_norm(middle, gain_two.astype(f32), shift_two.astype(f32)).astype(bf16)
    hidden = dot32(normed_two, up_w) + up_b.astype(f32)
    activated = jax.nn.gelu(hidden, approximate=False).astype(bf16)
    output = middle + dot32(activated, down_w) + down_b.astype(f32)
    return output, (stream, normed, joined, attended, lse, middle, normed_two, hidden, activated)


def norm_backward(grad_normed, values, gain, shift):
    unused, back = jax.vjp(layer_norm, values, gain.astype(f32), shift.astype(f32))
    return back(grad_normed)


def layer_backward(grad_stream, cache, weights, fq, fk, tie):
    stream, normed, joined, attended, lse, middle, normed_two, hidden, activated = cache
    gain_one, shift_one, qkv_w, qv_b, out_w, out_b, gain_two, shift_two, up_w, up_b, down_w, down_b = weights
    grad_low = grad_stream.astype(bf16)
    grad_down_w = jnp.einsum("tf,td->fd", activated, grad_low, preferred_element_type=f32).astype(bf16)
    grad_down_b = jnp.sum(grad_low.astype(f32), axis=0)
    grad_activated = dot_nt(grad_low, down_w)
    unused, gelu_back = jax.vjp(partial(jax.nn.gelu, approximate=False), hidden)
    grad_hidden = gelu_back(grad_activated)[0].astype(bf16)
    grad_up_w = jnp.einsum("td,tf->df", normed_two, grad_hidden, preferred_element_type=f32).astype(bf16)
    grad_up_b = jnp.sum(grad_hidden.astype(f32), axis=0)
    grad_hidden = tie("hidden", grad_hidden, (grad_down_w, grad_up_w))
    grad_normed = dot_nt(grad_hidden, up_w)
    grad_input, grad_gain_two, grad_shift_two = norm_backward(grad_normed, middle, gain_two, shift_two)
    grad_middle = grad_stream + grad_input
    branch = grad_middle.astype(bf16)
    grad_out_w = jnp.einsum("tc,td->cd", attended, branch, preferred_element_type=f32).astype(bf16)
    grad_out_b = jnp.sum(branch.astype(f32), axis=0)
    grad_attended = dot_nt(branch, out_w).astype(bf16)
    grad_attended = tie("attended", grad_attended, (grad_out_w,))
    grad_joined, column_sums = attend_backward(joined, grad_attended, attended, lse, fq, fk)
    grad_joined = tie("joined", grad_joined, ())
    grad_qkv_w = jnp.einsum("td,te->de", normed, grad_joined, preferred_element_type=f32).astype(bf16)
    grad_joined = tie("qkv", grad_joined, (grad_qkv_w,))
    grad_qv_b = column_sums.reshape(-1)
    grad_normed = dot_nt(grad_joined, qkv_w)
    grad_input, grad_gain_one, grad_shift_one = norm_backward(grad_normed, stream, gain_one, shift_one)
    small = (
        grad_gain_one,
        grad_shift_one,
        grad_qv_b,
        grad_out_b,
        grad_gain_two,
        grad_shift_two,
        grad_up_b,
        grad_down_b,
    )
    return grad_middle + grad_input, (grad_qkv_w, grad_out_w, grad_up_w, grad_down_w), small


def local(n, *arguments):
    (
        patches,
        img_length,
        img_start,
        class_count,
        *stacked,
        cls_weight,
        cls_bias,
        logit_grad,
    ) = arguments
    me = lax.axis_index("dp")
    row_count, width = patches.shape
    up_width = stacked[8].shape[2]
    slot_count = img_length.shape[0]
    positions = jnp.arange(row_count, dtype=jnp.int32)
    inside = (positions[None, :] >= img_start[:, None]) & (
        positions[None, :] < (img_start + img_length)[:, None]
    )
    member = inside.astype(f32)
    live_rows = jnp.sum(inside.astype(jnp.int32), axis=0)
    segment = (
        jnp.sum(inside.astype(jnp.int32) * jnp.arange(slot_count, dtype=jnp.int32)[:, None], axis=0)
        + (1 - live_rows) * slot_count
    )
    fq, fk = seg_features(segment, slot_count)
    counts = jnp.maximum(img_length, 1).astype(f32)
    live_columns = jnp.arange(cls_weight.shape[1], dtype=jnp.int32) < class_count[0]
    masked_grad = jnp.where(live_columns[None, :], logit_grad, jnp.zeros_like(logit_grad))
    pooled_grad = lax.psum_scatter(
        dot_nt(masked_grad, cls_weight), "dp", scatter_dimension=0, tiled=True
    )
    stream = patches.astype(f32)
    layers = [tuple(weight[layer] for weight in stacked) for layer in range(LAYERS)]
    caches = []
    for weights in layers:
        stream, cache = layer_forward(stream, weights, fq, fk)
        caches.append(cache)
    sums = jnp.dot(member, stream, precision=HIGHEST, preferred_element_type=f32)
    side = jnp.broadcast_to(counts[:, None], (slot_count, 128))
    gathered = lax.all_gather(jnp.concatenate([sums, side], axis=1), "dp", axis=0, tiled=True)
    grad_stream = jnp.einsum(
        "it,id->td",
        member,
        pooled_grad / counts[:, None],
        precision=HIGHEST,
        preferred_element_type=f32,
    )
    last = {}

    def tie_last(name, value, grads):
        last[name] = grads
        if name != "qkv":
            return value
        both = pack(last["hidden"] + last["attended"] + grads, n, width)
        value, both = lax.optimization_barrier((value, both))
        last["sum"] = lax.psum_scatter(both, "dp", scatter_dimension=0, tiled=False)
        return value

    def tie_first(name, value, grads):
        if name == "hidden":
            first.append(pair_sum(pack(grads[:1], n, width), pack(grads[1:], n, width), me, n))
        if name == "qkv":
            return value
        return fence(value, first)

    first = []
    grad_stream, unused, small_last = layer_backward(grad_stream, caches[1], layers[1], fq, fk, tie_last)
    grad_stream, gathered = lax.optimization_barrier((grad_stream, gathered))
    grad_stream, grads, small_first = layer_backward(grad_stream, caches[0], layers[0], fq, fk, tie_first)
    grad_stream, last["sum"] = lax.optimization_barrier((grad_stream, last["sum"]))
    grad_qkv_w, grad_out_w = grads[:2]
    small, sizes = pack_small([jnp.stack(pair) for pair in zip(small_first, small_last)], n, width)
    qk = 2 * width
    side_a = jnp.concatenate([pack([grad_qkv_w[:, :qk]], n, width), small], axis=1)
    side_b = pack([grad_qkv_w[:, qk:], grad_out_w], n, width)
    first.append(pair_sum(side_a, side_b, me, n))
    while any(e.result is None for e in first):
        grad_stream = fence(grad_stream, first)
    gathered = (gathered[:, :width] / gathered[:, width : width + 1]).astype(bf16)
    scores = dot32(gathered, cls_weight) + cls_bias.astype(f32)
    logits = jnp.where(live_columns[None, :], scores, 0.0)
    grad_cls_weight = jnp.einsum("id,ic->dc", gathered, masked_grad, preferred_element_type=f32)
    grad_cls_bias = jnp.sum(masked_grad.astype(f32), axis=0)
    square = (width, width)
    wide = (width, up_width)
    tall = (up_width, width)
    down_last, up_last, out_last, qkv_last = unpack(
        last["sum"].astype(f32), [tall, wide, square, (width, 3 * width)], n
    )
    (down_first,) = unpack(first[0].result[0], [tall], n)
    (up_first,) = unpack(first[0].result[1], [wide], n)
    (qk_first,) = unpack(first[1].result[0][: 2 * (width // n)], [(width, qk)], n)
    v_first, out_first = unpack(first[1].result[1], [square, square], n)
    qkv_first = jnp.concatenate([qk_first, v_first], axis=1)
    qkv_sum = jnp.stack([qkv_first, qkv_last])
    out_sum = jnp.stack([out_first, out_last])
    up_sum = jnp.stack([up_first, up_last])
    down_sum = jnp.stack([down_first, down_last])
    gain_one, shift_one, qv_b, out_b, gain_two, shift_two, up_b, down_b = unpack_small(
        first[1].result[0][2 * (width // n) :], sizes
    )
    return (
        logits,
        grad_stream,
        gain_one,
        shift_one,
        qkv_sum,
        qv_b,
        out_sum,
        out_b,
        gain_two,
        shift_two,
        up_sum,
        up_b,
        down_sum,
        down_b,
        grad_cls_weight,
        grad_cls_bias,
    )


def solution(mesh):
    whole = P()
    placed = (
        (P("dp", None), P("dp"), P("dp"), P("dp"))
        + (whole,) * 12
        + (P(None, "dp"), P("dp"), P(None, "dp"))
    )
    vector = P(None, "dp")
    matrix = P(None, "dp", None)
    return jax.shard_map(
        partial(local, mesh.size),
        mesh=mesh,
        in_specs=placed,
        out_specs=(
            P(None, "dp"),
            P("dp", None),
            vector,
            vector,
            matrix,
            vector,
            matrix,
            vector,
            vector,
            vector,
            matrix,
            vector,
            matrix,
            vector,
            P(None, "dp"),
            P("dp"),
        ),
        check_vma=False,
    )
```

```python
from functools import partial

import jax
import jax.numpy as jnp
from jax import lax
from jax.experimental import pallas as pl
from jax.experimental.pallas import tpu as pltpu
from jax.sharding import PartitionSpec as P

HD = 64
LAYERS = 2
BIG = 1e30
EPSILON = 1e-06
HIGHEST = lax.Precision.HIGHEST
NT = (((1,), (1,)), ((), ()))
f32 = jnp.float32
bf16 = jnp.bfloat16
VMEM_LIMIT = 56 << 20
ROWS_STEP = 256


def dot32(left, right):
    return jnp.dot(left, right, preferred_element_type=f32)


def dot_nt(left, right):
    return lax.dot_general(left, right, NT, preferred_element_type=f32)


def seg_features(segment, slot_count):
    lane = jnp.arange(128, dtype=jnp.int32) % HD
    hit = segment[:, None] == lane[None, :]
    live = (lane <= slot_count)[None, :]
    query_side = (hit & live).astype(bf16)
    key_side = jnp.where(live & ~hit, -BIG, 0.0).astype(bf16)
    return query_side, key_side


def attend_forward_kernel(q_ref, k_ref, v_ref, fq_ref, fk_ref, o_ref, lse_ref, *, chunk):
    rows = q_ref.shape[0]
    left = lax.broadcasted_iota(jnp.int32, (rows, 128), 1) < HD
    q = q_ref[...] * jnp.asarray(HD**-0.5, bf16)
    k = k_ref[...]
    fq = fq_ref[...]
    fk = fk_ref[...]
    v_t = v_ref[...].T
    q_side = [jnp.where(left, q, fq), jnp.where(left, fq, q)]
    k_side = [jnp.where(left, k, fk), jnp.where(left, fk, k)]
    for c in range(rows // chunk):
        span = slice(c * chunk, (c + 1) * chunk)
        outs = []
        for h in range(2):
            scores = dot_nt(k_side[h], q_side[h][span])
            largest = jnp.max(scores, axis=0, keepdims=True)
            p = jnp.exp(scores - largest)
            total = jnp.sum(p, axis=0, keepdims=True)
            mixed = dot32(v_t[h * HD : (h + 1) * HD], p.astype(bf16))
            outs.append(mixed / total)
            lse_ref[0, h : h + 1, span] = largest + jnp.log(total)
        o_ref[span, :] = jnp.concatenate(outs, axis=0).T.astype(bf16)


def attend_forward(joined, fq, fk):
    rows = joined.shape[0]
    width = joined.shape[1] // 3
    n = width // 128
    col = lambda off: pl.BlockSpec((rows, 128), lambda i, off=off: (0, off + i))
    full = pl.BlockSpec((rows, 128), lambda i: (0, 0))
    return pl.pallas_call(
        partial(attend_forward_kernel, chunk=rows),
        grid=(n,),
        in_specs=[col(0), col(n), col(2 * n), full, full],
        out_specs=[
            pl.BlockSpec((rows, 128), lambda i: (0, i)),
            pl.BlockSpec((1, 2, rows), lambda i: (i, 0, 0)),
        ],
        out_shape=[
            jax.ShapeDtypeStruct((rows, width), bf16),
            jax.ShapeDtypeStruct((n, 2, rows), f32),
        ],
        compiler_params=pltpu.CompilerParams(vmem_limit_bytes=VMEM_LIMIT),
        cost_estimate=pl.CostEstimate(
            flops=16 * rows * rows * width, bytes_accessed=10 * rows * width, transcendentals=0
        ),
        name="attend_forward",
    )(joined, joined, joined, fq, fk)


def attend_backward_kernel(
    q_ref, k_ref, v_ref, g_ref, o_ref, lse_ref, fq_ref, fk_ref, dj_ref, cs_ref, *, chunk
):
    rows = q_ref.shape[0]
    width = dj_ref.shape[1] // 3
    step = pl.program_id(0)
    left = lax.broadcasted_iota(jnp.int32, (rows, 128), 1) < HD
    left_chunk = left[:chunk]
    scale = HD**-0.5
    q = q_ref[...] * jnp.asarray(scale, bf16)
    k = k_ref[...]
    v = v_ref[...]
    g = g_ref[...]
    fq = fq_ref[...]
    fk = fk_ref[...]
    zero = jnp.zeros_like(q)
    k_t = k.T
    product_t = (g.astype(f32) * o_ref[...].astype(f32)).T
    q_side = [jnp.where(left, q, fq), jnp.where(left, fq, q)]
    k_side = [jnp.where(left, k, fk), jnp.where(left, fk, k)]
    v_side = [jnp.where(left, v, zero), jnp.where(left, zero, v)]
    delta = [jnp.sum(product_t[h * HD : (h + 1) * HD], axis=0, keepdims=True) for h in range(2)]
    lse = [lse_ref[0, h : h + 1, :] for h in range(2)]
    dq = [None, None]
    sum_v = jnp.zeros((1, 128), f32)
    for c in range(rows // chunk):
        span = slice(c * chunk, (c + 1) * chunk)
        dk = []
        dv = []
        for h in range(2):
            scores = dot_nt(k_side[h][span], q_side[h])
            p = jnp.exp(scores - lse[h])
            dp = dot_nt(v_side[h][span], g)
            dv.append(dot32(p.astype(bf16), g))
            ds = (p * (dp - delta[h])).astype(bf16)
            dk.append(dot32(ds, q))
            part = dot32(k_t[h * HD : (h + 1) * HD, span], ds)
            dq[h] = part if dq[h] is None else dq[h] + part
        dk_low = jnp.where(left_chunk, dk[0], dk[1]).astype(bf16)
        dv_low = jnp.where(left_chunk, dv[0], dv[1]).astype(bf16)
        dj_ref[span, pl.ds(pl.multiple_of(width + step * 128, 128), 128)] = dk_low
        dj_ref[span, pl.ds(pl.multiple_of(2 * width + step * 128, 128), 128)] = dv_low
        sum_v += jnp.sum(dv_low.astype(f32), axis=0, keepdims=True)
    dq_low = (jnp.concatenate(dq, axis=0) * scale).T.astype(bf16)
    dj_ref[:, pl.ds(pl.multiple_of(step * 128, 128), 128)] = dq_low
    cs_ref[0:1, :] = jnp.sum(dq_low.astype(f32), axis=0, keepdims=True)
    cs_ref[1:2, :] = sum_v


def attend_backward(joined, grad_attended, attended, lse, fq, fk):
    rows = joined.shape[0]
    width = joined.shape[1] // 3
    n = width // 128
    col = lambda off: pl.BlockSpec((rows, 128), lambda i, off=off: (0, off + i))
    full = pl.BlockSpec((rows, 128), lambda i: (0, 0))
    return pl.pallas_call(
        partial(attend_backward_kernel, chunk=rows // 2),
        grid=(n,),
        in_specs=[
            col(0),
            col(n),
            col(2 * n),
            col(0),
            col(0),
            pl.BlockSpec((1, 2, rows), lambda i: (i, 0, 0)),
            full,
            full,
        ],
        out_specs=[
            pl.BlockSpec((rows, 3 * width), lambda i: (0, 0)),
            pl.BlockSpec((2, 128), lambda i: (0, i)),
        ],
        out_shape=[
            jax.ShapeDtypeStruct((rows, 3 * width), bf16),
            jax.ShapeDtypeStruct((2, width), f32),
        ],
        compiler_params=pltpu.CompilerParams(vmem_limit_bytes=VMEM_LIMIT),
        cost_estimate=pl.CostEstimate(
            flops=40 * rows * rows * width, bytes_accessed=16 * rows * width, transcendentals=0
        ),
        name="attend_backward",
    )(joined, joined, joined, grad_attended, attended, lse, fq, fk)


def total(values):
    out = values[0].astype(f32)
    for value in values[1:]:
        out = out + value.astype(f32)
    return out


def pick(values, axis, index):
    return lax.dynamic_index_in_dim(values, index, axis, keepdims=False)


def pack(grads, n, width):
    pieces = []
    for grad in grads:
        rows, columns = grad.shape
        blocks = grad.reshape(n, rows // n, columns)
        pieces += [blocks[:, :, at : at + width] for at in range(0, columns, width)]
    return jnp.concatenate(pieces, axis=1)


def unpack(packed, shapes, n):
    width = packed.shape[1]
    outs = []
    start = 0
    for rows, columns in shapes:
        count = rows // n
        pieces = []
        for unused in range(0, columns, width):
            pieces.append(packed[start : start + count])
            start += count
        outs.append(jnp.concatenate(pieces, axis=1))
    return outs


class PairSum:
    def __init__(self, a, b, me):
        self.me = me
        self.n = a.shape[0]
        self.rows = a.shape[1]
        dims = (4, 2, 2, 2)
        self.terms = [[a.reshape(dims + a.shape[1:])], [b.reshape(dims + b.shape[1:])]]
        self.round = 0
        self.result = None
        self.pending = None

    def bit(self, at):
        return (self.me >> at) & 1

    def steps(self):
        x, y = self.bit(1), self.bit(2)
        core = self.bit(0)
        top = self.me >> 3
        return [((3, core), (3, core)), ((2, x), (1, y)), ((1, y), (1, x)), ((0, top), (0, top))][self.round]

    def part(self, which, other):
        axis, mine = self.steps()[which]
        return total([pick(t, axis, mine ^ other) for t in self.terms[which]]).astype(bf16)

    def sends(self):
        if self.round == 0:
            return [jnp.concatenate([self.part(0, 1), self.part(1, 1)], axis=-2)]
        if self.round < 3:
            return [self.part(0, 1), self.part(1, 1)]
        return [jnp.concatenate([self.part(0, k), self.part(1, k)], axis=-2) for k in (1, 2, 3)]

    def launch(self, sends):
        partners = [[1], [2, 4], [4, 2], [8, 16, 24]][self.round]
        self.pending = [
            lax.ppermute(sent, "dp", [(i, i ^ p) for i in range(self.n)])
            for sent, p in zip(sends, partners)
        ]

    def land(self, came):
        self.pending = None
        steps = self.steps()
        if self.round in (0, 3):
            came = [
                [value[..., : self.rows, :] for value in came],
                [value[..., self.rows :, :] for value in came],
            ]
        else:
            came = [[came[0]], [came[1]]]
        for which in (0, 1):
            axis, mine = steps[which]
            self.terms[which] = [pick(t, axis, mine) for t in self.terms[which]] + came[which]
        self.round += 1
        if self.round == 4:
            self.result = [total(self.terms[0]), total(self.terms[1])]


class Scattered:
    def __init__(self, a, b):
        both = jnp.concatenate([a, b], axis=1)
        out = lax.psum_scatter(both, "dp", scatter_dimension=0, tiled=False).astype(f32)
        self.result = [out[: a.shape[1]], out[a.shape[1] :]]
        self.pending = None


def pair_sum(a, b, me, n):
    if n == 32 and a.shape[1] % 8 == 0 and b.shape[1] % 8 == 0:
        return PairSum(a, b, me)
    return Scattered(a, b)


def fence(main, exchanges):
    flying = [e for e in exchanges if e.pending is not None]
    main, came = lax.optimization_barrier((main, [e.pending for e in flying]))
    for e, values in zip(flying, came):
        e.land(values)
    ready = [e for e in exchanges if e.result is None]
    main, sends = lax.optimization_barrier((main, [e.sends() for e in ready]))
    for e, values in zip(ready, sends):
        e.launch(values)
    return main


def pack_small(vectors, n, width):
    pieces = [vector.reshape(LAYERS, n, -1).transpose(1, 0, 2).reshape(n, -1) for vector in vectors]
    packed = jnp.concatenate(pieces, axis=1).astype(bf16)
    padded = jnp.pad(packed, ((0, 0), (0, -packed.shape[1] % (8 * width))))
    return padded.reshape(n, -1, width), [piece.shape[1] for piece in pieces]


def unpack_small(block, sizes):
    flat = block.reshape(-1)
    outs = []
    start = 0
    for size in sizes:
        outs.append(flat[start : start + size].reshape(LAYERS, -1))
        start += size
    return outs


def row_block(width):
    return pl.BlockSpec((ROWS_STEP, width), lambda i: (i, 0))


def vector(layer, width):
    return pl.BlockSpec((None, 1, width), lambda i: (layer, 0, 0))


def resident(layer, rows, columns):
    return pl.BlockSpec((None, rows, columns), lambda i: (layer, 0, 0), pipeline_mode=pl.Buffered(1))


def kept(rows, columns):
    return pl.BlockSpec((rows, columns), lambda i: (0, 0))


def standardize(values):
    center = values - jnp.mean(values, axis=-1, keepdims=True)
    scale = lax.rsqrt(jnp.mean(center * center, axis=-1, keepdims=True) + EPSILON)
    return center * scale, scale


def columns_sum(values):
    return jnp.sum(values, axis=0, keepdims=True)


def dense_call(kernel, name, rows, in_specs, out_specs, out_shape, flops, moved):
    return pl.pallas_call(
        kernel,
        grid=(rows // ROWS_STEP,),
        in_specs=in_specs,
        out_specs=out_specs,
        out_shape=out_shape,
        compiler_params=pltpu.CompilerParams(vmem_limit_bytes=VMEM_LIMIT),
        cost_estimate=pl.CostEstimate(flops=flops, bytes_accessed=moved, transcendentals=0),
        name=name,
    )


def project_kernel(stream_ref, gain_ref, shift_ref, w_ref, b_ref, normed_ref, joined_ref):
    unit, unused = standardize(stream_ref[...].astype(f32))
    normed = (unit * gain_ref[...].astype(f32) + shift_ref[...].astype(f32)).astype(bf16)
    normed_ref[...] = normed
    joined_ref[...] = (dot32(normed, w_ref[...]) + b_ref[...].astype(f32)).astype(bf16)


def project(layer, stream, gain, shift, qkv_w, bias):
    rows, width = stream.shape
    out = jax.ShapeDtypeStruct
    return dense_call(
        project_kernel,
        "project",
        rows,
        [row_block(width), vector(layer, width), vector(layer, width)]
        + [resident(layer, width, 3 * width), vector(layer, 3 * width)],
        [row_block(width), row_block(3 * width)],
        [out((rows, width), bf16), out((rows, 3 * width), bf16)],
        6 * rows * width * width,
        12 * rows * width + 6 * width * width,
    )(stream, gain, shift, qkv_w, bias)


def mlp_forward_kernel(
    att_ref, stream_ref, out_w_ref, out_b_ref, gain_ref, shift_ref, up_w_ref, up_b_ref,
    down_w_ref, down_b_ref, middle_ref, normed_ref, act_ref, slope_ref, result_ref,
):
    width = att_ref.shape[1]
    middle = (
        stream_ref[...].astype(f32) + dot32(att_ref[...], out_w_ref[...]) + out_b_ref[...].astype(f32)
    )
    middle_ref[...] = middle
    unit, unused = standardize(middle)
    normed = (unit * gain_ref[...].astype(f32) + shift_ref[...].astype(f32)).astype(bf16)
    normed_ref[...] = normed
    result = middle + down_b_ref[...].astype(f32)
    for at in range(0, up_w_ref.shape[1], width):
        span = slice(at, at + width)
        hidden = dot32(normed, up_w_ref[:, span]) + up_b_ref[:, span].astype(f32)
        below = 0.5 + 0.5 * lax.erf(hidden * 0.7071067811865476)
        act = (hidden * below).astype(bf16)
        slope = below + hidden * (0.3989422804014327 * jnp.exp(-0.5 * (hidden * hidden)))
        act_ref[:, span] = act
        slope_ref[:, span] = slope.astype(bf16)
        result = result + dot32(act, down_w_ref[span, :])
    result_ref[...] = result


def mlp_forward(layer, attended, stream, out_w, out_b, gain, shift, up_w, up_b, down_w, down_b):
    rows, width = attended.shape
    up = up_w.shape[2]
    out = jax.ShapeDtypeStruct
    return dense_call(
        mlp_forward_kernel,
        "mlp_forward",
        rows,
        [row_block(width), row_block(width), resident(layer, width, width)]
        + [vector(layer, width)] * 3
        + [resident(layer, width, up), vector(layer, up), resident(layer, up, width), vector(layer, width)],
        [row_block(width), row_block(width), row_block(up), row_block(up), row_block(width)],
        [
            out((rows, width), f32),
            out((rows, width), bf16),
            out((rows, up), bf16),
            out((rows, up), bf16),
            out((rows, width), f32),
        ],
        2 * rows * width * (width + 2 * up),
        4 * rows * (4 * width + up) + 4 * width * (width + up),
    )(attended, stream, out_w, out_b, gain, shift, up_w, up_b, down_w, down_b)


def mlp_backward_kernel(
    grad_ref, slope_ref, middle_ref, gain_ref, up_w_ref, down_w_ref, out_w_ref,
    low_ref, hidden_ref, grad_middle_ref, branch_ref, attended_ref, up_sum_ref, sums_ref,
):
    width = grad_ref.shape[1]

    @pl.when(pl.program_id(0) == 0)
    def _():
        up_sum_ref[...] = jnp.zeros_like(up_sum_ref)
        sums_ref[...] = jnp.zeros_like(sums_ref)

    grad = grad_ref[...]
    low = grad.astype(bf16)
    low_ref[...] = low
    normed = jnp.zeros(grad.shape, f32)
    for at in range(0, up_w_ref.shape[1], width):
        span = slice(at, at + width)
        act = dot_nt(low, down_w_ref[span, :])
        hidden = (slope_ref[:, span].astype(f32) * act).astype(bf16)
        hidden_ref[:, span] = hidden
        up_sum_ref[:, span] += columns_sum(hidden.astype(f32))
        normed = normed + dot_nt(hidden, up_w_ref[:, span])
    unit, scale = standardize(middle_ref[...])
    scaled = normed * gain_ref[...].astype(f32)
    inner = scaled - jnp.mean(scaled, axis=-1, keepdims=True)
    inner = inner - unit * jnp.mean(scaled * unit, axis=-1, keepdims=True)
    middle = grad + inner * scale
    grad_middle_ref[...] = middle
    branch = middle.astype(bf16)
    branch_ref[...] = branch
    attended_ref[...] = dot_nt(branch, out_w_ref[...]).astype(bf16)
    sums_ref[0:1, :] += columns_sum(low.astype(f32))
    sums_ref[1:2, :] += columns_sum(normed * unit)
    sums_ref[2:3, :] += columns_sum(normed)
    sums_ref[3:4, :] += columns_sum(branch.astype(f32))


def mlp_backward(layer, grad, slope, middle, gain, up_w, down_w, out_w):
    rows, width = grad.shape
    up = up_w.shape[2]
    out = jax.ShapeDtypeStruct
    return dense_call(
        mlp_backward_kernel,
        "mlp_backward",
        rows,
        [row_block(width), row_block(up), row_block(width), vector(layer, width)]
        + [resident(layer, width, up), resident(layer, up, width), resident(layer, width, width)],
        [row_block(width), row_block(up)] + [row_block(width)] * 3 + [kept(1, up), kept(8, width)],
        [
            out((rows, width), bf16),
            out((rows, up), bf16),
            out((rows, width), f32),
            out((rows, width), bf16),
            out((rows, width), bf16),
            out((1, up), f32),
            out((8, width), f32),
        ],
        2 * rows * width * (width + 2 * up),
        4 * rows * (5 * width + up) + 4 * width * (width + up),
    )(grad, slope, middle, gain, up_w, down_w, out_w)


def project_backward_kernel(joined_ref, stream_ref, grad_ref, gain_ref, w_ref, result_ref, sums_ref):
    @pl.when(pl.program_id(0) == 0)
    def _():
        sums_ref[...] = jnp.zeros_like(sums_ref)

    normed = dot_nt(joined_ref[...], w_ref[...])
    unit, scale = standardize(stream_ref[...].astype(f32))
    scaled = normed * gain_ref[...].astype(f32)
    inner = scaled - jnp.mean(scaled, axis=-1, keepdims=True)
    inner = inner - unit * jnp.mean(scaled * unit, axis=-1, keepdims=True)
    result_ref[...] = grad_ref[...] + inner * scale
    sums_ref[0:1, :] += columns_sum(normed * unit)
    sums_ref[1:2, :] += columns_sum(normed)


def project_backward(layer, joined, stream, grad, gain, qkv_w):
    rows, width = grad.shape
    out = jax.ShapeDtypeStruct
    return dense_call(
        project_backward_kernel,
        "project_backward",
        rows,
        [row_block(3 * width), row_block(width), row_block(width), vector(layer, width)]
        + [resident(layer, width, 3 * width)],
        [row_block(width), kept(8, width)],
        [out((rows, width), f32), out((8, width), f32)],
        6 * rows * width * width,
        18 * rows * width + 6 * width * width,
    )(joined, stream, grad, gain, qkv_w)


def layer_forward(layer, stream, weights, fq, fk):
    gain_one, shift_one, qkv_w, bias, out_w, out_b, gain_two, shift_two, up_w, up_b, down_w, down_b = weights
    normed, joined = project(layer, stream, gain_one, shift_one, qkv_w, bias)
    attended, lse = attend_forward(joined, fq, fk)
    middle, normed_two, activated, slope, output = mlp_forward(
        layer, attended, stream, out_w, out_b, gain_two, shift_two, up_w, up_b, down_w, down_b
    )
    return output, (stream, normed, joined, attended, lse, middle, normed_two, slope, activated)


def layer_backward(layer, grad_stream, cache, weights, fq, fk, tie):
    stream, normed, joined, attended, lse, middle, normed_two, slope, activated = cache
    gain_one, shift_one, qkv_w, bias, out_w, out_b, gain_two, shift_two, up_w, up_b, down_w, down_b = weights
    low, grad_hidden, grad_middle, branch, grad_attended, grad_up_b, sums = mlp_backward(
        layer, grad_stream, slope, middle, gain_two, up_w, down_w, out_w
    )
    grad_down_w = jnp.einsum("tf,td->fd", activated, low, preferred_element_type=f32).astype(bf16)
    grad_up_w = jnp.einsum("td,tf->df", normed_two, grad_hidden, preferred_element_type=f32).astype(bf16)
    branch = tie("hidden", branch, (grad_down_w, grad_up_w))
    grad_out_w = jnp.einsum("tc,td->cd", attended, branch, preferred_element_type=f32).astype(bf16)
    grad_attended = tie("attended", grad_attended, (grad_out_w,))
    grad_joined, column_sums = attend_backward(joined, grad_attended, attended, lse, fq, fk)
    grad_joined = tie("joined", grad_joined, ())
    grad_qkv_w = jnp.einsum("td,te->de", normed, grad_joined, preferred_element_type=f32).astype(bf16)
    grad_joined = tie("qkv", grad_joined, (grad_qkv_w,))
    grad_input, sums_one = project_backward(layer, grad_joined, stream, grad_middle, gain_one, qkv_w)
    small = (
        sums_one[0],
        sums_one[1],
        column_sums.reshape(-1),
        sums[3],
        sums[1],
        sums[2],
        grad_up_b[0],
        sums[0],
    )
    return grad_input, (grad_qkv_w, grad_out_w, grad_up_w, grad_down_w), small


def local(n, *arguments):
    (
        patches,
        img_length,
        img_start,
        class_count,
        *stacked,
        cls_weight,
        cls_bias,
        logit_grad,
    ) = arguments
    me = lax.axis_index("dp")
    row_count, width = patches.shape
    up_width = stacked[8].shape[2]
    slot_count = img_length.shape[0]
    positions = jnp.arange(row_count, dtype=jnp.int32)
    inside = (positions[None, :] >= img_start[:, None]) & (
        positions[None, :] < (img_start + img_length)[:, None]
    )
    member = inside.astype(f32)
    live_rows = jnp.sum(inside.astype(jnp.int32), axis=0)
    segment = (
        jnp.sum(inside.astype(jnp.int32) * jnp.arange(slot_count, dtype=jnp.int32)[:, None], axis=0)
        + (1 - live_rows) * slot_count
    )
    fq, fk = seg_features(segment, slot_count)
    counts = jnp.maximum(img_length, 1).astype(f32)
    live_columns = jnp.arange(cls_weight.shape[1], dtype=jnp.int32) < class_count[0]
    masked_grad = jnp.where(live_columns[None, :], logit_grad, jnp.zeros_like(logit_grad))
    pooled_grad = lax.psum_scatter(
        dot_nt(masked_grad, cls_weight), "dp", scatter_dimension=0, tiled=True
    )
    weights = [value[:, None, :] if value.ndim == 2 else value for value in stacked]
    qv_bias = weights[3]
    weights[3] = jnp.concatenate(
        [qv_bias[..., :width], jnp.zeros((LAYERS, 1, width), bf16), qv_bias[..., width:]], axis=-1
    )
    stream = patches
    caches = []
    for layer in range(LAYERS):
        stream, cache = layer_forward(layer, stream, weights, fq, fk)
        caches.append(cache)
    sums = jnp.dot(member, stream, precision=HIGHEST, preferred_element_type=f32)
    side = jnp.broadcast_to(counts[:, None], (slot_count, 128))
    gathered = lax.all_gather(jnp.concatenate([sums, side], axis=1), "dp", axis=0, tiled=True)
    grad_stream = jnp.einsum(
        "it,id->td",
        member,
        pooled_grad / counts[:, None],
        precision=HIGHEST,
        preferred_element_type=f32,
    )
    last = {}

    def tie_last(name, value, grads):
        last[name] = grads
        if name != "qkv":
            return value
        both = pack(last["hidden"] + last["attended"] + grads, n, width)
        value, both = lax.optimization_barrier((value, both))
        last["sum"] = lax.psum_scatter(both, "dp", scatter_dimension=0, tiled=False)
        return value

    def tie_first(name, value, grads):
        if name == "hidden":
            first.append(pair_sum(pack(grads[:1], n, width), pack(grads[1:], n, width), me, n))
        if name == "qkv":
            return value
        return fence(value, first)

    first = []
    grad_stream, unused, small_last = layer_backward(1, grad_stream, caches[1], weights, fq, fk, tie_last)
    grad_stream, gathered = lax.optimization_barrier((grad_stream, gathered))
    grad_stream, grads, small_first = layer_backward(0, grad_stream, caches[0], weights, fq, fk, tie_first)
    grad_stream, last["sum"] = lax.optimization_barrier((grad_stream, last["sum"]))
    grad_qkv_w, grad_out_w = grads[:2]
    small, sizes = pack_small([jnp.stack(pair) for pair in zip(small_first, small_last)], n, width)
    qk = 2 * width
    side_a = jnp.concatenate([pack([grad_qkv_w[:, :qk]], n, width), small], axis=1)
    side_b = pack([grad_qkv_w[:, qk:], grad_out_w], n, width)
    first.append(pair_sum(side_a, side_b, me, n))
    while any(e.result is None for e in first):
        grad_stream = fence(grad_stream, first)
    gathered = (gathered[:, :width] / gathered[:, width : width + 1]).astype(bf16)
    scores = dot32(gathered, cls_weight) + cls_bias.astype(f32)
    logits = jnp.where(live_columns[None, :], scores, 0.0)
    grad_cls_weight = jnp.einsum("id,ic->dc", gathered, masked_grad, preferred_element_type=f32)
    grad_cls_bias = jnp.sum(masked_grad.astype(f32), axis=0)
    square = (width, width)
    wide = (width, up_width)
    tall = (up_width, width)
    down_last, up_last, out_last, qkv_last = unpack(
        last["sum"].astype(f32), [tall, wide, square, (width, 3 * width)], n
    )
    (down_first,) = unpack(first[0].result[0], [tall], n)
    (up_first,) = unpack(first[0].result[1], [wide], n)
    (qk_first,) = unpack(first[1].result[0][: 2 * (width // n)], [(width, qk)], n)
    v_first, out_first = unpack(first[1].result[1], [square, square], n)
    qkv_first = jnp.concatenate([qk_first, v_first], axis=1)
    qkv_sum = jnp.stack([qkv_first, qkv_last])
    out_sum = jnp.stack([out_first, out_last])
    up_sum = jnp.stack([up_first, up_last])
    down_sum = jnp.stack([down_first, down_last])
    gain_one, shift_one, qv_b, out_b, gain_two, shift_two, up_b, down_b = unpack_small(
        first[1].result[0][2 * (width // n) :], sizes
    )
    return (
        logits,
        grad_stream,
        gain_one,
        shift_one,
        qkv_sum,
        qv_b,
        out_sum,
        out_b,
        gain_two,
        shift_two,
        up_sum,
        up_b,
        down_sum,
        down_b,
        grad_cls_weight,
        grad_cls_bias,
    )


def solution(mesh):
    whole = P()
    placed = (
        (P("dp", None), P("dp"), P("dp"), P("dp"))
        + (whole,) * 12
        + (P(None, "dp"), P("dp"), P(None, "dp"))
    )
    vector = P(None, "dp")
    matrix = P(None, "dp", None)
    return jax.shard_map(
        partial(local, mesh.size),
        mesh=mesh,
        in_specs=placed,
        out_specs=(
            P(None, "dp"),
            P("dp", None),
            vector,
            vector,
            matrix,
            vector,
            matrix,
            vector,
            vector,
            vector,
            matrix,
            vector,
            matrix,
            vector,
            P(None, "dp"),
            P("dp"),
        ),
        check_vma=False,
    )
```

```python
from functools import partial

import jax
import jax.numpy as jnp
from jax import lax
from jax.experimental import pallas as pl
from jax.experimental.pallas import tpu as pltpu
from jax.sharding import PartitionSpec as P

HD = 64
LAYERS = 2
BIG = 1e30
EPSILON = 1e-06
HIGHEST = lax.Precision.HIGHEST
NT = (((1,), (1,)), ((), ()))
f32 = jnp.float32
bf16 = jnp.bfloat16
VMEM_LIMIT = 56 << 20
ROWS_STEP = 256


def dot32(left, right):
    return jnp.dot(left, right, preferred_element_type=f32)


def dot_nt(left, right):
    return lax.dot_general(left, right, NT, preferred_element_type=f32)


def seg_features(segment, slot_count):
    lane = jnp.arange(128, dtype=jnp.int32) % HD
    hit = segment[:, None] == lane[None, :]
    live = (lane <= slot_count)[None, :]
    query_side = (hit & live).astype(bf16)
    key_side = jnp.where(live & ~hit, -BIG, 0.0).astype(bf16)
    return query_side, key_side


def attend_forward_kernel(q_ref, k_ref, v_ref, fq_ref, fk_ref, o_ref, lse_ref, *, chunk):
    rows = q_ref.shape[0]
    left = lax.broadcasted_iota(jnp.int32, (rows, 128), 1) < HD
    q = q_ref[...] * jnp.asarray(HD**-0.5, bf16)
    k = k_ref[...]
    fq = fq_ref[...]
    fk = fk_ref[...]
    v_t = v_ref[...].T
    q_side = [jnp.where(left, q, fq), jnp.where(left, fq, q)]
    k_side = [jnp.where(left, k, fk), jnp.where(left, fk, k)]
    for c in range(rows // chunk):
        span = slice(c * chunk, (c + 1) * chunk)
        outs = []
        for h in range(2):
            scores = dot_nt(k_side[h], q_side[h][span])
            largest = jnp.max(scores, axis=0, keepdims=True)
            p = jnp.exp(scores - largest)
            total = jnp.sum(p, axis=0, keepdims=True)
            mixed = dot32(v_t[h * HD : (h + 1) * HD], p.astype(bf16))
            outs.append(mixed / total)
            lse_ref[0, h : h + 1, span] = largest + jnp.log(total)
        o_ref[span, :] = jnp.concatenate(outs, axis=0).T.astype(bf16)


def attend_forward(joined, fq, fk):
    rows = joined.shape[0]
    width = joined.shape[1] // 3
    n = width // 128
    col = lambda off: pl.BlockSpec((rows, 128), lambda i, off=off: (0, off + i))
    full = pl.BlockSpec((rows, 128), lambda i: (0, 0))
    return pl.pallas_call(
        partial(attend_forward_kernel, chunk=rows),
        grid=(n,),
        in_specs=[col(0), col(n), col(2 * n), full, full],
        out_specs=[
            pl.BlockSpec((rows, 128), lambda i: (0, i)),
            pl.BlockSpec((1, 2, rows), lambda i: (i, 0, 0)),
        ],
        out_shape=[
            jax.ShapeDtypeStruct((rows, width), bf16),
            jax.ShapeDtypeStruct((n, 2, rows), f32),
        ],
        compiler_params=pltpu.CompilerParams(vmem_limit_bytes=VMEM_LIMIT),
        cost_estimate=pl.CostEstimate(flops=1, bytes_accessed=1, transcendentals=0),
        name="attend_forward",
    )(joined, joined, joined, fq, fk)


def attend_backward_kernel(
    q_ref, k_ref, v_ref, g_ref, o_ref, lse_ref, fq_ref, fk_ref, dj_ref, cs_ref, *, chunk
):
    rows = q_ref.shape[0]
    width = dj_ref.shape[1] // 3
    step = pl.program_id(0)
    left = lax.broadcasted_iota(jnp.int32, (rows, 128), 1) < HD
    left_chunk = left[:chunk]
    scale = HD**-0.5
    q = q_ref[...] * jnp.asarray(scale, bf16)
    k = k_ref[...]
    v = v_ref[...]
    g = g_ref[...]
    fq = fq_ref[...]
    fk = fk_ref[...]
    zero = jnp.zeros_like(q)
    k_t = k.T
    product_t = (g.astype(f32) * o_ref[...].astype(f32)).T
    q_side = [jnp.where(left, q, fq), jnp.where(left, fq, q)]
    k_side = [jnp.where(left, k, fk), jnp.where(left, fk, k)]
    v_side = [jnp.where(left, v, zero), jnp.where(left, zero, v)]
    delta = [jnp.sum(product_t[h * HD : (h + 1) * HD], axis=0, keepdims=True) for h in range(2)]
    lse = [lse_ref[0, h : h + 1, :] for h in range(2)]
    dq = [None, None]
    sum_v = jnp.zeros((1, 128), f32)
    for c in range(rows // chunk):
        span = slice(c * chunk, (c + 1) * chunk)
        dk = []
        dv = []
        for h in range(2):
            scores = dot_nt(k_side[h][span], q_side[h])
            p = jnp.exp(scores - lse[h])
            dp = dot_nt(v_side[h][span], g)
            dv.append(dot32(p.astype(bf16), g))
            ds = (p * (dp - delta[h])).astype(bf16)
            dk.append(dot32(ds, q))
            part = dot32(k_t[h * HD : (h + 1) * HD, span], ds)
            dq[h] = part if dq[h] is None else dq[h] + part
        dk_low = jnp.where(left_chunk, dk[0], dk[1]).astype(bf16)
        dv_low = jnp.where(left_chunk, dv[0], dv[1]).astype(bf16)
        dj_ref[span, pl.ds(pl.multiple_of(width + step * 128, 128), 128)] = dk_low
        dj_ref[span, pl.ds(pl.multiple_of(2 * width + step * 128, 128), 128)] = dv_low
        sum_v += jnp.sum(dv_low.astype(f32), axis=0, keepdims=True)
    dq_low = (jnp.concatenate(dq, axis=0) * scale).T.astype(bf16)
    dj_ref[:, pl.ds(pl.multiple_of(step * 128, 128), 128)] = dq_low
    cs_ref[0:1, :] = jnp.sum(dq_low.astype(f32), axis=0, keepdims=True)
    cs_ref[1:2, :] = sum_v


def attend_backward(joined, grad_attended, attended, lse, fq, fk):
    rows = joined.shape[0]
    width = joined.shape[1] // 3
    n = width // 128
    col = lambda off: pl.BlockSpec((rows, 128), lambda i, off=off: (0, off + i))
    full = pl.BlockSpec((rows, 128), lambda i: (0, 0))
    return pl.pallas_call(
        partial(attend_backward_kernel, chunk=rows // 2),
        grid=(n,),
        in_specs=[
            col(0),
            col(n),
            col(2 * n),
            col(0),
            col(0),
            pl.BlockSpec((1, 2, rows), lambda i: (i, 0, 0)),
            full,
            full,
        ],
        out_specs=[
            pl.BlockSpec((rows, 3 * width), lambda i: (0, 0)),
            pl.BlockSpec((2, 128), lambda i: (0, i)),
        ],
        out_shape=[
            jax.ShapeDtypeStruct((rows, 3 * width), bf16),
            jax.ShapeDtypeStruct((2, width), f32),
        ],
        compiler_params=pltpu.CompilerParams(vmem_limit_bytes=VMEM_LIMIT),
        cost_estimate=pl.CostEstimate(flops=1, bytes_accessed=1, transcendentals=0),
        name="attend_backward",
    )(joined, joined, joined, grad_attended, attended, lse, fq, fk)


def total(values):
    out = values[0].astype(f32)
    for value in values[1:]:
        out = out + value.astype(f32)
    return out


def pick(values, axis, index):
    return lax.dynamic_index_in_dim(values, index, axis, keepdims=False)


def pack(grads, n, width):
    pieces = []
    for grad in grads:
        rows, columns = grad.shape
        blocks = grad.reshape(n, rows // n, columns)
        pieces += [blocks[:, :, at : at + width] for at in range(0, columns, width)]
    return jnp.concatenate(pieces, axis=1)


def unpack(packed, shapes, n):
    width = packed.shape[1]
    outs = []
    start = 0
    for rows, columns in shapes:
        count = rows // n
        pieces = []
        for unused in range(0, columns, width):
            pieces.append(packed[start : start + count])
            start += count
        outs.append(jnp.concatenate(pieces, axis=1))
    return outs


class PairSum:
    def __init__(self, a, b, me):
        self.me = me
        self.n = a.shape[0]
        self.rows = a.shape[1]
        dims = (4, 2, 2, 2)
        self.terms = [[a.reshape(dims + a.shape[1:])], [b.reshape(dims + b.shape[1:])]]
        self.round = 0
        self.result = None
        self.pending = None

    def bit(self, at):
        return (self.me >> at) & 1

    def steps(self):
        x, y = self.bit(1), self.bit(2)
        core = self.bit(0)
        top = self.me >> 3
        return [((3, core), (3, core)), ((2, x), (1, y)), ((1, y), (1, x)), ((0, top), (0, top))][self.round]

    def part(self, which, other):
        axis, mine = self.steps()[which]
        return total([pick(t, axis, mine ^ other) for t in self.terms[which]]).astype(bf16)

    def sends(self):
        if self.round == 0:
            return [jnp.concatenate([self.part(0, 1), self.part(1, 1)], axis=-2)]
        if self.round < 3:
            return [self.part(0, 1), self.part(1, 1)]
        return [jnp.concatenate([self.part(0, k), self.part(1, k)], axis=-2) for k in (1, 2, 3)]

    def launch(self, sends):
        partners = [[1], [2, 4], [4, 2], [8, 16, 24]][self.round]
        self.pending = [
            lax.ppermute(sent, "dp", [(i, i ^ p) for i in range(self.n)])
            for sent, p in zip(sends, partners)
        ]

    def land(self, came):
        self.pending = None
        steps = self.steps()
        if self.round in (0, 3):
            came = [
                [value[..., : self.rows, :] for value in came],
                [value[..., self.rows :, :] for value in came],
            ]
        else:
            came = [[came[0]], [came[1]]]
        for which in (0, 1):
            axis, mine = steps[which]
            self.terms[which] = [pick(t, axis, mine) for t in self.terms[which]] + came[which]
        self.round += 1
        if self.round == 4:
            self.result = [total(self.terms[0]), total(self.terms[1])]


class Scattered:
    def __init__(self, a, b):
        both = jnp.concatenate([a, b], axis=1)
        out = lax.psum_scatter(both, "dp", scatter_dimension=0, tiled=False).astype(f32)
        self.result = [out[: a.shape[1]], out[a.shape[1] :]]
        self.pending = None


def pair_sum(a, b, me, n):
    if n == 32 and a.shape[1] % 8 == 0 and b.shape[1] % 8 == 0:
        return PairSum(a, b, me)
    return Scattered(a, b)


def fence(main, exchanges):
    flying = [e for e in exchanges if e.pending is not None]
    main, came = lax.optimization_barrier((main, [e.pending for e in flying]))
    for e, values in zip(flying, came):
        e.land(values)
    ready = [e for e in exchanges if e.result is None]
    main, sends = lax.optimization_barrier((main, [e.sends() for e in ready]))
    for e, values in zip(ready, sends):
        e.launch(values)
    return main


def pack_small(vectors, n, width):
    pieces = [vector.reshape(LAYERS, n, -1).transpose(1, 0, 2).reshape(n, -1) for vector in vectors]
    packed = jnp.concatenate(pieces, axis=1).astype(bf16)
    padded = jnp.pad(packed, ((0, 0), (0, -packed.shape[1] % (8 * width))))
    return padded.reshape(n, -1, width), [piece.shape[1] for piece in pieces]


def unpack_small(block, sizes):
    flat = block.reshape(-1)
    outs = []
    start = 0
    for size in sizes:
        outs.append(flat[start : start + size].reshape(LAYERS, -1))
        start += size
    return outs


def row_block(width):
    return pl.BlockSpec((ROWS_STEP, width), lambda i: (i, 0))


def vector(layer, width):
    return pl.BlockSpec((None, 1, width), lambda i: (layer, 0, 0))


def resident(layer, rows, columns):
    return pl.BlockSpec((None, rows, columns), lambda i: (layer, 0, 0), pipeline_mode=pl.Buffered(1))


def kept(rows, columns):
    return pl.BlockSpec((rows, columns), lambda i: (0, 0))


def standardize(values):
    center = values - jnp.mean(values, axis=-1, keepdims=True)
    scale = lax.rsqrt(jnp.mean(center * center, axis=-1, keepdims=True) + EPSILON)
    return center * scale, scale


def columns_sum(values):
    return jnp.sum(values, axis=0, keepdims=True)


def dense_call(kernel, name, rows, in_specs, out_specs, out_shape, flops, moved):
    return pl.pallas_call(
        kernel,
        grid=(rows // ROWS_STEP,),
        in_specs=in_specs,
        out_specs=out_specs,
        out_shape=out_shape,
        compiler_params=pltpu.CompilerParams(vmem_limit_bytes=VMEM_LIMIT),
        cost_estimate=pl.CostEstimate(flops=1, bytes_accessed=1, transcendentals=0),
        name=name,
    )


def project_kernel(stream_ref, gain_ref, shift_ref, w_ref, b_ref, normed_ref, joined_ref):
    unit, unused = standardize(stream_ref[...].astype(f32))
    normed = (unit * gain_ref[...].astype(f32) + shift_ref[...].astype(f32)).astype(bf16)
    normed_ref[...] = normed
    joined_ref[...] = (dot32(normed, w_ref[...]) + b_ref[...].astype(f32)).astype(bf16)


def project(layer, stream, gain, shift, qkv_w, bias):
    rows, width = stream.shape
    out = jax.ShapeDtypeStruct
    return dense_call(
        project_kernel,
        "project",
        rows,
        [row_block(width), vector(layer, width), vector(layer, width)]
        + [resident(layer, width, 3 * width), vector(layer, 3 * width)],
        [row_block(width), row_block(3 * width)],
        [out((rows, width), bf16), out((rows, 3 * width), bf16)],
        6 * rows * width * width,
        12 * rows * width + 6 * width * width,
    )(stream, gain, shift, qkv_w, bias)


def mlp_forward_kernel(
    att_ref, stream_ref, out_w_ref, out_b_ref, gain_ref, shift_ref, up_w_ref, up_b_ref,
    down_w_ref, down_b_ref, middle_ref, normed_ref, act_ref, slope_ref, result_ref,
):
    width = att_ref.shape[1]
    middle = (
        stream_ref[...].astype(f32) + dot32(att_ref[...], out_w_ref[...]) + out_b_ref[...].astype(f32)
    )
    middle_ref[...] = middle
    unit, unused = standardize(middle)
    normed = (unit * gain_ref[...].astype(f32) + shift_ref[...].astype(f32)).astype(bf16)
    normed_ref[...] = normed
    result = middle + down_b_ref[...].astype(f32)
    for at in range(0, up_w_ref.shape[1], width):
        span = slice(at, at + width)
        hidden = dot32(normed, up_w_ref[:, span]) + up_b_ref[:, span].astype(f32)
        below = 0.5 + 0.5 * lax.erf(hidden * 0.7071067811865476)
        act = (hidden * below).astype(bf16)
        slope = below + hidden * (0.3989422804014327 * jnp.exp(-0.5 * (hidden * hidden)))
        act_ref[:, span] = act
        slope_ref[:, span] = slope.astype(bf16)
        result = result + dot32(act, down_w_ref[span, :])
    result_ref[...] = result


def mlp_forward(layer, attended, stream, out_w, out_b, gain, shift, up_w, up_b, down_w, down_b):
    rows, width = attended.shape
    up = up_w.shape[2]
    out = jax.ShapeDtypeStruct
    return dense_call(
        mlp_forward_kernel,
        "mlp_forward",
        rows,
        [row_block(width), row_block(width), resident(layer, width, width)]
        + [vector(layer, width)] * 3
        + [resident(layer, width, up), vector(layer, up), resident(layer, up, width), vector(layer, width)],
        [row_block(width), row_block(width), row_block(up), row_block(up), row_block(width)],
        [
            out((rows, width), f32),
            out((rows, width), bf16),
            out((rows, up), bf16),
            out((rows, up), bf16),
            out((rows, width), f32),
        ],
        2 * rows * width * (width + 2 * up),
        4 * rows * (4 * width + up) + 4 * width * (width + up),
    )(attended, stream, out_w, out_b, gain, shift, up_w, up_b, down_w, down_b)


def mlp_backward_kernel(
    grad_ref, slope_ref, middle_ref, gain_ref, up_w_ref, down_w_ref, out_w_ref,
    low_ref, hidden_ref, grad_middle_ref, branch_ref, attended_ref, up_sum_ref, sums_ref,
):
    width = grad_ref.shape[1]

    @pl.when(pl.program_id(0) == 0)
    def _():
        up_sum_ref[...] = jnp.zeros_like(up_sum_ref)
        sums_ref[...] = jnp.zeros_like(sums_ref)

    grad = grad_ref[...]
    low = grad.astype(bf16)
    low_ref[...] = low
    normed = jnp.zeros(grad.shape, f32)
    for at in range(0, up_w_ref.shape[1], width):
        span = slice(at, at + width)
        act = dot_nt(low, down_w_ref[span, :])
        hidden = (slope_ref[:, span].astype(f32) * act).astype(bf16)
        hidden_ref[:, span] = hidden
        up_sum_ref[:, span] += columns_sum(hidden.astype(f32))
        normed = normed + dot_nt(hidden, up_w_ref[:, span])
    unit, scale = standardize(middle_ref[...])
    scaled = normed * gain_ref[...].astype(f32)
    inner = scaled - jnp.mean(scaled, axis=-1, keepdims=True)
    inner = inner - unit * jnp.mean(scaled * unit, axis=-1, keepdims=True)
    middle = grad + inner * scale
    grad_middle_ref[...] = middle
    branch = middle.astype(bf16)
    branch_ref[...] = branch
    attended_ref[...] = dot_nt(branch, out_w_ref[...]).astype(bf16)
    sums_ref[0:1, :] += columns_sum(low.astype(f32))
    sums_ref[1:2, :] += columns_sum(normed * unit)
    sums_ref[2:3, :] += columns_sum(normed)
    sums_ref[3:4, :] += columns_sum(branch.astype(f32))


def mlp_backward(layer, grad, slope, middle, gain, up_w, down_w, out_w):
    rows, width = grad.shape
    up = up_w.shape[2]
    out = jax.ShapeDtypeStruct
    return dense_call(
        mlp_backward_kernel,
        "mlp_backward",
        rows,
        [row_block(width), row_block(up), row_block(width), vector(layer, width)]
        + [resident(layer, width, up), resident(layer, up, width), resident(layer, width, width)],
        [row_block(width), row_block(up)] + [row_block(width)] * 3 + [kept(1, up), kept(8, width)],
        [
            out((rows, width), bf16),
            out((rows, up), bf16),
            out((rows, width), f32),
            out((rows, width), bf16),
            out((rows, width), bf16),
            out((1, up), f32),
            out((8, width), f32),
        ],
        2 * rows * width * (width + 2 * up),
        4 * rows * (5 * width + up) + 4 * width * (width + up),
    )(grad, slope, middle, gain, up_w, down_w, out_w)


def project_backward_kernel(joined_ref, stream_ref, grad_ref, gain_ref, w_ref, result_ref, sums_ref):
    @pl.when(pl.program_id(0) == 0)
    def _():
        sums_ref[...] = jnp.zeros_like(sums_ref)

    normed = dot_nt(joined_ref[...], w_ref[...])
    unit, scale = standardize(stream_ref[...].astype(f32))
    scaled = normed * gain_ref[...].astype(f32)
    inner = scaled - jnp.mean(scaled, axis=-1, keepdims=True)
    inner = inner - unit * jnp.mean(scaled * unit, axis=-1, keepdims=True)
    result_ref[...] = grad_ref[...] + inner * scale
    sums_ref[0:1, :] += columns_sum(normed * unit)
    sums_ref[1:2, :] += columns_sum(normed)


def project_backward(layer, joined, stream, grad, gain, qkv_w):
    rows, width = grad.shape
    out = jax.ShapeDtypeStruct
    return dense_call(
        project_backward_kernel,
        "project_backward",
        rows,
        [row_block(3 * width), row_block(width), row_block(width), vector(layer, width)]
        + [resident(layer, width, 3 * width)],
        [row_block(width), kept(8, width)],
        [out((rows, width), f32), out((8, width), f32)],
        6 * rows * width * width,
        18 * rows * width + 6 * width * width,
    )(joined, stream, grad, gain, qkv_w)


def layer_forward(layer, stream, weights, fq, fk):
    gain_one, shift_one, qkv_w, bias, out_w, out_b, gain_two, shift_two, up_w, up_b, down_w, down_b = weights
    normed, joined = project(layer, stream, gain_one, shift_one, qkv_w, bias)
    attended, lse = attend_forward(joined, fq, fk)
    middle, normed_two, activated, slope, output = mlp_forward(
        layer, attended, stream, out_w, out_b, gain_two, shift_two, up_w, up_b, down_w, down_b
    )
    return output, (stream, normed, joined, attended, lse, middle, normed_two, slope, activated)


def layer_backward(layer, grad_stream, cache, weights, fq, fk, tie):
    stream, normed, joined, attended, lse, middle, normed_two, slope, activated = cache
    gain_one, shift_one, qkv_w, bias, out_w, out_b, gain_two, shift_two, up_w, up_b, down_w, down_b = weights
    low, grad_hidden, grad_middle, branch, grad_attended, grad_up_b, sums = mlp_backward(
        layer, grad_stream, slope, middle, gain_two, up_w, down_w, out_w
    )
    grad_down_w = jnp.einsum("tf,td->fd", activated, low, preferred_element_type=f32).astype(bf16)
    grad_up_w = jnp.einsum("td,tf->df", normed_two, grad_hidden, preferred_element_type=f32).astype(bf16)
    branch = tie("hidden", branch, (grad_down_w, grad_up_w))
    grad_out_w = jnp.einsum("tc,td->cd", attended, branch, preferred_element_type=f32).astype(bf16)
    grad_attended = tie("attended", grad_attended, (grad_out_w,))
    grad_joined, column_sums = attend_backward(joined, grad_attended, attended, lse, fq, fk)
    grad_joined = tie("joined", grad_joined, ())
    grad_qkv_w = jnp.einsum("td,te->de", normed, grad_joined, preferred_element_type=f32).astype(bf16)
    grad_joined = tie("qkv", grad_joined, (grad_qkv_w,))
    grad_input, sums_one = project_backward(layer, grad_joined, stream, grad_middle, gain_one, qkv_w)
    small = (
        sums_one[0],
        sums_one[1],
        column_sums.reshape(-1),
        sums[3],
        sums[1],
        sums[2],
        grad_up_b[0],
        sums[0],
    )
    return grad_input, (grad_qkv_w, grad_out_w, grad_up_w, grad_down_w), small


def local(n, *arguments):
    (
        patches,
        img_length,
        img_start,
        class_count,
        *stacked,
        cls_weight,
        cls_bias,
        logit_grad,
    ) = arguments
    me = lax.axis_index("dp")
    row_count, width = patches.shape
    up_width = stacked[8].shape[2]
    slot_count = img_length.shape[0]
    positions = jnp.arange(row_count, dtype=jnp.int32)
    inside = (positions[None, :] >= img_start[:, None]) & (
        positions[None, :] < (img_start + img_length)[:, None]
    )
    member = inside.astype(f32)
    live_rows = jnp.sum(inside.astype(jnp.int32), axis=0)
    segment = (
        jnp.sum(inside.astype(jnp.int32) * jnp.arange(slot_count, dtype=jnp.int32)[:, None], axis=0)
        + (1 - live_rows) * slot_count
    )
    fq, fk = seg_features(segment, slot_count)
    counts = jnp.maximum(img_length, 1).astype(f32)
    live_columns = jnp.arange(cls_weight.shape[1], dtype=jnp.int32) < class_count[0]
    masked_grad = jnp.where(live_columns[None, :], logit_grad, jnp.zeros_like(logit_grad))
    pooled_grad = lax.psum_scatter(
        dot_nt(masked_grad, cls_weight), "dp", scatter_dimension=0, tiled=True
    )
    weights = [value[:, None, :] if value.ndim == 2 else value for value in stacked]
    qv_bias = weights[3]
    weights[3] = jnp.concatenate(
        [qv_bias[..., :width], jnp.zeros((LAYERS, 1, width), bf16), qv_bias[..., width:]], axis=-1
    )
    stream = patches
    caches = []
    for layer in range(LAYERS):
        stream, cache = layer_forward(layer, stream, weights, fq, fk)
        caches.append(cache)
    sums = jnp.dot(member, stream, precision=HIGHEST, preferred_element_type=f32)
    side = jnp.broadcast_to(counts[:, None], (slot_count, 128))
    gathered = lax.all_gather(jnp.concatenate([sums, side], axis=1), "dp", axis=0, tiled=True)
    grad_stream = jnp.einsum(
        "it,id->td",
        member,
        pooled_grad / counts[:, None],
        precision=HIGHEST,
        preferred_element_type=f32,
    )
    last = {}

    def tie_last(name, value, grads):
        last[name] = grads
        if name != "qkv":
            return value
        both = pack(last["hidden"] + last["attended"] + grads, n, width)
        value, both = lax.optimization_barrier((value, both))
        last["sum"] = lax.psum_scatter(both, "dp", scatter_dimension=0, tiled=False)
        return value

    def tie_first(name, value, grads):
        if name == "hidden":
            first.append(pair_sum(pack(grads[:1], n, width), pack(grads[1:], n, width), me, n))
        return fence(value, first)

    first = []
    grad_stream, unused, small_last = layer_backward(1, grad_stream, caches[1], weights, fq, fk, tie_last)
    grad_stream, gathered = lax.optimization_barrier((grad_stream, gathered))
    grad_stream, grads, small_first = layer_backward(0, grad_stream, caches[0], weights, fq, fk, tie_first)
    grad_qkv_w, grad_out_w = grads[:2]
    small, sizes = pack_small([jnp.stack(pair) for pair in zip(small_first, small_last)], n, width)
    qk = 2 * width
    side_a = jnp.concatenate([pack([grad_qkv_w[:, :qk]], n, width), small], axis=1)
    side_b = pack([grad_qkv_w[:, qk:], grad_out_w], n, width)
    first.append(pair_sum(side_a, side_b, me, n))
    for unused in range(2):
        grad_stream = fence(grad_stream, first[1:])
    grad_stream, last["sum"] = lax.optimization_barrier((grad_stream, last["sum"]))
    grad_stream = fence(grad_stream, first[1:])
    while any(e.result is None for e in first):
        grad_stream = fence(grad_stream, first)
    gathered = (gathered[:, :width] / gathered[:, width : width + 1]).astype(bf16)
    scores = dot32(gathered, cls_weight) + cls_bias.astype(f32)
    logits = jnp.where(live_columns[None, :], scores, 0.0)
    grad_cls_weight = jnp.einsum("id,ic->dc", gathered, masked_grad, preferred_element_type=f32)
    grad_cls_bias = jnp.sum(masked_grad.astype(f32), axis=0)
    square = (width, width)
    wide = (width, up_width)
    tall = (up_width, width)
    down_last, up_last, out_last, qkv_last = unpack(
        last["sum"].astype(f32), [tall, wide, square, (width, 3 * width)], n
    )
    (down_first,) = unpack(first[0].result[0], [tall], n)
    (up_first,) = unpack(first[0].result[1], [wide], n)
    (qk_first,) = unpack(first[1].result[0][: 2 * (width // n)], [(width, qk)], n)
    v_first, out_first = unpack(first[1].result[1], [square, square], n)
    qkv_first = jnp.concatenate([qk_first, v_first], axis=1)
    qkv_sum = jnp.stack([qkv_first, qkv_last])
    out_sum = jnp.stack([out_first, out_last])
    up_sum = jnp.stack([up_first, up_last])
    down_sum = jnp.stack([down_first, down_last])
    gain_one, shift_one, qv_b, out_b, gain_two, shift_two, up_b, down_b = unpack_small(
        first[1].result[0][2 * (width // n) :], sizes
    )
    return (
        logits,
        grad_stream,
        gain_one,
        shift_one,
        qkv_sum,
        qv_b,
        out_sum,
        out_b,
        gain_two,
        shift_two,
        up_sum,
        up_b,
        down_sum,
        down_b,
        grad_cls_weight,
        grad_cls_bias,
    )


def solution(mesh):
    whole = P()
    placed = (
        (P("dp", None), P("dp"), P("dp"), P("dp"))
        + (whole,) * 12
        + (P(None, "dp"), P("dp"), P(None, "dp"))
    )
    vector = P(None, "dp")
    matrix = P(None, "dp", None)
    return jax.shard_map(
        partial(local, mesh.size),
        mesh=mesh,
        in_specs=placed,
        out_specs=(
            P(None, "dp"),
            P("dp", None),
            vector,
            vector,
            matrix,
            vector,
            matrix,
            vector,
            vector,
            vector,
            matrix,
            vector,
            matrix,
            vector,
            P(None, "dp"),
            P("dp"),
        ),
        check_vma=False,
    )
```

```python
from functools import partial

import jax
import jax.numpy as jnp
from jax import lax
from jax.experimental import pallas as pl
from jax.experimental.pallas import tpu as pltpu
from jax.sharding import PartitionSpec as P

HD = 64
LAYERS = 2
BIG = 1e30
EPSILON = 1e-06
HIGHEST = lax.Precision.HIGHEST
NT = (((1,), (1,)), ((), ()))
f32 = jnp.float32
bf16 = jnp.bfloat16
VMEM_LIMIT = 56 << 20
ROWS_STEP = 256


def dot32(left, right):
    return jnp.dot(left, right, preferred_element_type=f32)


def dot_nt(left, right):
    return lax.dot_general(left, right, NT, preferred_element_type=f32)


def seg_features(segment, slot_count):
    lane = jnp.arange(128, dtype=jnp.int32) % HD
    hit = segment[:, None] == lane[None, :]
    live = (lane <= slot_count)[None, :]
    query_side = (hit & live).astype(bf16)
    key_side = jnp.where(live & ~hit, -BIG, 0.0).astype(bf16)
    return query_side, key_side


def attend_forward_kernel(q_ref, k_ref, v_ref, fq_ref, fk_ref, o_ref, lse_ref, *, chunk):
    rows = q_ref.shape[0]
    left = lax.broadcasted_iota(jnp.int32, (rows, 128), 1) < HD
    q = q_ref[...] * jnp.asarray(HD**-0.5, bf16)
    k = k_ref[...]
    fq = fq_ref[...]
    fk = fk_ref[...]
    v_t = v_ref[...].T
    q_side = [jnp.where(left, q, fq), jnp.where(left, fq, q)]
    k_side = [jnp.where(left, k, fk), jnp.where(left, fk, k)]
    for c in range(rows // chunk):
        span = slice(c * chunk, (c + 1) * chunk)
        outs = []
        for h in range(2):
            scores = dot_nt(k_side[h], q_side[h][span])
            largest = jnp.max(scores, axis=0, keepdims=True)
            p = jnp.exp(scores - largest)
            total = jnp.sum(p, axis=0, keepdims=True)
            mixed = dot32(v_t[h * HD : (h + 1) * HD], p.astype(bf16))
            outs.append(mixed / total)
            lse_ref[0, h : h + 1, span] = largest + jnp.log(total)
        o_ref[span, :] = jnp.concatenate(outs, axis=0).T.astype(bf16)


def attend_forward(joined, fq, fk):
    rows = joined.shape[0]
    width = joined.shape[1] // 3
    n = width // 128
    col = lambda off: pl.BlockSpec((rows, 128), lambda i, off=off: (0, off + i))
    full = pl.BlockSpec((rows, 128), lambda i: (0, 0))
    return pl.pallas_call(
        partial(attend_forward_kernel, chunk=rows),
        grid=(n,),
        in_specs=[col(0), col(n), col(2 * n), full, full],
        out_specs=[
            pl.BlockSpec((rows, 128), lambda i: (0, i)),
            pl.BlockSpec((1, 2, rows), lambda i: (i, 0, 0)),
        ],
        out_shape=[
            jax.ShapeDtypeStruct((rows, width), bf16),
            jax.ShapeDtypeStruct((n, 2, rows), f32),
        ],
        compiler_params=pltpu.CompilerParams(vmem_limit_bytes=VMEM_LIMIT),
        cost_estimate=pl.CostEstimate(flops=1, bytes_accessed=1, transcendentals=0),
        name="attend_forward",
    )(joined, joined, joined, fq, fk)


def attend_backward_kernel(
    q_ref, k_ref, v_ref, g_ref, o_ref, lse_ref, fq_ref, fk_ref, dj_ref, cs_ref, *, chunk
):
    rows = q_ref.shape[0]
    width = dj_ref.shape[1] // 3
    step = pl.program_id(0)
    left = lax.broadcasted_iota(jnp.int32, (rows, 128), 1) < HD
    left_chunk = left[:chunk]
    scale = HD**-0.5
    q = q_ref[...] * jnp.asarray(scale, bf16)
    k = k_ref[...]
    v = v_ref[...]
    g = g_ref[...]
    fq = fq_ref[...]
    fk = fk_ref[...]
    zero = jnp.zeros_like(q)
    k_t = k.T
    product_t = (g.astype(f32) * o_ref[...].astype(f32)).T
    q_side = [jnp.where(left, q, fq), jnp.where(left, fq, q)]
    k_side = [jnp.where(left, k, fk), jnp.where(left, fk, k)]
    v_side = [jnp.where(left, v, zero), jnp.where(left, zero, v)]
    delta = [jnp.sum(product_t[h * HD : (h + 1) * HD], axis=0, keepdims=True) for h in range(2)]
    lse = [lse_ref[0, h : h + 1, :] for h in range(2)]
    dq = [None, None]
    sum_v = jnp.zeros((1, 128), f32)
    for c in range(rows // chunk):
        span = slice(c * chunk, (c + 1) * chunk)
        dk = []
        dv = []
        for h in range(2):
            scores = dot_nt(k_side[h][span], q_side[h])
            p = jnp.exp(scores - lse[h])
            dp = dot_nt(v_side[h][span], g)
            dv.append(dot32(p.astype(bf16), g))
            ds = (p * (dp - delta[h])).astype(bf16)
            dk.append(dot32(ds, q))
            part = dot32(k_t[h * HD : (h + 1) * HD, span], ds)
            dq[h] = part if dq[h] is None else dq[h] + part
        dk_low = jnp.where(left_chunk, dk[0], dk[1]).astype(bf16)
        dv_low = jnp.where(left_chunk, dv[0], dv[1]).astype(bf16)
        dj_ref[span, pl.ds(pl.multiple_of(width + step * 128, 128), 128)] = dk_low
        dj_ref[span, pl.ds(pl.multiple_of(2 * width + step * 128, 128), 128)] = dv_low
        sum_v += jnp.sum(dv_low.astype(f32), axis=0, keepdims=True)
    dq_low = (jnp.concatenate(dq, axis=0) * scale).T.astype(bf16)
    dj_ref[:, pl.ds(pl.multiple_of(step * 128, 128), 128)] = dq_low
    cs_ref[0:1, :] = jnp.sum(dq_low.astype(f32), axis=0, keepdims=True)
    cs_ref[1:2, :] = sum_v


def attend_backward(joined, grad_attended, attended, lse, fq, fk):
    rows = joined.shape[0]
    width = joined.shape[1] // 3
    n = width // 128
    col = lambda off: pl.BlockSpec((rows, 128), lambda i, off=off: (0, off + i))
    full = pl.BlockSpec((rows, 128), lambda i: (0, 0))
    return pl.pallas_call(
        partial(attend_backward_kernel, chunk=rows // 2),
        grid=(n,),
        in_specs=[
            col(0),
            col(n),
            col(2 * n),
            col(0),
            col(0),
            pl.BlockSpec((1, 2, rows), lambda i: (i, 0, 0)),
            full,
            full,
        ],
        out_specs=[
            pl.BlockSpec((rows, 3 * width), lambda i: (0, 0)),
            pl.BlockSpec((2, 128), lambda i: (0, i)),
        ],
        out_shape=[
            jax.ShapeDtypeStruct((rows, 3 * width), bf16),
            jax.ShapeDtypeStruct((2, width), f32),
        ],
        compiler_params=pltpu.CompilerParams(vmem_limit_bytes=VMEM_LIMIT),
        cost_estimate=pl.CostEstimate(flops=1, bytes_accessed=1, transcendentals=0),
        name="attend_backward",
    )(joined, joined, joined, grad_attended, attended, lse, fq, fk)


def total(values):
    out = values[0].astype(f32)
    for value in values[1:]:
        out = out + value.astype(f32)
    return out


def pick(values, axis, index):
    return lax.dynamic_index_in_dim(values, index, axis, keepdims=False)


def pack(grads, n, width):
    pieces = []
    for grad in grads:
        rows, columns = grad.shape
        blocks = grad.reshape(n, rows // n, columns)
        pieces += [blocks[:, :, at : at + width] for at in range(0, columns, width)]
    return jnp.concatenate(pieces, axis=1)


def unpack(packed, shapes, n):
    width = packed.shape[1]
    outs = []
    start = 0
    for rows, columns in shapes:
        count = rows // n
        pieces = []
        for unused in range(0, columns, width):
            pieces.append(packed[start : start + count])
            start += count
        outs.append(jnp.concatenate(pieces, axis=1))
    return outs


class PairSum:
    def __init__(self, a, b, me):
        self.me = me
        self.n = a.shape[0]
        self.rows = a.shape[1]
        dims = (4, 2, 2, 2)
        self.terms = [[a.reshape(dims + a.shape[1:])], [b.reshape(dims + b.shape[1:])]]
        self.round = 0
        self.result = None
        self.pending = None

    def bit(self, at):
        return (self.me >> at) & 1

    def steps(self):
        x, y = self.bit(1), self.bit(2)
        core = self.bit(0)
        top = self.me >> 3
        return [((3, core), (3, core)), ((2, x), (1, y)), ((1, y), (1, x)), ((0, top), (0, top))][self.round]

    def part(self, which, other):
        axis, mine = self.steps()[which]
        return total([pick(t, axis, mine ^ other) for t in self.terms[which]]).astype(bf16)

    def sends(self):
        if self.round == 0:
            return [jnp.concatenate([self.part(0, 1), self.part(1, 1)], axis=-2)]
        if self.round < 3:
            return [self.part(0, 1), self.part(1, 1)]
        return [jnp.concatenate([self.part(0, k), self.part(1, k)], axis=-2) for k in (1, 2, 3)]

    def launch(self, sends):
        partners = [[1], [2, 4], [4, 2], [8, 16, 24]][self.round]
        self.pending = [
            lax.ppermute(sent, "dp", [(i, i ^ p) for i in range(self.n)])
            for sent, p in zip(sends, partners)
        ]

    def land(self, came):
        self.pending = None
        steps = self.steps()
        if self.round in (0, 3):
            came = [
                [value[..., : self.rows, :] for value in came],
                [value[..., self.rows :, :] for value in came],
            ]
        else:
            came = [[came[0]], [came[1]]]
        for which in (0, 1):
            axis, mine = steps[which]
            self.terms[which] = [pick(t, axis, mine) for t in self.terms[which]] + came[which]
        self.round += 1
        if self.round == 4:
            self.result = [total(self.terms[0]), total(self.terms[1])]


class SmallSum:
    def __init__(self, blocks, me):
        self.me = me
        self.n = blocks.shape[0]
        self.terms = [blocks.reshape((4, 4, 2) + blocks.shape[1:])]
        self.round = 0
        self.result = None
        self.pending = None

    def steps(self):
        me = self.me
        return [(2, me & 1, (1,), 1), (1, (me >> 1) & 3, (1, 2, 3), 2), (0, me >> 3, (1, 2, 3), 8)][self.round]

    def sends(self):
        axis, mine, others, unused = self.steps()
        return [total([pick(t, axis, mine ^ k) for t in self.terms]) for k in others]

    def launch(self, sends):
        unused, unused, others, unit = self.steps()
        self.pending = [
            lax.ppermute(sent, "dp", [(i, i ^ (k * unit)) for i in range(self.n)])
            for sent, k in zip(sends, others)
        ]

    def land(self, came):
        self.pending = None
        axis, mine, unused, unused = self.steps()
        self.terms = [pick(t, axis, mine) for t in self.terms] + list(came)
        self.round += 1
        if self.round == 3:
            self.result = total(self.terms)


class Summed:
    def __init__(self, blocks):
        self.result = lax.psum_scatter(blocks, "dp", scatter_dimension=0, tiled=False)
        self.pending = None


class Scattered:
    def __init__(self, a, b):
        both = jnp.concatenate([a, b], axis=1)
        out = lax.psum_scatter(both, "dp", scatter_dimension=0, tiled=False).astype(f32)
        self.result = [out[: a.shape[1]], out[a.shape[1] :]]
        self.pending = None


def pair_sum(a, b, me, n):
    if n == 32 and a.shape[1] % 8 == 0 and b.shape[1] % 8 == 0:
        return PairSum(a, b, me)
    return Scattered(a, b)


def fence(main, exchanges):
    flying = [e for e in exchanges if e.pending is not None]
    main, came = lax.optimization_barrier((main, [e.pending for e in flying]))
    for e, values in zip(flying, came):
        e.land(values)
    ready = [e for e in exchanges if e.result is None]
    main, sends = lax.optimization_barrier((main, [e.sends() for e in ready]))
    for e, values in zip(ready, sends):
        e.launch(values)
    return main


def small_sum(vectors, me, n):
    pieces = [vector.reshape(LAYERS, n, -1).transpose(1, 0, 2).reshape(n, -1) for vector in vectors]
    packed = jnp.concatenate(pieces, axis=1)
    blocks = jnp.pad(packed, ((0, 0), (0, -packed.shape[1] % 1024))).reshape(n, -1, 128)
    sizes = [piece.shape[1] for piece in pieces]
    return (SmallSum(blocks, me) if n == 32 else Summed(blocks)), sizes


def unpack_small(block, sizes):
    flat = block.reshape(-1)
    outs = []
    start = 0
    for size in sizes:
        outs.append(flat[start : start + size].reshape(LAYERS, -1))
        start += size
    return outs


def row_block(width):
    return pl.BlockSpec((ROWS_STEP, width), lambda i: (i, 0))


def vector(width):
    return pl.BlockSpec((LAYERS, width), lambda i: (0, 0))


def row(ref, layer):
    return ref[layer : layer + 1, :].astype(f32)


def resident(layer, rows, columns):
    return pl.BlockSpec((None, rows, columns), lambda i: (layer, 0, 0), pipeline_mode=pl.Buffered(1))


def kept(rows, columns):
    return pl.BlockSpec((rows, columns), lambda i: (0, 0))


def standardize(values):
    center = values - jnp.mean(values, axis=-1, keepdims=True)
    scale = lax.rsqrt(jnp.mean(center * center, axis=-1, keepdims=True) + EPSILON)
    return center * scale, scale


def columns_sum(values):
    return jnp.sum(values, axis=0, keepdims=True)


def dense_call(kernel, name, rows, in_specs, out_specs, out_shape, flops, moved):
    return pl.pallas_call(
        kernel,
        grid=(rows // ROWS_STEP,),
        in_specs=in_specs,
        out_specs=out_specs,
        out_shape=out_shape,
        compiler_params=pltpu.CompilerParams(vmem_limit_bytes=VMEM_LIMIT),
        cost_estimate=pl.CostEstimate(flops=1, bytes_accessed=1, transcendentals=0),
        name=name,
    )


def project_kernel(layer, stream_ref, gain_ref, shift_ref, w_ref, b_ref, normed_ref, joined_ref):
    unit, unused = standardize(stream_ref[...].astype(f32))
    normed = (unit * row(gain_ref, layer) + row(shift_ref, layer)).astype(bf16)
    normed_ref[...] = normed
    joined_ref[...] = (dot32(normed, w_ref[...]) + row(b_ref, layer)).astype(bf16)


def project(layer, stream, gain, shift, qkv_w, bias):
    rows, width = stream.shape
    out = jax.ShapeDtypeStruct
    return dense_call(
        partial(project_kernel, layer),
        "project",
        rows,
        [row_block(width), vector(width), vector(width)]
        + [resident(layer, width, 3 * width), vector(3 * width)],
        [row_block(width), row_block(3 * width)],
        [out((rows, width), bf16), out((rows, 3 * width), bf16)],
        6 * rows * width * width,
        12 * rows * width + 6 * width * width,
    )(stream, gain, shift, qkv_w, bias)


def mlp_forward_kernel(
    layer, att_ref, stream_ref, out_w_ref, out_b_ref, gain_ref, shift_ref, up_w_ref, up_b_ref,
    down_w_ref, down_b_ref, middle_ref, normed_ref, act_ref, slope_ref, result_ref,
):
    width = att_ref.shape[1]
    middle = (
        stream_ref[...].astype(f32) + dot32(att_ref[...], out_w_ref[...]) + row(out_b_ref, layer)
    )
    middle_ref[...] = middle
    unit, unused = standardize(middle)
    normed = (unit * row(gain_ref, layer) + row(shift_ref, layer)).astype(bf16)
    normed_ref[...] = normed
    result = middle + row(down_b_ref, layer)
    for at in range(0, up_w_ref.shape[1], width):
        span = slice(at, at + width)
        hidden = dot32(normed, up_w_ref[:, span]) + up_b_ref[layer : layer + 1, span].astype(f32)
        below = 0.5 + 0.5 * lax.erf(hidden * 0.7071067811865476)
        act = (hidden * below).astype(bf16)
        slope = below + hidden * (0.3989422804014327 * jnp.exp(-0.5 * (hidden * hidden)))
        act_ref[:, span] = act
        slope_ref[:, span] = slope.astype(bf16)
        result = result + dot32(act, down_w_ref[span, :])
    result_ref[...] = result


def mlp_forward(layer, attended, stream, out_w, out_b, gain, shift, up_w, up_b, down_w, down_b):
    rows, width = attended.shape
    up = up_w.shape[2]
    out = jax.ShapeDtypeStruct
    return dense_call(
        partial(mlp_forward_kernel, layer),
        "mlp_forward",
        rows,
        [row_block(width), row_block(width), resident(layer, width, width)]
        + [vector(width)] * 3
        + [resident(layer, width, up), vector(up), resident(layer, up, width), vector(width)],
        [row_block(width), row_block(width), row_block(up), row_block(up), row_block(width)],
        [
            out((rows, width), f32),
            out((rows, width), bf16),
            out((rows, up), bf16),
            out((rows, up), bf16),
            out((rows, width), f32),
        ],
        2 * rows * width * (width + 2 * up),
        4 * rows * (4 * width + up) + 4 * width * (width + up),
    )(attended, stream, out_w, out_b, gain, shift, up_w, up_b, down_w, down_b)


def mlp_backward_kernel(
    layer, grad_ref, slope_ref, middle_ref, gain_ref, up_w_ref, down_w_ref, out_w_ref,
    low_ref, hidden_ref, grad_middle_ref, branch_ref, attended_ref, up_sum_ref, sums_ref,
):
    width = grad_ref.shape[1]

    @pl.when(pl.program_id(0) == 0)
    def _():
        up_sum_ref[...] = jnp.zeros_like(up_sum_ref)
        sums_ref[...] = jnp.zeros_like(sums_ref)

    grad = grad_ref[...]
    low = grad.astype(bf16)
    low_ref[...] = low
    normed = jnp.zeros(grad.shape, f32)
    for at in range(0, up_w_ref.shape[1], width):
        span = slice(at, at + width)
        act = dot_nt(low, down_w_ref[span, :])
        hidden = (slope_ref[:, span].astype(f32) * act).astype(bf16)
        hidden_ref[:, span] = hidden
        up_sum_ref[:, span] += columns_sum(hidden.astype(f32))
        normed = normed + dot_nt(hidden, up_w_ref[:, span])
    unit, scale = standardize(middle_ref[...])
    scaled = normed * row(gain_ref, layer)
    inner = scaled - jnp.mean(scaled, axis=-1, keepdims=True)
    inner = inner - unit * jnp.mean(scaled * unit, axis=-1, keepdims=True)
    middle = grad + inner * scale
    grad_middle_ref[...] = middle
    branch = middle.astype(bf16)
    branch_ref[...] = branch
    attended_ref[...] = dot_nt(branch, out_w_ref[...]).astype(bf16)
    sums_ref[0:1, :] += columns_sum(low.astype(f32))
    sums_ref[1:2, :] += columns_sum(normed * unit)
    sums_ref[2:3, :] += columns_sum(normed)
    sums_ref[3:4, :] += columns_sum(branch.astype(f32))


def mlp_backward(layer, grad, slope, middle, gain, up_w, down_w, out_w):
    rows, width = grad.shape
    up = up_w.shape[2]
    out = jax.ShapeDtypeStruct
    return dense_call(
        partial(mlp_backward_kernel, layer),
        "mlp_backward",
        rows,
        [row_block(width), row_block(up), row_block(width), vector(width)]
        + [resident(layer, width, up), resident(layer, up, width), resident(layer, width, width)],
        [row_block(width), row_block(up)] + [row_block(width)] * 3 + [kept(1, up), kept(8, width)],
        [
            out((rows, width), bf16),
            out((rows, up), bf16),
            out((rows, width), f32),
            out((rows, width), bf16),
            out((rows, width), bf16),
            out((1, up), f32),
            out((8, width), f32),
        ],
        2 * rows * width * (width + 2 * up),
        4 * rows * (5 * width + up) + 4 * width * (width + up),
    )(grad, slope, middle, gain, up_w, down_w, out_w)


def project_backward_kernel(layer, joined_ref, stream_ref, grad_ref, gain_ref, w_ref, result_ref, sums_ref):
    @pl.when(pl.program_id(0) == 0)
    def _():
        sums_ref[...] = jnp.zeros_like(sums_ref)

    normed = dot_nt(joined_ref[...], w_ref[...])
    unit, scale = standardize(stream_ref[...].astype(f32))
    scaled = normed * row(gain_ref, layer)
    inner = scaled - jnp.mean(scaled, axis=-1, keepdims=True)
    inner = inner - unit * jnp.mean(scaled * unit, axis=-1, keepdims=True)
    result_ref[...] = grad_ref[...] + inner * scale
    sums_ref[0:1, :] += columns_sum(normed * unit)
    sums_ref[1:2, :] += columns_sum(normed)


def project_backward(layer, joined, stream, grad, gain, qkv_w):
    rows, width = grad.shape
    out = jax.ShapeDtypeStruct
    return dense_call(
        partial(project_backward_kernel, layer),
        "project_backward",
        rows,
        [row_block(3 * width), row_block(width), row_block(width), vector(width)]
        + [resident(layer, width, 3 * width)],
        [row_block(width), kept(8, width)],
        [out((rows, width), f32), out((8, width), f32)],
        6 * rows * width * width,
        18 * rows * width + 6 * width * width,
    )(joined, stream, grad, gain, qkv_w)


def layer_forward(layer, stream, weights, fq, fk):
    gain_one, shift_one, qkv_w, bias, out_w, out_b, gain_two, shift_two, up_w, up_b, down_w, down_b = weights
    normed, joined = project(layer, stream, gain_one, shift_one, qkv_w, bias)
    attended, lse = attend_forward(joined, fq, fk)
    middle, normed_two, activated, slope, output = mlp_forward(
        layer, attended, stream, out_w, out_b, gain_two, shift_two, up_w, up_b, down_w, down_b
    )
    return output, (stream, normed, joined, attended, lse, middle, normed_two, slope, activated)


def layer_backward(layer, grad_stream, cache, weights, fq, fk, tie):
    stream, normed, joined, attended, lse, middle, normed_two, slope, activated = cache
    gain_one, shift_one, qkv_w, bias, out_w, out_b, gain_two, shift_two, up_w, up_b, down_w, down_b = weights
    low, grad_hidden, grad_middle, branch, grad_attended, grad_up_b, sums = mlp_backward(
        layer, grad_stream, slope, middle, gain_two, up_w, down_w, out_w
    )
    grad_down_w = jnp.einsum("tf,td->fd", activated, low, preferred_element_type=f32).astype(bf16)
    grad_up_w = jnp.einsum("td,tf->df", normed_two, grad_hidden, preferred_element_type=f32).astype(bf16)
    branch = tie("hidden", branch, (grad_down_w, grad_up_w))
    grad_out_w = jnp.einsum("tc,td->cd", attended, branch, preferred_element_type=f32).astype(bf16)
    grad_attended = tie("attended", grad_attended, (grad_out_w,))
    grad_joined, column_sums = attend_backward(joined, grad_attended, attended, lse, fq, fk)
    grad_joined = tie("joined", grad_joined, ())
    grad_qkv_w = jnp.einsum("td,te->de", normed, grad_joined, preferred_element_type=f32).astype(bf16)
    grad_joined = tie("qkv", grad_joined, (grad_qkv_w,))
    grad_input, sums_one = project_backward(layer, grad_joined, stream, grad_middle, gain_one, qkv_w)
    small = (
        sums_one[0],
        sums_one[1],
        column_sums.reshape(-1),
        sums[3],
        sums[1],
        sums[2],
        grad_up_b[0],
        sums[0],
    )
    return grad_input, (grad_qkv_w, grad_out_w, grad_up_w, grad_down_w), small


def local(n, *arguments):
    (
        patches,
        img_length,
        img_start,
        class_count,
        *stacked,
        cls_weight,
        cls_bias,
        logit_grad,
    ) = arguments
    me = lax.axis_index("dp")
    row_count, width = patches.shape
    up_width = stacked[8].shape[2]
    slot_count = img_length.shape[0]
    positions = jnp.arange(row_count, dtype=jnp.int32)
    inside = (positions[None, :] >= img_start[:, None]) & (
        positions[None, :] < (img_start + img_length)[:, None]
    )
    member = inside.astype(f32)
    live_rows = jnp.sum(inside.astype(jnp.int32), axis=0)
    segment = (
        jnp.sum(inside.astype(jnp.int32) * jnp.arange(slot_count, dtype=jnp.int32)[:, None], axis=0)
        + (1 - live_rows) * slot_count
    )
    fq, fk = seg_features(segment, slot_count)
    counts = jnp.maximum(img_length, 1).astype(f32)
    live_columns = jnp.arange(cls_weight.shape[1], dtype=jnp.int32) < class_count[0]
    masked_grad = jnp.where(live_columns[None, :], logit_grad, jnp.zeros_like(logit_grad))
    pooled_grad = lax.psum_scatter(
        dot_nt(masked_grad, cls_weight), "dp", scatter_dimension=0, tiled=True
    )
    weights = list(stacked)
    qv_bias = weights[3]
    weights[3] = jnp.concatenate(
        [qv_bias[:, :width], jnp.zeros((LAYERS, width), bf16), qv_bias[:, width:]], axis=1
    )
    stream = patches
    caches = []
    for layer in range(LAYERS):
        stream, cache = layer_forward(layer, stream, weights, fq, fk)
        caches.append(cache)
    sums = jnp.dot(member, stream, precision=HIGHEST, preferred_element_type=f32)
    side = jnp.broadcast_to(counts[:, None], (slot_count, 128))
    gathered = lax.all_gather(jnp.concatenate([sums, side], axis=1), "dp", axis=0, tiled=True)
    grad_stream = jnp.einsum(
        "it,id->td",
        member,
        pooled_grad / counts[:, None],
        precision=HIGHEST,
        preferred_element_type=f32,
    )
    last = {}

    def tie_last(name, value, grads):
        last[name] = grads
        if name != "qkv":
            return value
        both = pack(last["hidden"] + last["attended"] + grads, n, width)
        value, both = lax.optimization_barrier((value, both))
        last["sum"] = lax.psum_scatter(both, "dp", scatter_dimension=0, tiled=False)
        return value

    qk = 2 * width

    def tie_first(name, value, grads):
        if name == "hidden":
            first.append(pair_sum(pack(grads[:1], n, width), pack(grads[1:], n, width), me, n))
        if name == "attended":
            last["out"] = grads[0]
            value, last["out"] = fence((value, last["out"]), first)
            return value
        if name == "qkv":
            side_a = pack([grads[0][:, :qk]], n, width)
            side_b = pack([grads[0][:, qk:], last["out"]], n, width)
            first.append(pair_sum(side_a, side_b, me, n))
            return fence(value, first[1:])
        return fence(value, first)

    first = []
    grad_stream, unused, small_last = layer_backward(1, grad_stream, caches[1], weights, fq, fk, tie_last)
    grad_stream, gathered = lax.optimization_barrier((grad_stream, gathered))
    grad_stream, unused, small_first = layer_backward(0, grad_stream, caches[0], weights, fq, fk, tie_first)
    small, sizes = small_sum([jnp.stack(pair) for pair in zip(small_first, small_last)], me, n)
    first.append(small)
    grad_stream = fence(grad_stream, first)
    grad_stream = fence(grad_stream, first[1:])
    grad_stream, last["sum"] = lax.optimization_barrier((grad_stream, last["sum"]))
    while any(e.result is None for e in first):
        grad_stream = fence(grad_stream, first)
    gathered = (gathered[:, :width] / gathered[:, width : width + 1]).astype(bf16)
    scores = dot32(gathered, cls_weight) + cls_bias.astype(f32)
    logits = jnp.where(live_columns[None, :], scores, 0.0)
    grad_cls_weight = jnp.einsum("id,ic->dc", gathered, masked_grad, preferred_element_type=f32)
    grad_cls_bias = jnp.sum(masked_grad.astype(f32), axis=0)
    square = (width, width)
    wide = (width, up_width)
    tall = (up_width, width)
    down_last, up_last, out_last, qkv_last = unpack(
        last["sum"].astype(f32), [tall, wide, square, (width, 3 * width)], n
    )
    (down_first,) = unpack(first[0].result[0], [tall], n)
    (up_first,) = unpack(first[0].result[1], [wide], n)
    (qk_first,) = unpack(first[1].result[0], [(width, qk)], n)
    v_first, out_first = unpack(first[1].result[1], [square, square], n)
    qkv_first = jnp.concatenate([qk_first, v_first], axis=1)
    qkv_sum = jnp.stack([qkv_first, qkv_last])
    out_sum = jnp.stack([out_first, out_last])
    up_sum = jnp.stack([up_first, up_last])
    down_sum = jnp.stack([down_first, down_last])
    gain_one, shift_one, qv_b, out_b, gain_two, shift_two, up_b, down_b = unpack_small(
        small.result, sizes
    )
    return (
        logits,
        grad_stream,
        gain_one,
        shift_one,
        qkv_sum,
        qv_b,
        out_sum,
        out_b,
        gain_two,
        shift_two,
        up_sum,
        up_b,
        down_sum,
        down_b,
        grad_cls_weight,
        grad_cls_bias,
    )


def solution(mesh):
    whole = P()
    placed = (
        (P("dp", None), P("dp"), P("dp"), P("dp"))
        + (whole,) * 12
        + (P(None, "dp"), P("dp"), P(None, "dp"))
    )
    vector = P(None, "dp")
    matrix = P(None, "dp", None)
    return jax.shard_map(
        partial(local, mesh.size),
        mesh=mesh,
        in_specs=placed,
        out_specs=(
            P(None, "dp"),
            P("dp", None),
            vector,
            vector,
            matrix,
            vector,
            matrix,
            vector,
            vector,
            vector,
            matrix,
            vector,
            matrix,
            vector,
            P(None, "dp"),
            P("dp"),
        ),
        check_vma=False,
    )
```

```python
from functools import partial

import jax
import jax.numpy as jnp
from jax import lax
from jax.experimental import pallas as pl
from jax.experimental.pallas import tpu as pltpu
from jax.sharding import PartitionSpec as P

HD = 64
LAYERS = 2
BIG = 1e30
EPSILON = 1e-06
HIGHEST = lax.Precision.HIGHEST
NT = (((1,), (1,)), ((), ()))
f32 = jnp.float32
bf16 = jnp.bfloat16
VMEM_LIMIT = 56 << 20
ROWS_STEP = 256


def dot32(left, right):
    return jnp.dot(left, right, preferred_element_type=f32)


def dot_nt(left, right):
    return lax.dot_general(left, right, NT, preferred_element_type=f32)


def seg_features(segment, slot_count):
    lane = jnp.arange(128, dtype=jnp.int32) % HD
    hit = segment[:, None] == lane[None, :]
    live = (lane <= slot_count)[None, :]
    query_side = (hit & live).astype(bf16)
    key_side = jnp.where(live & ~hit, -BIG, 0.0).astype(bf16)
    return query_side, key_side


def attend_forward_kernel(q_ref, k_ref, v_ref, fq_ref, fk_ref, o_ref, lse_ref, *, chunk):
    rows = q_ref.shape[0]
    left = lax.broadcasted_iota(jnp.int32, (rows, 128), 1) < HD
    q = q_ref[...] * jnp.asarray(HD**-0.5, bf16)
    k = k_ref[...]
    fq = fq_ref[...]
    fk = fk_ref[...]
    v_t = v_ref[...].T
    q_side = [jnp.where(left, q, fq), jnp.where(left, fq, q)]
    k_side = [jnp.where(left, k, fk), jnp.where(left, fk, k)]
    for c in range(rows // chunk):
        span = slice(c * chunk, (c + 1) * chunk)
        outs = []
        for h in range(2):
            scores = dot_nt(k_side[h], q_side[h][span])
            largest = jnp.max(scores, axis=0, keepdims=True)
            p = jnp.exp(scores - largest)
            total = jnp.sum(p, axis=0, keepdims=True)
            mixed = dot32(v_t[h * HD : (h + 1) * HD], p.astype(bf16))
            outs.append(mixed / total)
            lse_ref[0, h : h + 1, span] = largest + jnp.log(total)
        o_ref[span, :] = jnp.concatenate(outs, axis=0).T.astype(bf16)


def attend_forward(joined, fq, fk):
    rows = joined.shape[0]
    width = joined.shape[1] // 3
    n = width // 128
    col = lambda off: pl.BlockSpec((rows, 128), lambda i, off=off: (0, off + i))
    full = pl.BlockSpec((rows, 128), lambda i: (0, 0))
    return pl.pallas_call(
        partial(attend_forward_kernel, chunk=rows),
        grid=(n,),
        in_specs=[col(0), col(n), col(2 * n), full, full],
        out_specs=[
            pl.BlockSpec((rows, 128), lambda i: (0, i)),
            pl.BlockSpec((1, 2, rows), lambda i: (i, 0, 0)),
        ],
        out_shape=[
            jax.ShapeDtypeStruct((rows, width), bf16),
            jax.ShapeDtypeStruct((n, 2, rows), f32),
        ],
        compiler_params=pltpu.CompilerParams(vmem_limit_bytes=VMEM_LIMIT),
        cost_estimate=pl.CostEstimate(flops=1, bytes_accessed=1, transcendentals=0),
        name="attend_forward",
    )(joined, joined, joined, fq, fk)


def attend_backward_kernel(
    q_ref, k_ref, v_ref, g_ref, o_ref, lse_ref, fq_ref, fk_ref, dj_ref, cs_ref, *, chunk
):
    rows = q_ref.shape[0]
    width = dj_ref.shape[1] // 3
    step = pl.program_id(0)
    left = lax.broadcasted_iota(jnp.int32, (rows, 128), 1) < HD
    left_chunk = left[:chunk]
    scale = HD**-0.5
    q = q_ref[...] * jnp.asarray(scale, bf16)
    k = k_ref[...]
    v = v_ref[...]
    g = g_ref[...]
    fq = fq_ref[...]
    fk = fk_ref[...]
    zero = jnp.zeros_like(q)
    k_t = k.T
    product_t = (g.astype(f32) * o_ref[...].astype(f32)).T
    q_side = [jnp.where(left, q, fq), jnp.where(left, fq, q)]
    k_side = [jnp.where(left, k, fk), jnp.where(left, fk, k)]
    v_side = [jnp.where(left, v, zero), jnp.where(left, zero, v)]
    delta = [jnp.sum(product_t[h * HD : (h + 1) * HD], axis=0, keepdims=True) for h in range(2)]
    lse = [lse_ref[0, h : h + 1, :] for h in range(2)]
    dq = [None, None]
    sum_v = jnp.zeros((1, 128), f32)
    for c in range(rows // chunk):
        span = slice(c * chunk, (c + 1) * chunk)
        dk = []
        dv = []
        for h in range(2):
            scores = dot_nt(k_side[h][span], q_side[h])
            p = jnp.exp(scores - lse[h])
            dp = dot_nt(v_side[h][span], g)
            dv.append(dot32(p.astype(bf16), g))
            ds = (p * (dp - delta[h])).astype(bf16)
            dk.append(dot32(ds, q))
            part = dot32(k_t[h * HD : (h + 1) * HD, span], ds)
            dq[h] = part if dq[h] is None else dq[h] + part
        dk_low = jnp.where(left_chunk, dk[0], dk[1]).astype(bf16)
        dv_low = jnp.where(left_chunk, dv[0], dv[1]).astype(bf16)
        dj_ref[span, pl.ds(pl.multiple_of(width + step * 128, 128), 128)] = dk_low
        dj_ref[span, pl.ds(pl.multiple_of(2 * width + step * 128, 128), 128)] = dv_low
        sum_v += jnp.sum(dv_low.astype(f32), axis=0, keepdims=True)
    dq_low = (jnp.concatenate(dq, axis=0) * scale).T.astype(bf16)
    dj_ref[:, pl.ds(pl.multiple_of(step * 128, 128), 128)] = dq_low
    cs_ref[0:1, :] = jnp.sum(dq_low.astype(f32), axis=0, keepdims=True)
    cs_ref[1:2, :] = sum_v


def attend_backward(joined, grad_attended, attended, lse, fq, fk):
    rows = joined.shape[0]
    width = joined.shape[1] // 3
    n = width // 128
    col = lambda off: pl.BlockSpec((rows, 128), lambda i, off=off: (0, off + i))
    full = pl.BlockSpec((rows, 128), lambda i: (0, 0))
    return pl.pallas_call(
        partial(attend_backward_kernel, chunk=rows // 2),
        grid=(n,),
        in_specs=[
            col(0),
            col(n),
            col(2 * n),
            col(0),
            col(0),
            pl.BlockSpec((1, 2, rows), lambda i: (i, 0, 0)),
            full,
            full,
        ],
        out_specs=[
            pl.BlockSpec((rows, 3 * width), lambda i: (0, 0)),
            pl.BlockSpec((2, 128), lambda i: (0, i)),
        ],
        out_shape=[
            jax.ShapeDtypeStruct((rows, 3 * width), bf16),
            jax.ShapeDtypeStruct((2, width), f32),
        ],
        compiler_params=pltpu.CompilerParams(vmem_limit_bytes=VMEM_LIMIT),
        cost_estimate=pl.CostEstimate(flops=1, bytes_accessed=1, transcendentals=0),
        name="attend_backward",
    )(joined, joined, joined, grad_attended, attended, lse, fq, fk)


def total(values):
    out = values[0].astype(f32)
    for value in values[1:]:
        out = out + value.astype(f32)
    return out


def pick(values, axis, index):
    return lax.dynamic_index_in_dim(values, index, axis, keepdims=False)


def pack(grads, n, width):
    pieces = []
    for grad in grads:
        rows, columns = grad.shape
        blocks = grad.reshape(n, rows // n, columns)
        pieces += [blocks[:, :, at : at + width] for at in range(0, columns, width)]
    return jnp.concatenate(pieces, axis=1)


def unpack(packed, shapes, n):
    width = packed.shape[1]
    outs = []
    start = 0
    for rows, columns in shapes:
        count = rows // n
        pieces = []
        for unused in range(0, columns, width):
            pieces.append(packed[start : start + count])
            start += count
        outs.append(jnp.concatenate(pieces, axis=1))
    return outs


class PairSum:
    def __init__(self, a, b, me):
        self.me = me
        self.n = a.shape[0]
        self.rows = a.shape[1]
        dims = (4, 2, 2, 2)
        self.terms = [[a.reshape(dims + a.shape[1:])], [b.reshape(dims + b.shape[1:])]]
        self.round = 0
        self.result = None
        self.pending = None

    def bit(self, at):
        return (self.me >> at) & 1

    def steps(self):
        x, y = self.bit(1), self.bit(2)
        core = self.bit(0)
        top = self.me >> 3
        return [((3, core), (3, core)), ((2, x), (1, y)), ((1, y), (1, x)), ((0, top), (0, top))][self.round]

    def part(self, which, other):
        axis, mine = self.steps()[which]
        return total([pick(t, axis, mine ^ other) for t in self.terms[which]]).astype(bf16)

    def sends(self):
        if self.round == 0:
            return [jnp.concatenate([self.part(0, 1), self.part(1, 1)], axis=-2)]
        if self.round < 3:
            return [self.part(0, 1), self.part(1, 1)]
        return [jnp.concatenate([self.part(0, k), self.part(1, k)], axis=-2) for k in (1, 2, 3)]

    def launch(self, sends):
        partners = [[1], [2, 4], [4, 2], [8, 16, 24]][self.round]
        self.pending = [
            lax.ppermute(sent, "dp", [(i, i ^ p) for i in range(self.n)])
            for sent, p in zip(sends, partners)
        ]

    def land(self, came):
        self.pending = None
        steps = self.steps()
        if self.round in (0, 3):
            came = [
                [value[..., : self.rows, :] for value in came],
                [value[..., self.rows :, :] for value in came],
            ]
        else:
            came = [[came[0]], [came[1]]]
        for which in (0, 1):
            axis, mine = steps[which]
            self.terms[which] = [pick(t, axis, mine) for t in self.terms[which]] + came[which]
        self.round += 1
        if self.round == 4:
            self.result = [total(self.terms[0]), total(self.terms[1])]


class Scattered:
    def __init__(self, a, b):
        both = jnp.concatenate([a, b], axis=1)
        out = lax.psum_scatter(both, "dp", scatter_dimension=0, tiled=False).astype(f32)
        self.result = [out[: a.shape[1]], out[a.shape[1] :]]
        self.pending = None


def pair_sum(a, b, me, n):
    if n == 32 and a.shape[1] % 8 == 0 and b.shape[1] % 8 == 0:
        return PairSum(a, b, me)
    return Scattered(a, b)


def fence(main, exchanges):
    flying = [e for e in exchanges if e.pending is not None]
    main, came = lax.optimization_barrier((main, [e.pending for e in flying]))
    for e, values in zip(flying, came):
        e.land(values)
    ready = [e for e in exchanges if e.result is None]
    main, sends = lax.optimization_barrier((main, [e.sends() for e in ready]))
    for e, values in zip(ready, sends):
        e.launch(values)
    return main


def pack_small(vectors, n, width):
    pieces = [vector.reshape(LAYERS, n, -1).transpose(1, 0, 2).reshape(n, -1) for vector in vectors]
    packed = jnp.concatenate(pieces, axis=1).astype(bf16)
    padded = jnp.pad(packed, ((0, 0), (0, -packed.shape[1] % (8 * width))))
    return padded.reshape(n, -1, width), [piece.shape[1] for piece in pieces]


def unpack_small(block, sizes):
    flat = block.reshape(-1)
    outs = []
    start = 0
    for size in sizes:
        outs.append(flat[start : start + size].reshape(LAYERS, -1))
        start += size
    return outs


def row_block(width):
    return pl.BlockSpec((ROWS_STEP, width), lambda i: (i, 0))


def vector(width):
    return pl.BlockSpec((LAYERS, width), lambda i: (0, 0))


def row(ref, layer):
    return ref[layer : layer + 1, :].astype(f32)


def resident(layer, rows, columns):
    return pl.BlockSpec((None, rows, columns), lambda i: (layer, 0, 0), pipeline_mode=pl.Buffered(1))


def kept(rows, columns):
    return pl.BlockSpec((rows, columns), lambda i: (0, 0))


def standardize(values):
    center = values - jnp.mean(values, axis=-1, keepdims=True)
    scale = lax.rsqrt(jnp.mean(center * center, axis=-1, keepdims=True) + EPSILON)
    return center * scale, scale


def columns_sum(values):
    return jnp.sum(values, axis=0, keepdims=True)


def dense_call(kernel, name, rows, in_specs, out_specs, out_shape, flops, moved):
    return pl.pallas_call(
        kernel,
        grid=(rows // ROWS_STEP,),
        in_specs=in_specs,
        out_specs=out_specs,
        out_shape=out_shape,
        compiler_params=pltpu.CompilerParams(vmem_limit_bytes=VMEM_LIMIT),
        cost_estimate=pl.CostEstimate(flops=1, bytes_accessed=1, transcendentals=0),
        name=name,
    )


def project_kernel(layer, stream_ref, gain_ref, shift_ref, w_ref, b_ref, normed_ref, joined_ref):
    unit, unused = standardize(stream_ref[...].astype(f32))
    normed = (unit * row(gain_ref, layer) + row(shift_ref, layer)).astype(bf16)
    normed_ref[...] = normed
    joined_ref[...] = (dot32(normed, w_ref[...]) + row(b_ref, layer)).astype(bf16)


def project(layer, stream, gain, shift, qkv_w, bias):
    rows, width = stream.shape
    out = jax.ShapeDtypeStruct
    return dense_call(
        partial(project_kernel, layer),
        "project",
        rows,
        [row_block(width), vector(width), vector(width)]
        + [resident(layer, width, 3 * width), vector(3 * width)],
        [row_block(width), row_block(3 * width)],
        [out((rows, width), bf16), out((rows, 3 * width), bf16)],
        6 * rows * width * width,
        12 * rows * width + 6 * width * width,
    )(stream, gain, shift, qkv_w, bias)


def mlp_forward_kernel(
    layer, att_ref, stream_ref, out_w_ref, out_b_ref, gain_ref, shift_ref, up_w_ref, up_b_ref,
    down_w_ref, down_b_ref, middle_ref, normed_ref, act_ref, slope_ref, result_ref,
):
    width = att_ref.shape[1]
    middle = (
        stream_ref[...].astype(f32) + dot32(att_ref[...], out_w_ref[...]) + row(out_b_ref, layer)
    )
    middle_ref[...] = middle
    unit, unused = standardize(middle)
    normed = (unit * row(gain_ref, layer) + row(shift_ref, layer)).astype(bf16)
    normed_ref[...] = normed
    result = middle + row(down_b_ref, layer)
    for at in range(0, up_w_ref.shape[1], width):
        span = slice(at, at + width)
        hidden = dot32(normed, up_w_ref[:, span]) + up_b_ref[layer : layer + 1, span].astype(f32)
        below = 0.5 + 0.5 * lax.erf(hidden * 0.7071067811865476)
        act = (hidden * below).astype(bf16)
        slope = below + hidden * (0.3989422804014327 * jnp.exp(-0.5 * (hidden * hidden)))
        act_ref[:, span] = act
        slope_ref[:, span] = slope.astype(bf16)
        result = result + dot32(act, down_w_ref[span, :])
    result_ref[...] = result


def mlp_forward(layer, attended, stream, out_w, out_b, gain, shift, up_w, up_b, down_w, down_b):
    rows, width = attended.shape
    up = up_w.shape[2]
    out = jax.ShapeDtypeStruct
    return dense_call(
        partial(mlp_forward_kernel, layer),
        "mlp_forward",
        rows,
        [row_block(width), row_block(width), resident(layer, width, width)]
        + [vector(width)] * 3
        + [resident(layer, width, up), vector(up), resident(layer, up, width), vector(width)],
        [row_block(width), row_block(width), row_block(up), row_block(up), row_block(width)],
        [
            out((rows, width), f32),
            out((rows, width), bf16),
            out((rows, up), bf16),
            out((rows, up), bf16),
            out((rows, width), f32),
        ],
        2 * rows * width * (width + 2 * up),
        4 * rows * (4 * width + up) + 4 * width * (width + up),
    )(attended, stream, out_w, out_b, gain, shift, up_w, up_b, down_w, down_b)


def mlp_backward_kernel(
    layer, grad_ref, slope_ref, middle_ref, gain_ref, up_w_ref, down_w_ref, out_w_ref,
    low_ref, hidden_ref, grad_middle_ref, branch_ref, attended_ref, up_sum_ref, sums_ref,
):
    width = grad_ref.shape[1]

    @pl.when(pl.program_id(0) == 0)
    def _():
        up_sum_ref[...] = jnp.zeros_like(up_sum_ref)
        sums_ref[...] = jnp.zeros_like(sums_ref)

    grad = grad_ref[...]
    low = grad.astype(bf16)
    low_ref[...] = low
    normed = jnp.zeros(grad.shape, f32)
    for at in range(0, up_w_ref.shape[1], width):
        span = slice(at, at + width)
        act = dot_nt(low, down_w_ref[span, :])
        hidden = (slope_ref[:, span].astype(f32) * act).astype(bf16)
        hidden_ref[:, span] = hidden
        up_sum_ref[:, span] += columns_sum(hidden.astype(f32))
        normed = normed + dot_nt(hidden, up_w_ref[:, span])
    unit, scale = standardize(middle_ref[...])
    scaled = normed * row(gain_ref, layer)
    inner = scaled - jnp.mean(scaled, axis=-1, keepdims=True)
    inner = inner - unit * jnp.mean(scaled * unit, axis=-1, keepdims=True)
    middle = grad + inner * scale
    grad_middle_ref[...] = middle
    branch = middle.astype(bf16)
    branch_ref[...] = branch
    attended_ref[...] = dot_nt(branch, out_w_ref[...]).astype(bf16)
    sums_ref[0:1, :] += columns_sum(low.astype(f32))
    sums_ref[1:2, :] += columns_sum(normed * unit)
    sums_ref[2:3, :] += columns_sum(normed)
    sums_ref[3:4, :] += columns_sum(branch.astype(f32))


def mlp_backward(layer, grad, slope, middle, gain, up_w, down_w, out_w):
    rows, width = grad.shape
    up = up_w.shape[2]
    out = jax.ShapeDtypeStruct
    return dense_call(
        partial(mlp_backward_kernel, layer),
        "mlp_backward",
        rows,
        [row_block(width), row_block(up), row_block(width), vector(width)]
        + [resident(layer, width, up), resident(layer, up, width), resident(layer, width, width)],
        [row_block(width), row_block(up)] + [row_block(width)] * 3 + [kept(1, up), kept(8, width)],
        [
            out((rows, width), bf16),
            out((rows, up), bf16),
            out((rows, width), f32),
            out((rows, width), bf16),
            out((rows, width), bf16),
            out((1, up), f32),
            out((8, width), f32),
        ],
        2 * rows * width * (width + 2 * up),
        4 * rows * (5 * width + up) + 4 * width * (width + up),
    )(grad, slope, middle, gain, up_w, down_w, out_w)


def project_backward_kernel(layer, joined_ref, stream_ref, grad_ref, gain_ref, w_ref, result_ref, sums_ref):
    @pl.when(pl.program_id(0) == 0)
    def _():
        sums_ref[...] = jnp.zeros_like(sums_ref)

    normed = dot_nt(joined_ref[...], w_ref[...])
    unit, scale = standardize(stream_ref[...].astype(f32))
    scaled = normed * row(gain_ref, layer)
    inner = scaled - jnp.mean(scaled, axis=-1, keepdims=True)
    inner = inner - unit * jnp.mean(scaled * unit, axis=-1, keepdims=True)
    result_ref[...] = grad_ref[...] + inner * scale
    sums_ref[0:1, :] += columns_sum(normed * unit)
    sums_ref[1:2, :] += columns_sum(normed)


def project_backward(layer, joined, stream, grad, gain, qkv_w):
    rows, width = grad.shape
    out = jax.ShapeDtypeStruct
    return dense_call(
        partial(project_backward_kernel, layer),
        "project_backward",
        rows,
        [row_block(3 * width), row_block(width), row_block(width), vector(width)]
        + [resident(layer, width, 3 * width)],
        [row_block(width), kept(8, width)],
        [out((rows, width), f32), out((8, width), f32)],
        6 * rows * width * width,
        18 * rows * width + 6 * width * width,
    )(joined, stream, grad, gain, qkv_w)


def layer_forward(layer, stream, weights, fq, fk):
    gain_one, shift_one, qkv_w, bias, out_w, out_b, gain_two, shift_two, up_w, up_b, down_w, down_b = weights
    normed, joined = project(layer, stream, gain_one, shift_one, qkv_w, bias)
    attended, lse = attend_forward(joined, fq, fk)
    middle, normed_two, activated, slope, output = mlp_forward(
        layer, attended, stream, out_w, out_b, gain_two, shift_two, up_w, up_b, down_w, down_b
    )
    return output, (stream, normed, joined, attended, lse, middle, normed_two, slope, activated)


def layer_backward(layer, grad_stream, cache, weights, fq, fk, tie):
    stream, normed, joined, attended, lse, middle, normed_two, slope, activated = cache
    gain_one, shift_one, qkv_w, bias, out_w, out_b, gain_two, shift_two, up_w, up_b, down_w, down_b = weights
    low, grad_hidden, grad_middle, branch, grad_attended, grad_up_b, sums = mlp_backward(
        layer, grad_stream, slope, middle, gain_two, up_w, down_w, out_w
    )
    grad_down_w = jnp.einsum("tf,td->fd", activated, low, preferred_element_type=f32).astype(bf16)
    grad_up_w = jnp.einsum("td,tf->df", normed_two, grad_hidden, preferred_element_type=f32).astype(bf16)
    branch = tie("hidden", branch, (grad_down_w, grad_up_w))
    grad_out_w = jnp.einsum("tc,td->cd", attended, branch, preferred_element_type=f32).astype(bf16)
    grad_attended = tie("attended", grad_attended, (grad_out_w,))
    grad_joined, column_sums = attend_backward(joined, grad_attended, attended, lse, fq, fk)
    grad_joined = tie("joined", grad_joined, ())
    grad_input, sums_one = project_backward(layer, grad_joined, stream, grad_middle, gain_one, qkv_w)
    grad_input, grad_joined = tie("input", (grad_input, grad_joined), ())
    grad_qkv_w = jnp.einsum("td,te->de", normed, grad_joined, preferred_element_type=f32).astype(bf16)
    small = (
        sums_one[0],
        sums_one[1],
        column_sums.reshape(-1),
        sums[3],
        sums[1],
        sums[2],
        grad_up_b[0],
        sums[0],
    )
    return grad_input, (grad_qkv_w, grad_out_w, grad_up_w, grad_down_w), small


def local(n, *arguments):
    (
        patches,
        img_length,
        img_start,
        class_count,
        *stacked,
        cls_weight,
        cls_bias,
        logit_grad,
    ) = arguments
    me = lax.axis_index("dp")
    row_count, width = patches.shape
    up_width = stacked[8].shape[2]
    slot_count = img_length.shape[0]
    positions = jnp.arange(row_count, dtype=jnp.int32)
    inside = (positions[None, :] >= img_start[:, None]) & (
        positions[None, :] < (img_start + img_length)[:, None]
    )
    member = inside.astype(f32)
    live_rows = jnp.sum(inside.astype(jnp.int32), axis=0)
    segment = (
        jnp.sum(inside.astype(jnp.int32) * jnp.arange(slot_count, dtype=jnp.int32)[:, None], axis=0)
        + (1 - live_rows) * slot_count
    )
    fq, fk = seg_features(segment, slot_count)
    counts = jnp.maximum(img_length, 1).astype(f32)
    live_columns = jnp.arange(cls_weight.shape[1], dtype=jnp.int32) < class_count[0]
    masked_grad = jnp.where(live_columns[None, :], logit_grad, jnp.zeros_like(logit_grad))
    pooled_grad = lax.psum_scatter(
        dot_nt(masked_grad, cls_weight), "dp", scatter_dimension=0, tiled=True
    )
    weights = list(stacked)
    qv_bias = weights[3]
    weights[3] = jnp.concatenate(
        [qv_bias[:, :width], jnp.zeros((LAYERS, width), bf16), qv_bias[:, width:]], axis=1
    )
    stream = patches
    caches = []
    for layer in range(LAYERS):
        stream, cache = layer_forward(layer, stream, weights, fq, fk)
        caches.append(cache)
    sums = jnp.dot(member, stream, precision=HIGHEST, preferred_element_type=f32)
    side = jnp.broadcast_to(counts[:, None], (slot_count, 128))
    gathered = lax.all_gather(jnp.concatenate([sums, side], axis=1), "dp", axis=0, tiled=True)
    grad_stream = jnp.einsum(
        "it,id->td",
        member,
        pooled_grad / counts[:, None],
        precision=HIGHEST,
        preferred_element_type=f32,
    )
    qk = 2 * width
    last = {}
    first = []

    def tie_last(name, value, grads):
        last[name] = grads
        if name != "attended":
            return value
        both = pack(last["hidden"] + grads, n, width)
        value, both = lax.optimization_barrier((value, both))
        last["sum"] = lax.psum_scatter(both, "dp", scatter_dimension=0, tiled=False)
        return value

    def tie_first(name, value, grads):
        if name == "hidden":
            side_a = pack([grads[0], last["qkv"][:, :width]], n, width)
            side_b = pack([grads[1], last["qkv"][:, width:]], n, width)
            first.append(pair_sum(side_a, side_b, me, n))
        if name == "attended":
            value, last["out"] = fence((value, grads[0]), first)
            return value
        if name == "input":
            value, last["sum"] = lax.optimization_barrier((value, last["sum"]))
        return fence(value, first)

    grad_stream, grads, small_last = layer_backward(1, grad_stream, caches[1], weights, fq, fk, tie_last)
    grad_stream, last["qkv"] = lax.optimization_barrier((grad_stream, grads[0]))
    grad_stream, grads, small_first = layer_backward(0, grad_stream, caches[0], weights, fq, fk, tie_first)
    small, sizes = pack_small([jnp.stack(pair) for pair in zip(small_first, small_last)], n, width)
    side_a = jnp.concatenate([pack([grads[0][:, :qk]], n, width), small], axis=1)
    side_b = pack([grads[0][:, qk:], last["out"]], n, width)
    first.append(pair_sum(side_a, side_b, me, n))
    for unused in range(3):
        grad_stream = fence(grad_stream, first[1:])
    while any(e.result is None for e in first):
        grad_stream = fence(grad_stream, first)
    gathered = (gathered[:, :width] / gathered[:, width : width + 1]).astype(bf16)
    scores = dot32(gathered, cls_weight) + cls_bias.astype(f32)
    logits = jnp.where(live_columns[None, :], scores, 0.0)
    grad_cls_weight = jnp.einsum("id,ic->dc", gathered, masked_grad, preferred_element_type=f32)
    grad_cls_bias = jnp.sum(masked_grad.astype(f32), axis=0)
    square = (width, width)
    wide = (width, up_width)
    tall = (up_width, width)
    down_last, up_last, out_last = unpack(last["sum"].astype(f32), [tall, wide, square], n)
    down_first, q_last = unpack(first[0].result[0], [tall, square], n)
    up_first, kv_last = unpack(first[0].result[1], [wide, (width, qk)], n)
    qkv_last = jnp.concatenate([q_last, kv_last], axis=1)
    qk_rows = 2 * (width // n)
    (qk_first,) = unpack(first[1].result[0][:qk_rows], [(width, qk)], n)
    v_first, out_first = unpack(first[1].result[1], [square, square], n)
    qkv_first = jnp.concatenate([qk_first, v_first], axis=1)
    qkv_sum = jnp.stack([qkv_first, qkv_last])
    out_sum = jnp.stack([out_first, out_last])
    up_sum = jnp.stack([up_first, up_last])
    down_sum = jnp.stack([down_first, down_last])
    gain_one, shift_one, qv_b, out_b, gain_two, shift_two, up_b, down_b = unpack_small(
        first[1].result[0][qk_rows:], sizes
    )
    return (
        logits,
        grad_stream,
        gain_one,
        shift_one,
        qkv_sum,
        qv_b,
        out_sum,
        out_b,
        gain_two,
        shift_two,
        up_sum,
        up_b,
        down_sum,
        down_b,
        grad_cls_weight,
        grad_cls_bias,
    )


def solution(mesh):
    whole = P()
    placed = (
        (P("dp", None), P("dp"), P("dp"), P("dp"))
        + (whole,) * 12
        + (P(None, "dp"), P("dp"), P(None, "dp"))
    )
    vector = P(None, "dp")
    matrix = P(None, "dp", None)
    return jax.shard_map(
        partial(local, mesh.size),
        mesh=mesh,
        in_specs=placed,
        out_specs=(
            P(None, "dp"),
            P("dp", None),
            vector,
            vector,
            matrix,
            vector,
            matrix,
            vector,
            vector,
            vector,
            matrix,
            vector,
            matrix,
            vector,
            P(None, "dp"),
            P("dp"),
        ),
        check_vma=False,
    )
```

```python
from functools import partial

import jax
import jax.numpy as jnp
from jax import lax
from jax.experimental import pallas as pl
from jax.experimental.pallas import tpu as pltpu
from jax.sharding import PartitionSpec as P

HD = 64
LAYERS = 2
BIG = 1e30
EPSILON = 1e-06
HIGHEST = lax.Precision.HIGHEST
NT = (((1,), (1,)), ((), ()))
f32 = jnp.float32
bf16 = jnp.bfloat16
VMEM_LIMIT = 56 << 20
ROWS_STEP = 256


def dot32(left, right):
    return jnp.dot(left, right, preferred_element_type=f32)


def dot_nt(left, right):
    return lax.dot_general(left, right, NT, preferred_element_type=f32)


def seg_features(segment, slot_count):
    lane = jnp.arange(128, dtype=jnp.int32) % HD
    hit = segment[:, None] == lane[None, :]
    live = (lane <= slot_count)[None, :]
    query_side = (hit & live).astype(bf16)
    key_side = jnp.where(live & ~hit, -BIG, 0.0).astype(bf16)
    return query_side, key_side


def attend_forward_kernel(q_ref, k_ref, v_ref, fq_ref, fk_ref, o_ref, lse_ref, *, chunk):
    rows = q_ref.shape[0]
    left = lax.broadcasted_iota(jnp.int32, (rows, 128), 1) < HD
    q = q_ref[...] * jnp.asarray(HD**-0.5, bf16)
    k = k_ref[...]
    fq = fq_ref[...]
    fk = fk_ref[...]
    v_t = v_ref[...].T
    q_side = [jnp.where(left, q, fq), jnp.where(left, fq, q)]
    k_side = [jnp.where(left, k, fk), jnp.where(left, fk, k)]
    for c in range(rows // chunk):
        span = slice(c * chunk, (c + 1) * chunk)
        outs = []
        for h in range(2):
            scores = dot_nt(k_side[h], q_side[h][span])
            largest = jnp.max(scores, axis=0, keepdims=True)
            p = jnp.exp(scores - largest)
            total = jnp.sum(p, axis=0, keepdims=True)
            mixed = dot32(v_t[h * HD : (h + 1) * HD], p.astype(bf16))
            outs.append(mixed / total)
            lse_ref[0, h : h + 1, span] = largest + jnp.log(total)
        o_ref[span, :] = jnp.concatenate(outs, axis=0).T.astype(bf16)


def attend_forward(joined, fq, fk):
    rows = joined.shape[0]
    width = joined.shape[1] // 3
    n = width // 128
    col = lambda off: pl.BlockSpec((rows, 128), lambda i, off=off: (0, off + i))
    full = pl.BlockSpec((rows, 128), lambda i: (0, 0))
    return pl.pallas_call(
        partial(attend_forward_kernel, chunk=rows),
        grid=(n,),
        in_specs=[col(0), col(n), col(2 * n), full, full],
        out_specs=[
            pl.BlockSpec((rows, 128), lambda i: (0, i)),
            pl.BlockSpec((1, 2, rows), lambda i: (i, 0, 0)),
        ],
        out_shape=[
            jax.ShapeDtypeStruct((rows, width), bf16),
            jax.ShapeDtypeStruct((n, 2, rows), f32),
        ],
        compiler_params=pltpu.CompilerParams(vmem_limit_bytes=VMEM_LIMIT),
        cost_estimate=pl.CostEstimate(flops=1, bytes_accessed=1, transcendentals=0),
        name="attend_forward",
    )(joined, joined, joined, fq, fk)


def attend_backward_kernel(
    q_ref, k_ref, v_ref, g_ref, o_ref, lse_ref, fq_ref, fk_ref, dj_ref, cs_ref, *, chunk
):
    rows = q_ref.shape[0]
    width = dj_ref.shape[1] // 3
    step = pl.program_id(0)
    left = lax.broadcasted_iota(jnp.int32, (rows, 128), 1) < HD
    left_chunk = left[:chunk]
    scale = HD**-0.5
    q = q_ref[...] * jnp.asarray(scale, bf16)
    k = k_ref[...]
    v = v_ref[...]
    g = g_ref[...]
    fq = fq_ref[...]
    fk = fk_ref[...]
    zero = jnp.zeros_like(q)
    k_t = k.T
    product_t = (g.astype(f32) * o_ref[...].astype(f32)).T
    q_side = [jnp.where(left, q, fq), jnp.where(left, fq, q)]
    k_side = [jnp.where(left, k, fk), jnp.where(left, fk, k)]
    v_side = [jnp.where(left, v, zero), jnp.where(left, zero, v)]
    delta = [jnp.sum(product_t[h * HD : (h + 1) * HD], axis=0, keepdims=True) for h in range(2)]
    lse = [lse_ref[0, h : h + 1, :] for h in range(2)]
    dq = [None, None]
    sum_v = jnp.zeros((1, 128), f32)
    for c in range(rows // chunk):
        span = slice(c * chunk, (c + 1) * chunk)
        dk = []
        dv = []
        for h in range(2):
            scores = dot_nt(k_side[h][span], q_side[h])
            p = jnp.exp(scores - lse[h])
            dp = dot_nt(v_side[h][span], g)
            dv.append(dot32(p.astype(bf16), g))
            ds = (p * (dp - delta[h])).astype(bf16)
            dk.append(dot32(ds, q))
            part = dot32(k_t[h * HD : (h + 1) * HD, span], ds)
            dq[h] = part if dq[h] is None else dq[h] + part
        dk_low = jnp.where(left_chunk, dk[0], dk[1]).astype(bf16)
        dv_low = jnp.where(left_chunk, dv[0], dv[1]).astype(bf16)
        dj_ref[span, pl.ds(pl.multiple_of(width + step * 128, 128), 128)] = dk_low
        dj_ref[span, pl.ds(pl.multiple_of(2 * width + step * 128, 128), 128)] = dv_low
        sum_v += jnp.sum(dv_low.astype(f32), axis=0, keepdims=True)
    dq_low = (jnp.concatenate(dq, axis=0) * scale).T.astype(bf16)
    dj_ref[:, pl.ds(pl.multiple_of(step * 128, 128), 128)] = dq_low
    cs_ref[0:1, :] = jnp.sum(dq_low.astype(f32), axis=0, keepdims=True)
    cs_ref[1:2, :] = sum_v


def attend_backward(joined, grad_attended, attended, lse, fq, fk):
    rows = joined.shape[0]
    width = joined.shape[1] // 3
    n = width // 128
    col = lambda off: pl.BlockSpec((rows, 128), lambda i, off=off: (0, off + i))
    full = pl.BlockSpec((rows, 128), lambda i: (0, 0))
    return pl.pallas_call(
        partial(attend_backward_kernel, chunk=rows // 2),
        grid=(n,),
        in_specs=[
            col(0),
            col(n),
            col(2 * n),
            col(0),
            col(0),
            pl.BlockSpec((1, 2, rows), lambda i: (i, 0, 0)),
            full,
            full,
        ],
        out_specs=[
            pl.BlockSpec((rows, 3 * width), lambda i: (0, 0)),
            pl.BlockSpec((2, 128), lambda i: (0, i)),
        ],
        out_shape=[
            jax.ShapeDtypeStruct((rows, 3 * width), bf16),
            jax.ShapeDtypeStruct((2, width), f32),
        ],
        compiler_params=pltpu.CompilerParams(vmem_limit_bytes=VMEM_LIMIT),
        cost_estimate=pl.CostEstimate(flops=1, bytes_accessed=1, transcendentals=0),
        name="attend_backward",
    )(joined, joined, joined, grad_attended, attended, lse, fq, fk)


def total(values):
    out = values[0].astype(f32)
    for value in values[1:]:
        out = out + value.astype(f32)
    return out


def pick(values, axis, index):
    return lax.dynamic_index_in_dim(values, index, axis, keepdims=False)


def pack(grads, n, width):
    pieces = []
    for grad in grads:
        rows, columns = grad.shape
        blocks = grad.reshape(n, rows // n, columns)
        pieces += [blocks[:, :, at : at + width] for at in range(0, columns, width)]
    return jnp.concatenate(pieces, axis=1)


def unpack(packed, shapes, n):
    width = packed.shape[1]
    outs = []
    start = 0
    for rows, columns in shapes:
        count = rows // n
        pieces = []
        for unused in range(0, columns, width):
            pieces.append(packed[start : start + count])
            start += count
        outs.append(jnp.concatenate(pieces, axis=1))
    return outs


class PairSum:
    def __init__(self, a, b, me):
        self.me = me
        self.n = a.shape[0]
        self.rows = a.shape[1]
        dims = (4, 2, 2, 2)
        self.terms = [[a.reshape(dims + a.shape[1:])], [b.reshape(dims + b.shape[1:])]]
        self.round = 0
        self.result = None
        self.pending = None

    def bit(self, at):
        return (self.me >> at) & 1

    def steps(self):
        x, y = self.bit(1), self.bit(2)
        core = self.bit(0)
        top = self.me >> 3
        return [((3, core), (3, core)), ((2, x), (1, y)), ((1, y), (1, x)), ((0, top), (0, top))][self.round]

    def part(self, which, other):
        axis, mine = self.steps()[which]
        return total([pick(t, axis, mine ^ other) for t in self.terms[which]]).astype(bf16)

    def sends(self):
        if self.round < 3:
            return [self.part(0, 1), self.part(1, 1)]
        return [jnp.concatenate([self.part(0, k), self.part(1, k)], axis=-2) for k in (1, 2, 3)]

    def launch(self, sends):
        partners = [[1, 1], [2, 4], [4, 2], [8, 16, 24]][self.round]
        self.pending = [
            lax.ppermute(sent, "dp", [(i, i ^ p) for i in range(self.n)])
            for sent, p in zip(sends, partners)
        ]

    def land(self, came):
        self.pending = None
        steps = self.steps()
        if self.round == 3:
            came = [
                [value[..., : self.rows, :] for value in came],
                [value[..., self.rows :, :] for value in came],
            ]
        else:
            came = [[came[0]], [came[1]]]
        for which in (0, 1):
            axis, mine = steps[which]
            self.terms[which] = [pick(t, axis, mine) for t in self.terms[which]] + came[which]
        self.round += 1
        if self.round == 4:
            self.result = [total(self.terms[0]), total(self.terms[1])]


class Scattered:
    def __init__(self, a, b):
        both = jnp.concatenate([a, b], axis=1)
        out = lax.psum_scatter(both, "dp", scatter_dimension=0, tiled=False).astype(f32)
        self.result = [out[: a.shape[1]], out[a.shape[1] :]]
        self.pending = None


def pair_sum(a, b, me, n):
    if n == 32 and a.shape[1] % 8 == 0 and b.shape[1] % 8 == 0:
        return PairSum(a, b, me)
    return Scattered(a, b)


def fence(main, exchanges):
    flying = [e for e in exchanges if e.pending is not None]
    main, came = lax.optimization_barrier((main, [e.pending for e in flying]))
    for e, values in zip(flying, came):
        e.land(values)
    ready = [e for e in exchanges if e.result is None]
    main, sends = lax.optimization_barrier((main, [e.sends() for e in ready]))
    for e, values in zip(ready, sends):
        e.launch(values)
    return main


def pack_small(vectors, n, width):
    pieces = [vector.reshape(LAYERS, n, -1).transpose(1, 0, 2).reshape(n, -1) for vector in vectors]
    packed = jnp.concatenate(pieces, axis=1).astype(bf16)
    padded = jnp.pad(packed, ((0, 0), (0, -packed.shape[1] % (8 * width))))
    return padded.reshape(n, -1, width), [piece.shape[1] for piece in pieces]


def unpack_small(block, sizes):
    flat = block.reshape(-1)
    outs = []
    start = 0
    for size in sizes:
        outs.append(flat[start : start + size].reshape(LAYERS, -1))
        start += size
    return outs


def row_block(width):
    return pl.BlockSpec((ROWS_STEP, width), lambda i: (i, 0))


def vector(width):
    return pl.BlockSpec((LAYERS, width), lambda i: (0, 0))


def row(ref, layer):
    return ref[layer : layer + 1, :].astype(f32)


def resident(layer, rows, columns):
    return pl.BlockSpec((None, rows, columns), lambda i: (layer, 0, 0), pipeline_mode=pl.Buffered(1))


def kept(rows, columns):
    return pl.BlockSpec((rows, columns), lambda i: (0, 0))


def standardize(values):
    center = values - jnp.mean(values, axis=-1, keepdims=True)
    scale = lax.rsqrt(jnp.mean(center * center, axis=-1, keepdims=True) + EPSILON)
    return center * scale, scale


def columns_sum(values):
    return jnp.sum(values, axis=0, keepdims=True)


def dense_call(kernel, name, rows, in_specs, out_specs, out_shape, flops, moved):
    return pl.pallas_call(
        kernel,
        grid=(rows // ROWS_STEP,),
        in_specs=in_specs,
        out_specs=out_specs,
        out_shape=out_shape,
        compiler_params=pltpu.CompilerParams(vmem_limit_bytes=VMEM_LIMIT),
        cost_estimate=pl.CostEstimate(flops=1, bytes_accessed=1, transcendentals=0),
        name=name,
    )


def project_kernel(layer, stream_ref, gain_ref, shift_ref, w_ref, b_ref, normed_ref, joined_ref):
    unit, unused = standardize(stream_ref[...].astype(f32))
    normed = (unit * row(gain_ref, layer) + row(shift_ref, layer)).astype(bf16)
    normed_ref[...] = normed
    joined_ref[...] = (dot32(normed, w_ref[...]) + row(b_ref, layer)).astype(bf16)


def project(layer, stream, gain, shift, qkv_w, bias):
    rows, width = stream.shape
    out = jax.ShapeDtypeStruct
    return dense_call(
        partial(project_kernel, layer),
        "project",
        rows,
        [row_block(width), vector(width), vector(width)]
        + [resident(layer, width, 3 * width), vector(3 * width)],
        [row_block(width), row_block(3 * width)],
        [out((rows, width), bf16), out((rows, 3 * width), bf16)],
        6 * rows * width * width,
        12 * rows * width + 6 * width * width,
    )(stream, gain, shift, qkv_w, bias)


def mlp_forward_kernel(
    layer, att_ref, stream_ref, out_w_ref, out_b_ref, gain_ref, shift_ref, up_w_ref, up_b_ref,
    down_w_ref, down_b_ref, middle_ref, normed_ref, act_ref, slope_ref, result_ref,
):
    width = att_ref.shape[1]
    middle = (
        stream_ref[...].astype(f32) + dot32(att_ref[...], out_w_ref[...]) + row(out_b_ref, layer)
    )
    middle_ref[...] = middle
    unit, unused = standardize(middle)
    normed = (unit * row(gain_ref, layer) + row(shift_ref, layer)).astype(bf16)
    normed_ref[...] = normed
    result = middle + row(down_b_ref, layer)
    for at in range(0, up_w_ref.shape[1], width):
        span = slice(at, at + width)
        hidden = dot32(normed, up_w_ref[:, span]) + up_b_ref[layer : layer + 1, span].astype(f32)
        below = 0.5 + 0.5 * lax.erf(hidden * 0.7071067811865476)
        act = (hidden * below).astype(bf16)
        slope = below + hidden * (0.3989422804014327 * jnp.exp(-0.5 * (hidden * hidden)))
        act_ref[:, span] = act
        slope_ref[:, span] = slope.astype(bf16)
        result = result + dot32(act, down_w_ref[span, :])
    result_ref[...] = result


def mlp_forward(layer, attended, stream, out_w, out_b, gain, shift, up_w, up_b, down_w, down_b):
    rows, width = attended.shape
    up = up_w.shape[2]
    out = jax.ShapeDtypeStruct
    return dense_call(
        partial(mlp_forward_kernel, layer),
        "mlp_forward",
        rows,
        [row_block(width), row_block(width), resident(layer, width, width)]
        + [vector(width)] * 3
        + [resident(layer, width, up), vector(up), resident(layer, up, width), vector(width)],
        [row_block(width), row_block(width), row_block(up), row_block(up), row_block(width)],
        [
            out((rows, width), f32),
            out((rows, width), bf16),
            out((rows, up), bf16),
            out((rows, up), bf16),
            out((rows, width), f32),
        ],
        2 * rows * width * (width + 2 * up),
        4 * rows * (4 * width + up) + 4 * width * (width + up),
    )(attended, stream, out_w, out_b, gain, shift, up_w, up_b, down_w, down_b)


def mlp_backward_kernel(
    layer, grad_ref, slope_ref, middle_ref, gain_ref, up_w_ref, down_w_ref, out_w_ref,
    low_ref, hidden_ref, grad_middle_ref, branch_ref, attended_ref, up_sum_ref, sums_ref,
):
    width = grad_ref.shape[1]

    @pl.when(pl.program_id(0) == 0)
    def _():
        up_sum_ref[...] = jnp.zeros_like(up_sum_ref)
        sums_ref[...] = jnp.zeros_like(sums_ref)

    grad = grad_ref[...]
    low = grad.astype(bf16)
    low_ref[...] = low
    normed = jnp.zeros(grad.shape, f32)
    for at in range(0, up_w_ref.shape[1], width):
        span = slice(at, at + width)
        act = dot_nt(low, down_w_ref[span, :])
        hidden = (slope_ref[:, span].astype(f32) * act).astype(bf16)
        hidden_ref[:, span] = hidden
        up_sum_ref[:, span] += columns_sum(hidden.astype(f32))
        normed = normed + dot_nt(hidden, up_w_ref[:, span])
    unit, scale = standardize(middle_ref[...])
    scaled = normed * row(gain_ref, layer)
    inner = scaled - jnp.mean(scaled, axis=-1, keepdims=True)
    inner = inner - unit * jnp.mean(scaled * unit, axis=-1, keepdims=True)
    middle = grad + inner * scale
    grad_middle_ref[...] = middle
    branch = middle.astype(bf16)
    branch_ref[...] = branch
    attended_ref[...] = dot_nt(branch, out_w_ref[...]).astype(bf16)
    sums_ref[0:1, :] += columns_sum(low.astype(f32))
    sums_ref[1:2, :] += columns_sum(normed * unit)
    sums_ref[2:3, :] += columns_sum(normed)
    sums_ref[3:4, :] += columns_sum(branch.astype(f32))


def mlp_backward(layer, grad, slope, middle, gain, up_w, down_w, out_w):
    rows, width = grad.shape
    up = up_w.shape[2]
    out = jax.ShapeDtypeStruct
    return dense_call(
        partial(mlp_backward_kernel, layer),
        "mlp_backward",
        rows,
        [row_block(width), row_block(up), row_block(width), vector(width)]
        + [resident(layer, width, up), resident(layer, up, width), resident(layer, width, width)],
        [row_block(width), row_block(up)] + [row_block(width)] * 3 + [kept(1, up), kept(8, width)],
        [
            out((rows, width), bf16),
            out((rows, up), bf16),
            out((rows, width), f32),
            out((rows, width), bf16),
            out((rows, width), bf16),
            out((1, up), f32),
            out((8, width), f32),
        ],
        2 * rows * width * (width + 2 * up),
        4 * rows * (5 * width + up) + 4 * width * (width + up),
    )(grad, slope, middle, gain, up_w, down_w, out_w)


def project_backward_kernel(layer, joined_ref, stream_ref, grad_ref, gain_ref, w_ref, result_ref, sums_ref):
    @pl.when(pl.program_id(0) == 0)
    def _():
        sums_ref[...] = jnp.zeros_like(sums_ref)

    normed = dot_nt(joined_ref[...], w_ref[...])
    unit, scale = standardize(stream_ref[...].astype(f32))
    scaled = normed * row(gain_ref, layer)
    inner = scaled - jnp.mean(scaled, axis=-1, keepdims=True)
    inner = inner - unit * jnp.mean(scaled * unit, axis=-1, keepdims=True)
    result_ref[...] = grad_ref[...] + inner * scale
    sums_ref[0:1, :] += columns_sum(normed * unit)
    sums_ref[1:2, :] += columns_sum(normed)


def project_backward(layer, joined, stream, grad, gain, qkv_w):
    rows, width = grad.shape
    out = jax.ShapeDtypeStruct
    return dense_call(
        partial(project_backward_kernel, layer),
        "project_backward",
        rows,
        [row_block(3 * width), row_block(width), row_block(width), vector(width)]
        + [resident(layer, width, 3 * width)],
        [row_block(width), kept(8, width)],
        [out((rows, width), f32), out((8, width), f32)],
        6 * rows * width * width,
        18 * rows * width + 6 * width * width,
    )(joined, stream, grad, gain, qkv_w)


def layer_forward(layer, stream, weights, fq, fk):
    gain_one, shift_one, qkv_w, bias, out_w, out_b, gain_two, shift_two, up_w, up_b, down_w, down_b = weights
    normed, joined = project(layer, stream, gain_one, shift_one, qkv_w, bias)
    attended, lse = attend_forward(joined, fq, fk)
    middle, normed_two, activated, slope, output = mlp_forward(
        layer, attended, stream, out_w, out_b, gain_two, shift_two, up_w, up_b, down_w, down_b
    )
    return output, (stream, normed, joined, attended, lse, middle, normed_two, slope, activated)


def layer_backward(layer, grad_stream, cache, weights, fq, fk, tie):
    stream, normed, joined, attended, lse, middle, normed_two, slope, activated = cache
    gain_one, shift_one, qkv_w, bias, out_w, out_b, gain_two, shift_two, up_w, up_b, down_w, down_b = weights
    low, grad_hidden, grad_middle, branch, grad_attended, grad_up_b, sums = mlp_backward(
        layer, grad_stream, slope, middle, gain_two, up_w, down_w, out_w
    )
    grad_down_w = jnp.einsum("tf,td->fd", activated, low, preferred_element_type=f32).astype(bf16)
    grad_up_w = jnp.einsum("td,tf->df", normed_two, grad_hidden, preferred_element_type=f32).astype(bf16)
    branch = tie("hidden", branch, (grad_down_w, grad_up_w))
    grad_out_w = jnp.einsum("tc,td->cd", attended, branch, preferred_element_type=f32).astype(bf16)
    grad_attended = tie("attended", grad_attended, (grad_out_w,))
    grad_joined, column_sums = attend_backward(joined, grad_attended, attended, lse, fq, fk)
    grad_joined = tie("joined", grad_joined, ())
    grad_qkv_w = jnp.einsum("td,te->de", normed, grad_joined, preferred_element_type=f32).astype(bf16)
    grad_joined = tie("qkv", grad_joined, (grad_qkv_w,))
    grad_input, sums_one = project_backward(layer, grad_joined, stream, grad_middle, gain_one, qkv_w)
    small = (
        sums_one[0],
        sums_one[1],
        column_sums.reshape(-1),
        sums[3],
        sums[1],
        sums[2],
        grad_up_b[0],
        sums[0],
    )
    return grad_input, (grad_qkv_w, grad_out_w, grad_up_w, grad_down_w), small


def local(n, *arguments):
    (
        patches,
        img_length,
        img_start,
        class_count,
        *stacked,
        cls_weight,
        cls_bias,
        logit_grad,
    ) = arguments
    me = lax.axis_index("dp")
    row_count, width = patches.shape
    up_width = stacked[8].shape[2]
    slot_count = img_length.shape[0]
    positions = jnp.arange(row_count, dtype=jnp.int32)
    inside = (positions[None, :] >= img_start[:, None]) & (
        positions[None, :] < (img_start + img_length)[:, None]
    )
    member = inside.astype(f32)
    live_rows = jnp.sum(inside.astype(jnp.int32), axis=0)
    segment = (
        jnp.sum(inside.astype(jnp.int32) * jnp.arange(slot_count, dtype=jnp.int32)[:, None], axis=0)
        + (1 - live_rows) * slot_count
    )
    fq, fk = seg_features(segment, slot_count)
    counts = jnp.maximum(img_length, 1).astype(f32)
    live_columns = jnp.arange(cls_weight.shape[1], dtype=jnp.int32) < class_count[0]
    masked_grad = jnp.where(live_columns[None, :], logit_grad, jnp.zeros_like(logit_grad))
    pooled_grad = lax.psum_scatter(
        dot_nt(masked_grad, cls_weight), "dp", scatter_dimension=0, tiled=True
    )
    weights = list(stacked)
    qv_bias = weights[3]
    weights[3] = jnp.concatenate(
        [qv_bias[:, :width], jnp.zeros((LAYERS, width), bf16), qv_bias[:, width:]], axis=1
    )
    stream = patches
    caches = []
    for layer in range(LAYERS):
        stream, cache = layer_forward(layer, stream, weights, fq, fk)
        caches.append(cache)
    sums = jnp.dot(member, stream, precision=HIGHEST, preferred_element_type=f32)
    side = jnp.broadcast_to(counts[:, None], (slot_count, 128))
    gathered = lax.all_gather(jnp.concatenate([sums, side], axis=1), "dp", axis=0, tiled=True)
    grad_stream = jnp.einsum(
        "it,id->td",
        member,
        pooled_grad / counts[:, None],
        precision=HIGHEST,
        preferred_element_type=f32,
    )
    qk = 2 * width
    last = {}
    first = []

    def tie_last(name, value, grads):
        last[name] = grads
        if name != "attended":
            return value
        both = pack(last["hidden"] + grads, n, width)
        value, both = lax.optimization_barrier((value, both))
        last["sum"] = lax.psum_scatter(both, "dp", scatter_dimension=0, tiled=False)
        return value

    def tie_first(name, value, grads):
        if name == "hidden":
            side_a = pack([grads[0], last["qkv"][:, :width]], n, width)
            side_b = pack([grads[1], last["qkv"][:, width:]], n, width)
            first.append(pair_sum(side_a, side_b, me, n))
        if name == "attended":
            value, last["out"] = fence((value, grads[0]), first)
            return value
        if name == "qkv":
            side_a = pack([grads[0][:, :qk]], n, width)
            side_b = pack([grads[0][:, qk:], last["out"]], n, width)
            value, last["a"], last["b"] = lax.optimization_barrier((value, side_a, side_b))
            return value
        return fence(value, first)

    grad_stream, grads, small_last = layer_backward(1, grad_stream, caches[1], weights, fq, fk, tie_last)
    grad_stream, last["qkv"] = lax.optimization_barrier((grad_stream, grads[0]))
    grad_stream, grads, small_first = layer_backward(0, grad_stream, caches[0], weights, fq, fk, tie_first)
    small, sizes = pack_small([jnp.stack(pair) for pair in zip(small_first, small_last)], n, width)
    side_a = jnp.concatenate([last["a"], small], axis=1)
    grad_stream, side_a, last["sum"] = lax.optimization_barrier((grad_stream, side_a, last["sum"]))
    first.append(pair_sum(side_a, last["b"], me, n))
    grad_stream = fence(grad_stream, first)
    for unused in range(2):
        grad_stream = fence(grad_stream, first[1:])
    while any(e.result is None for e in first):
        grad_stream = fence(grad_stream, first)
    gathered = (gathered[:, :width] / gathered[:, width : width + 1]).astype(bf16)
    scores = dot32(gathered, cls_weight) + cls_bias.astype(f32)
    logits = jnp.where(live_columns[None, :], scores, 0.0)
    grad_cls_weight = jnp.einsum("id,ic->dc", gathered, masked_grad, preferred_element_type=f32)
    grad_cls_bias = jnp.sum(masked_grad.astype(f32), axis=0)
    square = (width, width)
    wide = (width, up_width)
    tall = (up_width, width)
    down_last, up_last, out_last = unpack(last["sum"].astype(f32), [tall, wide, square], n)
    down_first, q_last = unpack(first[0].result[0], [tall, square], n)
    up_first, kv_last = unpack(first[0].result[1], [wide, (width, qk)], n)
    qkv_last = jnp.concatenate([q_last, kv_last], axis=1)
    qk_rows = 2 * (width // n)
    (qk_first,) = unpack(first[1].result[0][:qk_rows], [(width, qk)], n)
    v_first, out_first = unpack(first[1].result[1], [square, square], n)
    qkv_first = jnp.concatenate([qk_first, v_first], axis=1)
    qkv_sum = jnp.stack([qkv_first, qkv_last])
    out_sum = jnp.stack([out_first, out_last])
    up_sum = jnp.stack([up_first, up_last])
    down_sum = jnp.stack([down_first, down_last])
    gain_one, shift_one, qv_b, out_b, gain_two, shift_two, up_b, down_b = unpack_small(
        first[1].result[0][qk_rows:], sizes
    )
    return (
        logits,
        grad_stream,
        gain_one,
        shift_one,
        qkv_sum,
        qv_b,
        out_sum,
        out_b,
        gain_two,
        shift_two,
        up_sum,
        up_b,
        down_sum,
        down_b,
        grad_cls_weight,
        grad_cls_bias,
    )


def solution(mesh):
    whole = P()
    placed = (
        (P("dp", None), P("dp"), P("dp"), P("dp"))
        + (whole,) * 12
        + (P(None, "dp"), P("dp"), P(None, "dp"))
    )
    vector = P(None, "dp")
    matrix = P(None, "dp", None)
    return jax.shard_map(
        partial(local, mesh.size),
        mesh=mesh,
        in_specs=placed,
        out_specs=(
            P(None, "dp"),
            P("dp", None),
            vector,
            vector,
            matrix,
            vector,
            matrix,
            vector,
            vector,
            vector,
            matrix,
            vector,
            matrix,
            vector,
            P(None, "dp"),
            P("dp"),
        ),
        check_vma=False,
    )
```

```python
from functools import partial

import jax
import jax.numpy as jnp
from jax import lax
from jax.experimental import pallas as pl
from jax.experimental.pallas import tpu as pltpu
from jax.sharding import PartitionSpec as P

HD = 64
LAYERS = 2
BIG = 1e30
EPSILON = 1e-06
HIGHEST = lax.Precision.HIGHEST
NT = (((1,), (1,)), ((), ()))
f32 = jnp.float32
bf16 = jnp.bfloat16
VMEM_LIMIT = 56 << 20
ROWS_STEP = 256


def dot32(left, right):
    return jnp.dot(left, right, preferred_element_type=f32)


def dot_nt(left, right):
    return lax.dot_general(left, right, NT, preferred_element_type=f32)


def seg_features(segment, slot_count):
    lane = jnp.arange(128, dtype=jnp.int32) % HD
    hit = segment[:, None] == lane[None, :]
    live = (lane <= slot_count)[None, :]
    query_side = (hit & live).astype(bf16)
    key_side = jnp.where(live & ~hit, -BIG, 0.0).astype(bf16)
    return query_side, key_side


def attend_forward_kernel(q_ref, k_ref, v_ref, fq_ref, fk_ref, o_ref, lse_ref, *, chunk):
    rows = q_ref.shape[0]
    left = lax.broadcasted_iota(jnp.int32, (rows, 128), 1) < HD
    q = q_ref[...] * jnp.asarray(HD**-0.5, bf16)
    k = k_ref[...]
    fq = fq_ref[...]
    fk = fk_ref[...]
    v_t = v_ref[...].T
    q_side = [jnp.where(left, q, fq), jnp.where(left, fq, q)]
    k_side = [jnp.where(left, k, fk), jnp.where(left, fk, k)]
    for c in range(rows // chunk):
        span = slice(c * chunk, (c + 1) * chunk)
        outs = []
        for h in range(2):
            scores = dot_nt(k_side[h], q_side[h][span])
            largest = jnp.max(scores, axis=0, keepdims=True)
            p = jnp.exp(scores - largest)
            total = jnp.sum(p, axis=0, keepdims=True)
            mixed = dot32(v_t[h * HD : (h + 1) * HD], p.astype(bf16))
            outs.append(mixed / total)
            lse_ref[0, h : h + 1, span] = largest + jnp.log(total)
        o_ref[span, :] = jnp.concatenate(outs, axis=0).T.astype(bf16)


def attend_forward(joined, fq, fk):
    rows = joined.shape[0]
    width = joined.shape[1] // 3
    n = width // 128
    col = lambda off: pl.BlockSpec((rows, 128), lambda i, off=off: (0, off + i))
    full = pl.BlockSpec((rows, 128), lambda i: (0, 0))
    return pl.pallas_call(
        partial(attend_forward_kernel, chunk=rows),
        grid=(n,),
        in_specs=[col(0), col(n), col(2 * n), full, full],
        out_specs=[
            pl.BlockSpec((rows, 128), lambda i: (0, i)),
            pl.BlockSpec((1, 2, rows), lambda i: (i, 0, 0)),
        ],
        out_shape=[
            jax.ShapeDtypeStruct((rows, width), bf16),
            jax.ShapeDtypeStruct((n, 2, rows), f32),
        ],
        compiler_params=pltpu.CompilerParams(vmem_limit_bytes=VMEM_LIMIT),
        cost_estimate=pl.CostEstimate(flops=1, bytes_accessed=1, transcendentals=0),
        name="attend_forward",
    )(joined, joined, joined, fq, fk)


def attend_backward_kernel(
    q_ref, k_ref, v_ref, g_ref, o_ref, lse_ref, fq_ref, fk_ref, dj_ref, cs_ref, *, chunk
):
    rows = q_ref.shape[0]
    width = dj_ref.shape[1] // 3
    step = pl.program_id(0)
    left = lax.broadcasted_iota(jnp.int32, (rows, 128), 1) < HD
    left_chunk = left[:chunk]
    scale = HD**-0.5
    q = q_ref[...] * jnp.asarray(scale, bf16)
    k = k_ref[...]
    v = v_ref[...]
    g = g_ref[...]
    fq = fq_ref[...]
    fk = fk_ref[...]
    zero = jnp.zeros_like(q)
    k_t = k.T
    product_t = (g.astype(f32) * o_ref[...].astype(f32)).T
    q_side = [jnp.where(left, q, fq), jnp.where(left, fq, q)]
    k_side = [jnp.where(left, k, fk), jnp.where(left, fk, k)]
    v_side = [jnp.where(left, v, zero), jnp.where(left, zero, v)]
    delta = [jnp.sum(product_t[h * HD : (h + 1) * HD], axis=0, keepdims=True) for h in range(2)]
    lse = [lse_ref[0, h : h + 1, :] for h in range(2)]
    dq = [None, None]
    sum_v = jnp.zeros((1, 128), f32)
    for c in range(rows // chunk):
        span = slice(c * chunk, (c + 1) * chunk)
        dk = []
        dv = []
        for h in range(2):
            scores = dot_nt(k_side[h][span], q_side[h])
            p = jnp.exp(scores - lse[h])
            dp = dot_nt(v_side[h][span], g)
            dv.append(dot32(p.astype(bf16), g))
            ds = (p * (dp - delta[h])).astype(bf16)
            dk.append(dot32(ds, q))
            part = dot32(k_t[h * HD : (h + 1) * HD, span], ds)
            dq[h] = part if dq[h] is None else dq[h] + part
        dk_low = jnp.where(left_chunk, dk[0], dk[1]).astype(bf16)
        dv_low = jnp.where(left_chunk, dv[0], dv[1]).astype(bf16)
        dj_ref[span, pl.ds(pl.multiple_of(width + step * 128, 128), 128)] = dk_low
        dj_ref[span, pl.ds(pl.multiple_of(2 * width + step * 128, 128), 128)] = dv_low
        sum_v += jnp.sum(dv_low.astype(f32), axis=0, keepdims=True)
    dq_low = (jnp.concatenate(dq, axis=0) * scale).T.astype(bf16)
    dj_ref[:, pl.ds(pl.multiple_of(step * 128, 128), 128)] = dq_low
    cs_ref[0:1, :] = jnp.sum(dq_low.astype(f32), axis=0, keepdims=True)
    cs_ref[1:2, :] = sum_v


def attend_backward(joined, grad_attended, attended, lse, fq, fk):
    rows = joined.shape[0]
    width = joined.shape[1] // 3
    n = width // 128
    col = lambda off: pl.BlockSpec((rows, 128), lambda i, off=off: (0, off + i))
    full = pl.BlockSpec((rows, 128), lambda i: (0, 0))
    return pl.pallas_call(
        partial(attend_backward_kernel, chunk=rows // 2),
        grid=(n,),
        in_specs=[
            col(0),
            col(n),
            col(2 * n),
            col(0),
            col(0),
            pl.BlockSpec((1, 2, rows), lambda i: (i, 0, 0)),
            full,
            full,
        ],
        out_specs=[
            pl.BlockSpec((rows, 3 * width), lambda i: (0, 0)),
            pl.BlockSpec((2, 128), lambda i: (0, i)),
        ],
        out_shape=[
            jax.ShapeDtypeStruct((rows, 3 * width), bf16),
            jax.ShapeDtypeStruct((2, width), f32),
        ],
        compiler_params=pltpu.CompilerParams(vmem_limit_bytes=VMEM_LIMIT),
        cost_estimate=pl.CostEstimate(flops=1, bytes_accessed=1, transcendentals=0),
        name="attend_backward",
    )(joined, joined, joined, grad_attended, attended, lse, fq, fk)


def total(values):
    out = values[0].astype(f32)
    for value in values[1:]:
        out = out + value.astype(f32)
    return out


def pick(values, axis, index):
    return lax.dynamic_index_in_dim(values, index, axis, keepdims=False)


def pack(grads, n, width):
    pieces = []
    for grad in grads:
        rows, columns = grad.shape
        blocks = grad.reshape(n, rows // n, columns)
        pieces += [blocks[:, :, at : at + width] for at in range(0, columns, width)]
    return jnp.concatenate(pieces, axis=1)


def unpack(packed, shapes, n):
    width = packed.shape[1]
    outs = []
    start = 0
    for rows, columns in shapes:
        count = rows // n
        pieces = []
        for unused in range(0, columns, width):
            pieces.append(packed[start : start + count])
            start += count
        outs.append(jnp.concatenate(pieces, axis=1))
    return outs


class PairSum:
    def __init__(self, a, b, me):
        self.me = me
        self.n = a.shape[0]
        self.rows = a.shape[1]
        dims = (4, 2, 2, 2)
        self.terms = [[a.reshape(dims + a.shape[1:])], [b.reshape(dims + b.shape[1:])]]
        self.round = 0
        self.result = None
        self.pending = None

    def bit(self, at):
        return (self.me >> at) & 1

    def steps(self):
        x, y = self.bit(1), self.bit(2)
        core = self.bit(0)
        top = self.me >> 3
        return [((3, core), (3, core)), ((2, x), (1, y)), ((1, y), (1, x)), ((0, top), (0, top))][self.round]

    def part(self, which, other):
        axis, mine = self.steps()[which]
        return total([pick(t, axis, mine ^ other) for t in self.terms[which]]).astype(bf16)

    def sends(self):
        if self.round < 3:
            return [self.part(0, 1), self.part(1, 1)]
        return [jnp.concatenate([self.part(0, k), self.part(1, k)], axis=-2) for k in (1, 2, 3)]

    def launch(self, sends):
        partners = [[1, 1], [2, 4], [4, 2], [8, 16, 24]][self.round]
        self.pending = [
            lax.ppermute(sent, "dp", [(i, i ^ p) for i in range(self.n)])
            for sent, p in zip(sends, partners)
        ]

    def land(self, came):
        self.pending = None
        steps = self.steps()
        if self.round == 3:
            came = [
                [value[..., : self.rows, :] for value in came],
                [value[..., self.rows :, :] for value in came],
            ]
        else:
            came = [[came[0]], [came[1]]]
        for which in (0, 1):
            axis, mine = steps[which]
            self.terms[which] = [pick(t, axis, mine) for t in self.terms[which]] + came[which]
        self.round += 1
        if self.round == 4:
            self.result = [total(self.terms[0]), total(self.terms[1])]


class Scattered:
    def __init__(self, a, b):
        both = jnp.concatenate([a, b], axis=1)
        out = lax.psum_scatter(both, "dp", scatter_dimension=0, tiled=False).astype(f32)
        self.result = [out[: a.shape[1]], out[a.shape[1] :]]
        self.pending = None


def pair_sum(a, b, me, n):
    if n == 32 and a.shape[1] % 8 == 0 and b.shape[1] % 8 == 0:
        return PairSum(a, b, me)
    return Scattered(a, b)


def fence(main, exchanges):
    flying = [e for e in exchanges if e.pending is not None]
    main, came = lax.optimization_barrier((main, [e.pending for e in flying]))
    for e, values in zip(flying, came):
        e.land(values)
    ready = [e for e in exchanges if e.result is None]
    main, sends = lax.optimization_barrier((main, [e.sends() for e in ready]))
    for e, values in zip(ready, sends):
        e.launch(values)
    return main


def pack_small(vectors, n, width):
    pieces = [vector.reshape(LAYERS, n, -1).transpose(1, 0, 2).reshape(n, -1) for vector in vectors]
    packed = jnp.concatenate(pieces, axis=1).astype(bf16)
    padded = jnp.pad(packed, ((0, 0), (0, -packed.shape[1] % (8 * width))))
    return padded.reshape(n, -1, width), [piece.shape[1] for piece in pieces]


def unpack_small(block, sizes):
    flat = block.reshape(-1)
    outs = []
    start = 0
    for size in sizes:
        outs.append(flat[start : start + size].reshape(LAYERS, -1))
        start += size
    return outs


def row_block(width):
    return pl.BlockSpec((ROWS_STEP, width), lambda i: (i, 0))


def vector(width):
    return pl.BlockSpec((LAYERS, width), lambda i: (0, 0))


def row(ref, layer):
    return ref[layer : layer + 1, :].astype(f32)


def resident(layer, rows, columns):
    return pl.BlockSpec((None, rows, columns), lambda i: (layer, 0, 0), pipeline_mode=pl.Buffered(1))


def kept(rows, columns):
    return pl.BlockSpec((rows, columns), lambda i: (0, 0))


def standardize(values):
    center = values - jnp.mean(values, axis=-1, keepdims=True)
    scale = lax.rsqrt(jnp.mean(center * center, axis=-1, keepdims=True) + EPSILON)
    return center * scale, scale


def columns_sum(values):
    return jnp.sum(values, axis=0, keepdims=True)


def dense_call(kernel, name, rows, in_specs, out_specs, out_shape, flops, moved):
    return pl.pallas_call(
        kernel,
        grid=(rows // ROWS_STEP,),
        in_specs=in_specs,
        out_specs=out_specs,
        out_shape=out_shape,
        compiler_params=pltpu.CompilerParams(vmem_limit_bytes=VMEM_LIMIT),
        cost_estimate=pl.CostEstimate(flops=1, bytes_accessed=1, transcendentals=0),
        name=name,
    )


def project_kernel(layer, stream_ref, gain_ref, shift_ref, w_ref, b_ref, normed_ref, joined_ref):
    unit, unused = standardize(stream_ref[...].astype(f32))
    normed = (unit * row(gain_ref, layer) + row(shift_ref, layer)).astype(bf16)
    normed_ref[...] = normed
    joined_ref[...] = (dot32(normed, w_ref[...]) + row(b_ref, layer)).astype(bf16)


def project(layer, stream, gain, shift, qkv_w, bias):
    rows, width = stream.shape
    out = jax.ShapeDtypeStruct
    return dense_call(
        partial(project_kernel, layer),
        "project",
        rows,
        [row_block(width), vector(width), vector(width)]
        + [resident(layer, width, 3 * width), vector(3 * width)],
        [row_block(width), row_block(3 * width)],
        [out((rows, width), bf16), out((rows, 3 * width), bf16)],
        6 * rows * width * width,
        12 * rows * width + 6 * width * width,
    )(stream, gain, shift, qkv_w, bias)


def mlp_forward_kernel(
    layer, att_ref, stream_ref, out_w_ref, out_b_ref, gain_ref, shift_ref, up_w_ref, up_b_ref,
    down_w_ref, down_b_ref, middle_ref, normed_ref, act_ref, slope_ref, result_ref,
):
    width = att_ref.shape[1]
    middle = (
        stream_ref[...].astype(f32) + dot32(att_ref[...], out_w_ref[...]) + row(out_b_ref, layer)
    )
    middle_ref[...] = middle
    unit, unused = standardize(middle)
    normed = (unit * row(gain_ref, layer) + row(shift_ref, layer)).astype(bf16)
    normed_ref[...] = normed
    result = middle + row(down_b_ref, layer)
    for at in range(0, up_w_ref.shape[1], width):
        span = slice(at, at + width)
        hidden = dot32(normed, up_w_ref[:, span]) + up_b_ref[layer : layer + 1, span].astype(f32)
        below = 0.5 + 0.5 * lax.erf(hidden * 0.7071067811865476)
        act = (hidden * below).astype(bf16)
        slope = below + hidden * (0.3989422804014327 * jnp.exp(-0.5 * (hidden * hidden)))
        act_ref[:, span] = act
        slope_ref[:, span] = slope.astype(bf16)
        result = result + dot32(act, down_w_ref[span, :])
    result_ref[...] = result


def mlp_forward(layer, attended, stream, out_w, out_b, gain, shift, up_w, up_b, down_w, down_b):
    rows, width = attended.shape
    up = up_w.shape[2]
    out = jax.ShapeDtypeStruct
    return dense_call(
        partial(mlp_forward_kernel, layer),
        "mlp_forward",
        rows,
        [row_block(width), row_block(width), resident(layer, width, width)]
        + [vector(width)] * 3
        + [resident(layer, width, up), vector(up), resident(layer, up, width), vector(width)],
        [row_block(width), row_block(width), row_block(up), row_block(up), row_block(width)],
        [
            out((rows, width), f32),
            out((rows, width), bf16),
            out((rows, up), bf16),
            out((rows, up), bf16),
            out((rows, width), f32),
        ],
        2 * rows * width * (width + 2 * up),
        4 * rows * (4 * width + up) + 4 * width * (width + up),
    )(attended, stream, out_w, out_b, gain, shift, up_w, up_b, down_w, down_b)


def mlp_backward_kernel(
    layer, grad_ref, slope_ref, middle_ref, gain_ref, up_w_ref, down_w_ref, out_w_ref,
    low_ref, hidden_ref, grad_middle_ref, branch_ref, attended_ref, up_sum_ref, sums_ref,
):
    width = grad_ref.shape[1]

    @pl.when(pl.program_id(0) == 0)
    def _():
        up_sum_ref[...] = jnp.zeros_like(up_sum_ref)
        sums_ref[...] = jnp.zeros_like(sums_ref)

    grad = grad_ref[...]
    low = grad.astype(bf16)
    low_ref[...] = low
    normed = jnp.zeros(grad.shape, f32)
    for at in range(0, up_w_ref.shape[1], width):
        span = slice(at, at + width)
        act = dot_nt(low, down_w_ref[span, :])
        hidden = (slope_ref[:, span].astype(f32) * act).astype(bf16)
        hidden_ref[:, span] = hidden
        up_sum_ref[:, span] += columns_sum(hidden.astype(f32))
        normed = normed + dot_nt(hidden, up_w_ref[:, span])
    unit, scale = standardize(middle_ref[...])
    scaled = normed * row(gain_ref, layer)
    inner = scaled - jnp.mean(scaled, axis=-1, keepdims=True)
    inner = inner - unit * jnp.mean(scaled * unit, axis=-1, keepdims=True)
    middle = grad + inner * scale
    grad_middle_ref[...] = middle
    branch = middle.astype(bf16)
    branch_ref[...] = branch
    attended_ref[...] = dot_nt(branch, out_w_ref[...]).astype(bf16)
    sums_ref[0:1, :] += columns_sum(low.astype(f32))
    sums_ref[1:2, :] += columns_sum(normed * unit)
    sums_ref[2:3, :] += columns_sum(normed)
    sums_ref[3:4, :] += columns_sum(branch.astype(f32))


def mlp_backward(layer, grad, slope, middle, gain, up_w, down_w, out_w):
    rows, width = grad.shape
    up = up_w.shape[2]
    out = jax.ShapeDtypeStruct
    return dense_call(
        partial(mlp_backward_kernel, layer),
        "mlp_backward",
        rows,
        [row_block(width), row_block(up), row_block(width), vector(width)]
        + [resident(layer, width, up), resident(layer, up, width), resident(layer, width, width)],
        [row_block(width), row_block(up)] + [row_block(width)] * 3 + [kept(1, up), kept(8, width)],
        [
            out((rows, width), bf16),
            out((rows, up), bf16),
            out((rows, width), f32),
            out((rows, width), bf16),
            out((rows, width), bf16),
            out((1, up), f32),
            out((8, width), f32),
        ],
        2 * rows * width * (width + 2 * up),
        4 * rows * (5 * width + up) + 4 * width * (width + up),
    )(grad, slope, middle, gain, up_w, down_w, out_w)


def project_backward_kernel(layer, joined_ref, stream_ref, grad_ref, gain_ref, w_ref, result_ref, sums_ref):
    @pl.when(pl.program_id(0) == 0)
    def _():
        sums_ref[...] = jnp.zeros_like(sums_ref)

    normed = dot_nt(joined_ref[...], w_ref[...])
    unit, scale = standardize(stream_ref[...].astype(f32))
    scaled = normed * row(gain_ref, layer)
    inner = scaled - jnp.mean(scaled, axis=-1, keepdims=True)
    inner = inner - unit * jnp.mean(scaled * unit, axis=-1, keepdims=True)
    result_ref[...] = grad_ref[...] + inner * scale
    sums_ref[0:1, :] += columns_sum(normed * unit)
    sums_ref[1:2, :] += columns_sum(normed)


def project_backward(layer, joined, stream, grad, gain, qkv_w):
    rows, width = grad.shape
    out = jax.ShapeDtypeStruct
    return dense_call(
        partial(project_backward_kernel, layer),
        "project_backward",
        rows,
        [row_block(3 * width), row_block(width), row_block(width), vector(width)]
        + [resident(layer, width, 3 * width)],
        [row_block(width), kept(8, width)],
        [out((rows, width), f32), out((8, width), f32)],
        6 * rows * width * width,
        18 * rows * width + 6 * width * width,
    )(joined, stream, grad, gain, qkv_w)


def layer_forward(layer, stream, weights, fq, fk):
    gain_one, shift_one, qkv_w, bias, out_w, out_b, gain_two, shift_two, up_w, up_b, down_w, down_b = weights
    normed, joined = project(layer, stream, gain_one, shift_one, qkv_w, bias)
    attended, lse = attend_forward(joined, fq, fk)
    middle, normed_two, activated, slope, output = mlp_forward(
        layer, attended, stream, out_w, out_b, gain_two, shift_two, up_w, up_b, down_w, down_b
    )
    return output, (stream, normed, joined, attended, lse, middle, normed_two, slope, activated)


def layer_backward(layer, grad_stream, cache, weights, fq, fk, tie):
    stream, normed, joined, attended, lse, middle, normed_two, slope, activated = cache
    gain_one, shift_one, qkv_w, bias, out_w, out_b, gain_two, shift_two, up_w, up_b, down_w, down_b = weights
    low, grad_hidden, grad_middle, branch, grad_attended, grad_up_b, sums = mlp_backward(
        layer, grad_stream, slope, middle, gain_two, up_w, down_w, out_w
    )
    grad_down_w = jnp.einsum("tf,td->fd", activated, low, preferred_element_type=f32).astype(bf16)
    grad_up_w = jnp.einsum("td,tf->df", normed_two, grad_hidden, preferred_element_type=f32).astype(bf16)
    branch = tie("hidden", branch, (grad_down_w, grad_up_w))
    grad_out_w = jnp.einsum("tc,td->cd", attended, branch, preferred_element_type=f32).astype(bf16)
    grad_attended = tie("attended", grad_attended, (grad_out_w,))
    grad_joined, column_sums = attend_backward(joined, grad_attended, attended, lse, fq, fk)
    grad_joined = tie("joined", grad_joined, ())
    grad_qkv_w = jnp.einsum("td,te->de", normed, grad_joined, preferred_element_type=f32).astype(bf16)
    grad_joined = tie("qkv", grad_joined, (grad_qkv_w,))
    grad_input, sums_one = project_backward(layer, grad_joined, stream, grad_middle, gain_one, qkv_w)
    small = (
        sums_one[0],
        sums_one[1],
        column_sums.reshape(-1),
        sums[3],
        sums[1],
        sums[2],
        grad_up_b[0],
        sums[0],
    )
    return grad_input, (grad_qkv_w, grad_out_w, grad_up_w, grad_down_w), small


def local(n, *arguments):
    (
        patches,
        img_length,
        img_start,
        class_count,
        *stacked,
        cls_weight,
        cls_bias,
        logit_grad,
    ) = arguments
    me = lax.axis_index("dp")
    row_count, width = patches.shape
    up_width = stacked[8].shape[2]
    slot_count = img_length.shape[0]
    positions = jnp.arange(row_count, dtype=jnp.int32)
    inside = (positions[None, :] >= img_start[:, None]) & (
        positions[None, :] < (img_start + img_length)[:, None]
    )
    member = inside.astype(f32)
    live_rows = jnp.sum(inside.astype(jnp.int32), axis=0)
    segment = (
        jnp.sum(inside.astype(jnp.int32) * jnp.arange(slot_count, dtype=jnp.int32)[:, None], axis=0)
        + (1 - live_rows) * slot_count
    )
    fq, fk = seg_features(segment, slot_count)
    counts = jnp.maximum(img_length, 1).astype(f32)
    live_columns = jnp.arange(cls_weight.shape[1], dtype=jnp.int32) < class_count[0]
    masked_grad = jnp.where(live_columns[None, :], logit_grad, jnp.zeros_like(logit_grad))
    pooled_grad = lax.psum_scatter(
        dot_nt(masked_grad, cls_weight), "dp", scatter_dimension=0, tiled=True
    )
    weights = list(stacked)
    qv_bias = weights[3]
    weights[3] = jnp.concatenate(
        [qv_bias[:, :width], jnp.zeros((LAYERS, width), bf16), qv_bias[:, width:]], axis=1
    )
    stream = patches
    caches = []
    for layer in range(LAYERS):
        stream, cache = layer_forward(layer, stream, weights, fq, fk)
        caches.append(cache)
    sums = jnp.dot(member, stream, precision=HIGHEST, preferred_element_type=f32)
    side = jnp.broadcast_to(counts[:, None], (slot_count, 128))
    gathered = lax.all_gather(jnp.concatenate([sums, side], axis=1), "dp", axis=0, tiled=True)
    grad_stream = jnp.einsum(
        "it,id->td",
        member,
        pooled_grad / counts[:, None],
        precision=HIGHEST,
        preferred_element_type=f32,
    )
    qk = 2 * width
    last = {}
    first = []

    def tie_last(name, value, grads):
        last[name] = grads
        if name != "attended":
            return value
        both = pack(last["hidden"] + grads, n, width)
        value, both = lax.optimization_barrier((value, both))
        last["sum"] = lax.psum_scatter(both, "dp", scatter_dimension=0, tiled=False)
        return value

    def tie_first(name, value, grads):
        if name == "hidden":
            side_a = pack([grads[0], last["qkv"][:, :width]], n, width)
            side_b = pack([grads[1], last["qkv"][:, width:]], n, width)
            first.append(pair_sum(side_a, side_b, me, n))
        if name == "attended":
            value, last["out"] = fence((value, grads[0]), first)
            return value
        if name == "qkv":
            side_a = pack([grads[0][:, :qk]], n, width)
            side_b = pack([grads[0][:, qk:], last["out"]], n, width)
            value, last["a"], last["b"] = lax.optimization_barrier((value, side_a, side_b))
            return value
        return fence(value, first)

    grad_stream, grads, small_last = layer_backward(1, grad_stream, caches[1], weights, fq, fk, tie_last)
    grad_stream, last["qkv"] = lax.optimization_barrier((grad_stream, grads[0]))
    grad_stream, grads, small_first = layer_backward(0, grad_stream, caches[0], weights, fq, fk, tie_first)
    small, sizes = pack_small([jnp.stack(pair) for pair in zip(small_first, small_last)], n, width)
    side_a = jnp.concatenate([last["a"], small], axis=1)
    grad_stream, side_a, last["sum"] = lax.optimization_barrier((grad_stream, side_a, last["sum"]))
    first.append(pair_sum(side_a, last["b"], me, n))
    grad_stream = fence(grad_stream, first)
    for unused in range(2):
        grad_stream = fence(grad_stream, first[1:])
    grad_stream, gathered = fence((grad_stream, gathered), first)
    while any(e.result is None for e in first):
        grad_stream = fence(grad_stream, first)
    gathered = (gathered[:, :width] / gathered[:, width : width + 1]).astype(bf16)
    scores = dot32(gathered, cls_weight) + cls_bias.astype(f32)
    logits = jnp.where(live_columns[None, :], scores, 0.0)
    grad_cls_weight = jnp.einsum("id,ic->dc", gathered, masked_grad, preferred_element_type=f32)
    grad_cls_bias = jnp.sum(masked_grad.astype(f32), axis=0)
    square = (width, width)
    wide = (width, up_width)
    tall = (up_width, width)
    down_last, up_last, out_last = unpack(last["sum"].astype(f32), [tall, wide, square], n)
    down_first, q_last = unpack(first[0].result[0], [tall, square], n)
    up_first, kv_last = unpack(first[0].result[1], [wide, (width, qk)], n)
    qkv_last = jnp.concatenate([q_last, kv_last], axis=1)
    qk_rows = 2 * (width // n)
    (qk_first,) = unpack(first[1].result[0][:qk_rows], [(width, qk)], n)
    v_first, out_first = unpack(first[1].result[1], [square, square], n)
    qkv_first = jnp.concatenate([qk_first, v_first], axis=1)
    qkv_sum = jnp.stack([qkv_first, qkv_last])
    out_sum = jnp.stack([out_first, out_last])
    up_sum = jnp.stack([up_first, up_last])
    down_sum = jnp.stack([down_first, down_last])
    gain_one, shift_one, qv_b, out_b, gain_two, shift_two, up_b, down_b = unpack_small(
        first[1].result[0][qk_rows:], sizes
    )
    return (
        logits,
        grad_stream,
        gain_one,
        shift_one,
        qkv_sum,
        qv_b,
        out_sum,
        out_b,
        gain_two,
        shift_two,
        up_sum,
        up_b,
        down_sum,
        down_b,
        grad_cls_weight,
        grad_cls_bias,
    )


def solution(mesh):
    whole = P()
    placed = (
        (P("dp", None), P("dp"), P("dp"), P("dp"))
        + (whole,) * 12
        + (P(None, "dp"), P("dp"), P(None, "dp"))
    )
    vector = P(None, "dp")
    matrix = P(None, "dp", None)
    return jax.shard_map(
        partial(local, mesh.size),
        mesh=mesh,
        in_specs=placed,
        out_specs=(
            P(None, "dp"),
            P("dp", None),
            vector,
            vector,
            matrix,
            vector,
            matrix,
            vector,
            vector,
            vector,
            matrix,
            vector,
            matrix,
            vector,
            P(None, "dp"),
            P("dp"),
        ),
        check_vma=False,
    )
```
